512 devices in a mesh: dp: 32 (over x_lo, y, core), tensor: 16 (over x_hi, z).
Axes of the slice: x: 4 (x_hi: 2, x_lo: 2; x = x_hi * 2 + x_lo), y: 8, z: 8, core: 2. Of those that a mesh axis runs over, the one named last changes fastest.
Arguments:
- tokens: bfloat16 [8192, 4096], P(('dp', 'tensor')), may hold values from -110 to 110
- norm_gain: bfloat16 [4096], replicated, may hold values from 0.099609375 to 1.8984375
- query_weight: bfloat16 [4096, 4096], P('dp', 'tensor'), may hold values from -1 to 1
- kv_weight: bfloat16 [4096, 1024], P('dp', 'tensor'), may hold values from -1 to 1
- out_weight: bfloat16 [4096, 4096], P('tensor', 'dp'), may hold values from -0.09375 to 0.09375
- grad_out: bfloat16 [8192, 4096], P(('dp', 'tensor')), may hold values from -6 to 6
- doc_lengths: int32 [32, 4], P('dp'), may hold values from 1 to 128, 256 in all within a row
Outputs:
- input_grad: bfloat16 [8192, 4096], P(('dp', 'tensor'))
- query_weight_grad: float32 [4096, 4096], P('dp', 'tensor')
- kv_weight_grad: float32 [4096, 1024], P('dp', 'tensor')
The draws below stay inside these ranges and needn't reach their ends.
Inputs may be any that keep to these rules, and one draw needn't show every extreme that they name: `doc_lengths`: each row sums to 256.
All inputs are finite; a program needn't handle non-finite values.
Results may differ from the reference program's by a relative error of at most 0.025.
Values may be sent and summed in bfloat16 or wider, within the bound.
A program may use at most 64 MiB of HBM per device.

```python
import math
import jax
import jax.numpy as jnp
import numpy as np
from jax import lax

D = 4096
H = 32
KVH = 4
HD = 128
SEQ = 256
NDOC = 4
REPLICAS = 32
TOKENS = 8192
N_DP = 32
N_TENSOR = 16


def draw_tokens(key, part):
    noise = jax.random.truncated_normal(jax.random.fold_in(key, 1), -4.0, 4.0, (TOKENS, D), jnp.float32)
    pairing = jax.random.permutation(jax.random.fold_in(key, 2), N_DP)
    replica = jnp.arange(TOKENS) // SEQ
    column_block = jnp.arange(D) // (D // N_DP)
    spiked = jnp.where(pairing[replica][:, None] == column_block[None, :], 3.0, 1.0)
    rough = noise * spiked
    return rough.astype(jnp.bfloat16)


def drawn_weight(key, column_count):
    return jax.random.truncated_normal(jax.random.fold_in(key, 22), -3.0, 3.0, (D, column_count), jnp.float32) / math.sqrt(D)


def draw_query_weight(key, part):
    return drawn_weight(jax.random.fold_in(key, 31), H * HD).astype(jnp.bfloat16)


def draw_kv_weight(key, part):
    return drawn_weight(jax.random.fold_in(key, 32), 2 * KVH * HD).astype(jnp.bfloat16)


def level_of(rng, extent, shards, low, high):
    level = 1.0
    for dim, blocks in shards:
        heights = jax.random.uniform(jax.random.fold_in(jax.random.fold_in(rng, 6), dim), (blocks,), jnp.float32, low / len(shards), high / len(shards))
        level = level * jnp.repeat(jnp.exp(heights), extent[dim] // blocks).reshape((-1,) + (1,) * (len(extent) - 1 - dim))
    return level


def profile(number_of, total, most, skew):
    loads = [(1 << 20) // math.isqrt(standing ** skew) + 1 for standing in range(2, number_of + 1)]
    spare, counts = total - most - (number_of - 1), [1] * (number_of - 1)
    while spare > 0:
        movable = [i for i in range(number_of - 1) if counts[i] < most]
        mass, budget = sum([loads[i] for i in movable]), spare
        for i in movable:
            extra = min(most - counts[i], max(1, budget * loads[i] // mass), spare)
            counts[i] = counts[i] + extra
            spare = spare - extra
    return np.array([most] + counts)


def ragged_sizes(stream_key, count, total, limit, lean):
    if count == 2:
        one = jax.random.randint(stream_key, (), max(1, total - limit), min(limit, total - 1) + 1)
        return jnp.stack([one, total - one])
    sizes = jnp.asarray(profile(count, total, limit, lean), jnp.int32)
    twos = (count - 1) // 2
    source_of, taker = sizes[1:1 + 2 * twos:2], sizes[2:2 + 2 * twos:2]
    slack = jnp.minimum(source_of - 1, limit - taker)
    shifted = jax.random.randint(jax.random.fold_in(stream_key, 1), (twos,), 0, 1 << 20) % (slack + 1)
    sizes = sizes.at[1:1 + 2 * twos:2].set(source_of - shifted).at[2:2 + 2 * twos:2].set(taker + shifted)
    return sizes[jax.random.permutation(jax.random.fold_in(stream_key, 2), count)]


def scatter_about(key, shape, scale, bound, shards=(), kind=jnp.bfloat16):
    factor_of = level_of(key, shape, shards, -0.22, 0.18) if shards else 1.0
    values = jax.random.normal(key, shape, jnp.float32) * scale * factor_of
    return jnp.minimum(jnp.maximum(values, -bound), bound).astype(kind)


def setup_inputs(seed: int = 0) -> dict:
    arg_keys = jax.random.split(jax.random.key(seed), 8)
    tokens = draw_tokens(jax.random.fold_in(arg_keys[7], 71), 0)
    norm_gain = jnp.clip(1.0 + 0.18 * jax.random.normal(arg_keys[1], (D,), jnp.float32), 0.099609375, 1.8984375).astype(jnp.bfloat16)
    query_weight = draw_query_weight(jax.random.fold_in(arg_keys[7], 71), 0)
    kv_weight = draw_kv_weight(jax.random.fold_in(arg_keys[7], 71), 0)
    out_weight = scatter_about(arg_keys[4], (H * HD, D), (H * HD) ** -0.5, 0.09375, ((0, 16), (1, 32)))
    grad_out = scatter_about(arg_keys[5], (TOKENS, D), 1.0, 6.0, ((0, 512),))
    doc_lengths = jax.vmap(lambda own: ragged_sizes(own, NDOC, SEQ, SEQ // 2, 0))(jax.random.split(arg_keys[6], REPLICAS)).reshape((REPLICAS, NDOC)).astype(jnp.int32)
    return {"tokens": tokens, "norm_gain": norm_gain, "query_weight": query_weight, "kv_weight": kv_weight, "out_weight": out_weight, "grad_out": grad_out, "doc_lengths": doc_lengths}


epsilon = 1e-05

def rounded(value):
    return lax.optimization_barrier(value.astype(jnp.bfloat16)).astype(jnp.float32)

def document_mask(lengths, length_total):
    ends = jnp.cumsum(lengths.astype(jnp.int32)).astype(jnp.int32)
    positions = jnp.arange(length_total, dtype=jnp.int32)
    labels = lax.optimization_barrier(jnp.sum((ends[None, :] <= positions[:, None]).astype(jnp.int32), axis=1))
    return (labels[:, None] == labels[None, :]) & (positions[None, :] <= positions[:, None])

def reference(tokens, norm_gain, query_weight, kv_weight, out_weight, grad_out, doc_lengths):
    group = H // KVH
    query_cols = H * HD // N_TENSOR
    kv_cols = 2 * HD * KVH // N_TENSOR
    gain32 = norm_gain.astype(jnp.float32)
    query_blocks = query_weight.astype(jnp.float32).reshape(D, N_TENSOR, query_cols)
    kv_blocks = kv_weight.astype(jnp.float32).reshape(D, N_TENSOR, kv_cols)

    def replica(carry, inputs):
        row_block, grad_block, lengths = inputs
        values32 = row_block.astype(jnp.float32)
        root_mean = jnp.sqrt(lax.optimization_barrier(jnp.mean(values32 * values32, axis=-1)) + epsilon)
        unit = values32 / root_mean[:, None]
        normed = (unit * gain32).astype(jnp.bfloat16)
        queries = jnp.dot(normed, query_weight, preferred_element_type=jnp.float32).astype(jnp.bfloat16)
        keyvals = jnp.dot(normed, kv_weight, preferred_element_type=jnp.float32).astype(jnp.bfloat16)
        keyvals = keyvals.astype(jnp.float32).reshape(SEQ, KVH, 2, HD)
        key_rows = keyvals[:, :, 0]
        value_rows = keyvals[:, :, 1]
        grouped = queries.astype(jnp.float32).reshape(SEQ, KVH, group, HD)
        allowed = document_mask(lengths, SEQ)
        scores = jnp.einsum('qkgd,tkd->kgqt', grouped, key_rows) / math.sqrt(HD)
        scores = jnp.where(allowed, scores, -1e+30)
        peak = lax.optimization_barrier(jnp.max(scores, axis=-1, keepdims=True))
        expo = jnp.exp(scores - peak)
        probs = expo / lax.optimization_barrier(jnp.sum(expo, axis=-1, keepdims=True))
        probs_low = rounded(probs)
        out_grad = jnp.dot(grad_block, out_weight.T, preferred_element_type=jnp.float32)
        out_heads = rounded(out_grad).reshape(SEQ, KVH, group, HD)
        prob_grad = jnp.einsum('qkgd,tkd->kgqt', out_heads, value_rows)
        inner = lax.optimization_barrier(jnp.sum(probs * prob_grad, axis=-1, keepdims=True))
        score_grad = rounded(probs * (prob_grad - inner) / math.sqrt(HD))
        query_grad = jnp.einsum('kgqt,tkd->qkgd', score_grad, key_rows).astype(jnp.bfloat16).reshape(SEQ, H * HD)
        key_grad = jnp.einsum('kgqt,qkgd->tkd', score_grad, grouped)
        value_grad = jnp.einsum('kgqt,qkgd->tkd', probs_low, out_heads)
        kv_grad = jnp.stack([key_grad, value_grad], axis=2).astype(jnp.bfloat16).reshape(SEQ, KVH * 2 * HD)
        query_parts = jnp.einsum('snc,dnc->nsd', query_grad.astype(jnp.float32).reshape(SEQ, N_TENSOR, query_cols), query_blocks)
        kv_parts = jnp.einsum('snc,dnc->nsd', kv_grad.astype(jnp.float32).reshape(SEQ, N_TENSOR, kv_cols), kv_blocks)
        normed_grad = lax.optimization_barrier(jnp.sum(rounded(query_parts + kv_parts), axis=0))
        scaled = normed_grad * gain32
        input_grad = (grad_block.astype(jnp.float32) + (scaled - unit * lax.optimization_barrier(jnp.mean(scaled * unit, axis=-1, keepdims=True))) / root_mean[:, None]).astype(jnp.bfloat16)
        query_wgrad = jnp.dot(normed.T, query_grad, preferred_element_type=jnp.float32)
        kv_wgrad = jnp.dot(normed.T, kv_grad, preferred_element_type=jnp.float32)
        return ((carry[0] + rounded(query_wgrad), carry[1] + rounded(kv_wgrad)), input_grad)
    start_sums = (jnp.zeros((D, H * HD), jnp.float32), jnp.zeros((D, 2 * KVH * HD), jnp.float32))
    sums, input_grads = lax.scan(replica, start_sums, (tokens.reshape(N_DP, SEQ, D), grad_out.reshape(N_DP, SEQ, D), doc_lengths))
    return (input_grads.reshape(TOKENS, D), sums[0] / N_DP, sums[1] / N_DP)
```

```python
import functools
import math

import jax
import jax.numpy as jnp
from jax import lax
from jax.experimental import pallas as pl
from jax.experimental.pallas import tpu as pltpu
from jax.sharding import PartitionSpec as P

KVH = 4
HD = 128
MESH_ID = pl.DeviceIdType.MESH


epsilon = 1e-05


def partner_2(value, axis, bit):
    mask = 2**bit
    pairs = [(source, source ^ mask) for source in range(lax.axis_size(axis))]
    return lax.ppermute(value, axis, pairs)


def document_mask(lengths, length_total):
    ends = jnp.cumsum(lengths)
    positions = jnp.arange(length_total, dtype=jnp.int32)
    labels = jnp.sum((ends[None, :] <= positions[:, None]).astype(jnp.int32), axis=1)
    return (labels[:, None] == labels[None, :]) & (positions[None, :] <= positions[:, None])


def _enter(axis, n):
    me = lax.axis_index(axis)
    barrier = pltpu.get_barrier_semaphore()
    for j in range(1, n):
        pl.semaphore_signal(
            barrier, inc=1, device_id={axis: lax.rem(me + j, n)}, device_id_type=MESH_ID
        )
    pl.semaphore_wait(barrier, n - 1)
    return me


def _gather_body(axis, n, count, *refs):
    ins = refs[:count]
    outs = refs[count : 2 * count]
    send_sem, recv_sem, local_sem = refs[2 * count :]
    me = _enter(axis, n)
    local = []
    for i in range(count):
        copy = pltpu.make_async_copy(ins[i], outs[i].at[me], local_sem.at[i])
        copy.start()
        local.append(copy)
    remote = []
    for j in range(1, n):
        peer = lax.rem(me + j, n)
        for i in range(count):
            copy = pltpu.make_async_remote_copy(
                src_ref=ins[i],
                dst_ref=outs[i].at[me],
                send_sem=send_sem.at[i, j],
                recv_sem=recv_sem.at[i, j],
                device_id={axis: peer},
                device_id_type=MESH_ID,
            )
            copy.start()
            remote.append(copy)
    for copy in remote:
        copy.wait()
    for copy in local:
        copy.wait()


def push_gather(pieces, axis, n, cid):
    count = len(pieces)
    nbytes = sum(p.size * p.dtype.itemsize for p in pieces)
    return pl.pallas_call(
        functools.partial(_gather_body, axis, n, count),
        out_shape=[jax.ShapeDtypeStruct((n,) + p.shape, p.dtype) for p in pieces],
        in_specs=[pl.BlockSpec(memory_space=pl.ANY)] * count,
        out_specs=[pl.BlockSpec(memory_space=pl.ANY)] * count,
        scratch_shapes=[
            pltpu.SemaphoreType.DMA((count, n)),
            pltpu.SemaphoreType.DMA((count, n)),
            pltpu.SemaphoreType.DMA((count,)),
        ],
        compiler_params=pltpu.CompilerParams(collective_id=cid, has_side_effects=True),
        cost_estimate=pl.CostEstimate(
            flops=0, transcendentals=0, bytes_accessed=2 * n * nbytes
        ),
    )(*pieces)


def _scatter_body(axis, n, x_ref, o_ref, send_sem, recv_sem, local_sem):
    me = _enter(axis, n)
    local = pltpu.make_async_copy(x_ref.at[me], o_ref.at[me], local_sem)
    local.start()
    remote = []
    for j in range(1, n):
        peer = lax.rem(me + j, n)
        copy = pltpu.make_async_remote_copy(
            src_ref=x_ref.at[peer],
            dst_ref=o_ref.at[me],
            send_sem=send_sem.at[j],
            recv_sem=recv_sem.at[j],
            device_id={axis: peer},
            device_id_type=MESH_ID,
        )
        copy.start()
        remote.append(copy)
    for copy in remote:
        copy.wait()
    local.wait()


def push_scatter(x, axis, n, cid):
    nbytes = x.size * x.dtype.itemsize
    return pl.pallas_call(
        functools.partial(_scatter_body, axis, n),
        out_shape=jax.ShapeDtypeStruct(x.shape, x.dtype),
        in_specs=[pl.BlockSpec(memory_space=pl.ANY)],
        out_specs=pl.BlockSpec(memory_space=pl.ANY),
        scratch_shapes=[
            pltpu.SemaphoreType.DMA((n,)),
            pltpu.SemaphoreType.DMA((n,)),
            pltpu.SemaphoreType.DMA(()),
        ],
        compiler_params=pltpu.CompilerParams(collective_id=cid, has_side_effects=True),
        cost_estimate=pl.CostEstimate(flops=0, transcendentals=0, bytes_accessed=2 * nbytes),
    )(x)


def local(tokens, norm_gain, query_weight, kv_weight, out_weight, grad_out, doc_lengths):
    tensor_size = lax.axis_size("tensor")
    data_size = lax.axis_size("dp")
    tensor_index = lax.axis_index("tensor")
    sharers = tensor_size // KVH
    levels = sharers.bit_length() - 1
    contract_last = (((1,), (1,)), ((), ()))
    query_width = query_weight.shape[1]
    kv_width = kv_weight.shape[1]
    values32 = tokens.astype(jnp.float32)
    root_mean = jnp.sqrt(jnp.mean(values32 * values32, axis=-1) + epsilon)
    unit = values32 / root_mean[:, None]
    gain32 = norm_gain.astype(jnp.float32)
    normed_local = (unit * gain32).astype(jnp.bfloat16)
    rows = tokens.shape[0]
    normed_parts, grad_parts = push_gather([normed_local, grad_out], "tensor", tensor_size, 0)
    normed = normed_parts.reshape(tensor_size * rows, -1)
    grad_full = grad_parts.reshape(tensor_size * rows, -1)
    seq_length = normed.shape[0]
    weights_local = jnp.concatenate([query_weight, kv_weight, out_weight.T], axis=1)
    weights_full = lax.all_gather(weights_local, "dp", axis=0, tiled=True)
    query_full = weights_full[:, :query_width]
    kv_local = weights_full[:, query_width : query_width + kv_width]
    out_full_t = weights_full[:, query_width + kv_width :]
    queries = jnp.dot(normed, query_full, preferred_element_type=jnp.float32).astype(jnp.bfloat16)
    keyvals = jnp.dot(normed, kv_local, preferred_element_type=jnp.float32).astype(jnp.bfloat16)
    for bit_index in range(levels):
        partner = partner_2(keyvals, "tensor", bit_index)
        joined_upper_half = tensor_index >> bit_index & 1 == 1
        keyvals = jnp.concatenate(
            [
                jnp.where(joined_upper_half, partner, keyvals),
                jnp.where(joined_upper_half, keyvals, partner),
            ],
            axis=1,
        )
    key_rows = keyvals[:, :HD]
    value_rows = keyvals[:, HD:]
    out_grad = jnp.dot(grad_full, out_full_t, preferred_element_type=jnp.float32).astype(
        jnp.bfloat16
    )
    local_heads = queries.shape[1] // HD
    query_heads = queries.reshape(seq_length, local_heads, HD)
    out_heads = out_grad.reshape(seq_length, local_heads, HD)
    allowed = document_mask(doc_lengths[0], seq_length)
    scores = jnp.einsum(
        "qhd,td->hqt", query_heads, key_rows, preferred_element_type=jnp.float32
    ) / math.sqrt(HD)
    scores = jnp.where(allowed[None, :, :], scores, -1e30)
    peak = jnp.max(scores, axis=-1, keepdims=True)
    expo = jnp.exp(scores - peak)
    probs = expo / jnp.sum(expo, axis=-1, keepdims=True)
    probs_low = probs.astype(jnp.bfloat16)
    prob_grad = jnp.einsum("qhd,td->hqt", out_heads, value_rows, preferred_element_type=jnp.float32)
    inner = jnp.sum(probs * prob_grad, axis=-1, keepdims=True)
    score_grad = (probs * (prob_grad - inner) / math.sqrt(HD)).astype(jnp.bfloat16)
    query_grad = jnp.einsum("hqt,td->qhd", score_grad, key_rows, preferred_element_type=jnp.float32)
    query_grad = query_grad.astype(jnp.bfloat16).reshape(seq_length, local_heads * HD)
    key_part = jnp.einsum(
        "hqt,qhd->td", score_grad, query_heads, preferred_element_type=jnp.float32
    )
    value_part = jnp.einsum("hqt,qhd->td", probs_low, out_heads, preferred_element_type=jnp.float32)
    kv_partial = jnp.concatenate([key_part, value_part], axis=1)
    for bit_index in reversed(range(levels)):
        half_cols = kv_partial.shape[1] // 2
        upper_half = tensor_index >> bit_index & 1 == 1
        lower_cols = kv_partial[:, :half_cols]
        higher_cols = kv_partial[:, half_cols:]
        kept = jnp.where(upper_half, higher_cols, lower_cols)
        handed = jnp.where(upper_half, lower_cols, higher_cols)
        kv_partial = kept + partner_2(handed.astype(jnp.bfloat16), "tensor", bit_index).astype(
            handed.dtype
        )
    kv_grad = kv_partial.astype(jnp.bfloat16)
    from_query = lax.dot_general(
        query_grad, query_full, contract_last, preferred_element_type=jnp.float32
    )
    from_kv = lax.dot_general(kv_grad, kv_local, contract_last, preferred_element_type=jnp.float32)
    partial = (from_query + from_kv).astype(jnp.bfloat16).reshape(tensor_size, rows, -1)
    arrived = push_scatter(partial, "tensor", tensor_size, 1)
    normed_grad = jnp.sum(arrived.astype(jnp.float32), axis=0)
    scaled = normed_grad * gain32
    correction = unit * jnp.mean(scaled * unit, axis=-1, keepdims=True)
    input_grad = (grad_out.astype(jnp.float32) + (scaled - correction) / root_mean[:, None]).astype(
        jnp.bfloat16
    )
    combined = jnp.concatenate([query_grad, kv_grad], axis=1)
    weight_grads = (
        lax.psum_scatter(
            lax.dot_general(
                normed, combined, (((0,), (0,)), ((), ())), preferred_element_type=jnp.float32
            ).astype(jnp.bfloat16),
            "dp",
            scatter_dimension=0,
            tiled=True,
        ).astype(jnp.float32)
        / data_size
    )
    return (input_grad, weight_grads[:, :query_width], weight_grads[:, query_width:])


def solution(mesh):
    placed = (
        P(("dp", "tensor"), None),
        P(),
        P("dp", "tensor"),
        P("dp", "tensor"),
        P("tensor", "dp"),
        P(("dp", "tensor"), None),
        P("dp", None),
    )
    return jax.shard_map(
        local,
        mesh=mesh,
        in_specs=placed,
        out_specs=(P(("dp", "tensor"), None), P("dp", "tensor"), P("dp", "tensor")),
        check_vma=False,
    )
```

```python
import functools
import math

import jax
import jax.numpy as jnp
from jax import lax
from jax.experimental import pallas as pl
from jax.experimental.pallas import tpu as pltpu
from jax.sharding import PartitionSpec as P

KVH = 4
HD = 128
MESH_ID = pl.DeviceIdType.MESH


epsilon = 1e-05


def partner_2(value, axis, bit):
    mask = 2**bit
    pairs = [(source, source ^ mask) for source in range(lax.axis_size(axis))]
    return lax.ppermute(value, axis, pairs)


def document_mask(lengths, length_total):
    ends = jnp.cumsum(lengths)
    positions = jnp.arange(length_total, dtype=jnp.int32)
    labels = jnp.sum((ends[None, :] <= positions[:, None]).astype(jnp.int32), axis=1)
    return (labels[:, None] == labels[None, :]) & (positions[None, :] <= positions[:, None])


def _push_body(plan, *refs):
    count = len(plan)
    ins = refs[:count]
    outs = refs[count : 2 * count]
    send_sems = refs[2 * count : 3 * count]
    recv_sems = refs[3 * count : 4 * count]
    local_sem = refs[4 * count]
    barrier = pltpu.get_barrier_semaphore()
    mine = []
    expected = 0
    for axis, n, _ in plan:
        me = lax.axis_index(axis)
        mine.append(me)
        for j in range(1, n):
            pl.semaphore_signal(
                barrier, inc=1, device_id={axis: lax.rem(me + j, n)}, device_id_type=MESH_ID
            )
        expected += n - 1
    pl.semaphore_wait(barrier, expected)
    local = []
    for g, (axis, n, scatter) in enumerate(plan):
        me = mine[g]
        src = ins[g].at[me] if scatter else ins[g]
        copy = pltpu.make_async_copy(src, outs[g].at[me], local_sem.at[g])
        copy.start()
        local.append(copy)
    remote = []
    for j in range(1, max(n for _, n, _ in plan)):
        for g, (axis, n, scatter) in enumerate(plan):
            if j >= n:
                continue
            me = mine[g]
            peer = lax.rem(me + j, n)
            copy = pltpu.make_async_remote_copy(
                src_ref=ins[g].at[peer] if scatter else ins[g],
                dst_ref=outs[g].at[me],
                send_sem=send_sems[g].at[j],
                recv_sem=recv_sems[g].at[j],
                device_id={axis: peer},
                device_id_type=MESH_ID,
            )
            copy.start()
            remote.append(copy)
    for copy in remote:
        copy.wait()
    for copy in local:
        copy.wait()


def push_exchange(groups, cid):
    plan = tuple((axis, n, scatter) for axis, n, _, scatter in groups)
    arrays = [array for _, _, array, _ in groups]
    out_shape = []
    moved = 0
    for _, n, array, scatter in groups:
        shape = array.shape if scatter else (n,) + array.shape
        out_shape.append(jax.ShapeDtypeStruct(shape, array.dtype))
        moved += 2 * math.prod(shape) * array.dtype.itemsize
    count = len(groups)
    return pl.pallas_call(
        functools.partial(_push_body, plan),
        out_shape=out_shape,
        in_specs=[pl.BlockSpec(memory_space=pl.ANY)] * count,
        out_specs=[pl.BlockSpec(memory_space=pl.ANY)] * count,
        scratch_shapes=[pltpu.SemaphoreType.DMA((n,)) for _, n, _, _ in groups]
        + [pltpu.SemaphoreType.DMA((n,)) for _, n, _, _ in groups]
        + [pltpu.SemaphoreType.DMA((count,))],
        compiler_params=pltpu.CompilerParams(collective_id=cid, has_side_effects=True),
        cost_estimate=pl.CostEstimate(flops=0, transcendentals=0, bytes_accessed=moved),
    )(*arrays)


def local(tokens, norm_gain, query_weight, kv_weight, out_weight, grad_out, doc_lengths):
    tensor_size = lax.axis_size("tensor")
    data_size = lax.axis_size("dp")
    tensor_index = lax.axis_index("tensor")
    sharers = tensor_size // KVH
    levels = sharers.bit_length() - 1
    contract_last = (((1,), (1,)), ((), ()))
    query_width = query_weight.shape[1]
    kv_width = kv_weight.shape[1]
    values32 = tokens.astype(jnp.float32)
    root_mean = jnp.sqrt(jnp.mean(values32 * values32, axis=-1) + epsilon)
    unit = values32 / root_mean[:, None]
    gain32 = norm_gain.astype(jnp.float32)
    normed_local = (unit * gain32).astype(jnp.bfloat16)
    rows = tokens.shape[0]
    normed_parts, grad_parts = push_exchange(
        [("tensor", tensor_size, normed_local, False), ("tensor", tensor_size, grad_out, False)], 0
    )
    normed = normed_parts.reshape(tensor_size * rows, -1)
    grad_full = grad_parts.reshape(tensor_size * rows, -1)
    seq_length = normed.shape[0]
    weights_local = jnp.concatenate([query_weight, kv_weight, out_weight.T], axis=1)
    weights_full = lax.all_gather(weights_local, "dp", axis=0, tiled=True)
    query_full = weights_full[:, :query_width]
    kv_local = weights_full[:, query_width : query_width + kv_width]
    out_full_t = weights_full[:, query_width + kv_width :]
    queries = jnp.dot(normed, query_full, preferred_element_type=jnp.float32).astype(jnp.bfloat16)
    keyvals = jnp.dot(normed, kv_local, preferred_element_type=jnp.float32).astype(jnp.bfloat16)
    for bit_index in range(levels):
        partner = partner_2(keyvals, "tensor", bit_index)
        joined_upper_half = tensor_index >> bit_index & 1 == 1
        keyvals = jnp.concatenate(
            [
                jnp.where(joined_upper_half, partner, keyvals),
                jnp.where(joined_upper_half, keyvals, partner),
            ],
            axis=1,
        )
    key_rows = keyvals[:, :HD]
    value_rows = keyvals[:, HD:]
    out_grad = jnp.dot(grad_full, out_full_t, preferred_element_type=jnp.float32).astype(
        jnp.bfloat16
    )
    local_heads = queries.shape[1] // HD
    query_heads = queries.reshape(seq_length, local_heads, HD)
    out_heads = out_grad.reshape(seq_length, local_heads, HD)
    allowed = document_mask(doc_lengths[0], seq_length)
    scores = jnp.einsum(
        "qhd,td->hqt", query_heads, key_rows, preferred_element_type=jnp.float32
    ) / math.sqrt(HD)
    scores = jnp.where(allowed[None, :, :], scores, -1e30)
    peak = jnp.max(scores, axis=-1, keepdims=True)
    expo = jnp.exp(scores - peak)
    probs = expo / jnp.sum(expo, axis=-1, keepdims=True)
    probs_low = probs.astype(jnp.bfloat16)
    prob_grad = jnp.einsum("qhd,td->hqt", out_heads, value_rows, preferred_element_type=jnp.float32)
    inner = jnp.sum(probs * prob_grad, axis=-1, keepdims=True)
    score_grad = (probs * (prob_grad - inner) / math.sqrt(HD)).astype(jnp.bfloat16)
    query_grad = jnp.einsum("hqt,td->qhd", score_grad, key_rows, preferred_element_type=jnp.float32)
    query_grad = query_grad.astype(jnp.bfloat16).reshape(seq_length, local_heads * HD)
    key_part = jnp.einsum(
        "hqt,qhd->td", score_grad, query_heads, preferred_element_type=jnp.float32
    )
    value_part = jnp.einsum("hqt,qhd->td", probs_low, out_heads, preferred_element_type=jnp.float32)
    kv_partial = jnp.concatenate([key_part, value_part], axis=1)
    for bit_index in reversed(range(levels)):
        half_cols = kv_partial.shape[1] // 2
        upper_half = tensor_index >> bit_index & 1 == 1
        lower_cols = kv_partial[:, :half_cols]
        higher_cols = kv_partial[:, half_cols:]
        kept = jnp.where(upper_half, higher_cols, lower_cols)
        handed = jnp.where(upper_half, lower_cols, higher_cols)
        kv_partial = kept + partner_2(handed.astype(jnp.bfloat16), "tensor", bit_index).astype(
            handed.dtype
        )
    kv_grad = kv_partial.astype(jnp.bfloat16)
    from_query = lax.dot_general(
        query_grad, query_full, contract_last, preferred_element_type=jnp.float32
    )
    from_kv = lax.dot_general(kv_grad, kv_local, contract_last, preferred_element_type=jnp.float32)
    partial = (from_query + from_kv).astype(jnp.bfloat16).reshape(tensor_size, rows, -1)
    combined = jnp.concatenate([query_grad, kv_grad], axis=1)
    weight_partial = lax.dot_general(
        normed, combined, (((0,), (0,)), ((), ())), preferred_element_type=jnp.float32
    ).astype(jnp.bfloat16)
    weight_partial = weight_partial.reshape(data_size, -1, weight_partial.shape[1])
    arrived, weight_arrived = push_exchange(
        [("tensor", tensor_size, partial, True), ("dp", data_size, weight_partial, True)], 1
    )
    normed_grad = jnp.sum(arrived.astype(jnp.float32), axis=0)
    scaled = normed_grad * gain32
    correction = unit * jnp.mean(scaled * unit, axis=-1, keepdims=True)
    input_grad = (grad_out.astype(jnp.float32) + (scaled - correction) / root_mean[:, None]).astype(
        jnp.bfloat16
    )
    weight_grads = jnp.sum(weight_arrived.astype(jnp.float32), axis=0) / data_size
    return (input_grad, weight_grads[:, :query_width], weight_grads[:, query_width:])


def solution(mesh):
    placed = (
        P(("dp", "tensor"), None),
        P(),
        P("dp", "tensor"),
        P("dp", "tensor"),
        P("tensor", "dp"),
        P(("dp", "tensor"), None),
        P("dp", None),
    )
    return jax.shard_map(
        local,
        mesh=mesh,
        in_specs=placed,
        out_specs=(P(("dp", "tensor"), None), P("dp", "tensor"), P("dp", "tensor")),
        check_vma=False,
    )
```

```python
import functools
import math

import jax
import jax.numpy as jnp
from jax import lax
from jax.experimental import pallas as pl
from jax.experimental.pallas import tpu as pltpu
from jax.sharding import PartitionSpec as P

KVH = 4
HD = 128
MESH_ID = pl.DeviceIdType.MESH
RING = 8


epsilon = 1e-05


def partner_2(value, axis, bit):
    mask = 2**bit
    pairs = [(source, source ^ mask) for source in range(lax.axis_size(axis))]
    return lax.ppermute(value, axis, pairs)


def document_mask(lengths, length_total):
    ends = jnp.cumsum(lengths)
    positions = jnp.arange(length_total, dtype=jnp.int32)
    labels = jnp.sum((ends[None, :] <= positions[:, None]).astype(jnp.int32), axis=1)
    return (labels[:, None] == labels[None, :]) & (positions[None, :] <= positions[:, None])


def _push_body(plan, *refs):
    count = len(plan)
    ins = refs[:count]
    outs = refs[count : 2 * count]
    send_sems = refs[2 * count : 3 * count]
    recv_sems = refs[3 * count : 4 * count]
    local_sem = refs[4 * count]
    barrier = pltpu.get_barrier_semaphore()
    mine = []
    expected = 0
    for axis, n, _ in plan:
        me = lax.axis_index(axis)
        mine.append(me)
        for j in range(1, n):
            pl.semaphore_signal(
                barrier, inc=1, device_id={axis: lax.rem(me + j, n)}, device_id_type=MESH_ID
            )
        expected += n - 1
    pl.semaphore_wait(barrier, expected)
    local = []
    for g, (axis, n, scatter) in enumerate(plan):
        me = mine[g]
        src = ins[g].at[me] if scatter else ins[g]
        copy = pltpu.make_async_copy(src, outs[g].at[me], local_sem.at[g])
        copy.start()
        local.append(copy)
    remote = []
    for j in range(1, max(n for _, n, _ in plan)):
        for g, (axis, n, scatter) in enumerate(plan):
            if j >= n:
                continue
            me = mine[g]
            peer = lax.rem(me + j, n)
            copy = pltpu.make_async_remote_copy(
                src_ref=ins[g].at[peer] if scatter else ins[g],
                dst_ref=outs[g].at[me],
                send_sem=send_sems[g].at[j],
                recv_sem=recv_sems[g].at[j],
                device_id={axis: peer},
                device_id_type=MESH_ID,
            )
            copy.start()
            remote.append(copy)
    for copy in remote:
        copy.wait()
    for copy in local:
        copy.wait()


def push_exchange(groups, cid):
    plan = tuple((axis, n, scatter) for axis, n, _, scatter in groups)
    arrays = [array for _, _, array, _ in groups]
    out_shape = []
    moved = 0
    for _, n, array, scatter in groups:
        shape = array.shape if scatter else (n,) + array.shape
        out_shape.append(jax.ShapeDtypeStruct(shape, array.dtype))
        moved += 2 * math.prod(shape) * array.dtype.itemsize
    count = len(groups)
    return pl.pallas_call(
        functools.partial(_push_body, plan),
        out_shape=out_shape,
        in_specs=[pl.BlockSpec(memory_space=pl.ANY)] * count,
        out_specs=[pl.BlockSpec(memory_space=pl.ANY)] * count,
        scratch_shapes=[pltpu.SemaphoreType.DMA((n,)) for _, n, _, _ in groups]
        + [pltpu.SemaphoreType.DMA((n,)) for _, n, _, _ in groups]
        + [pltpu.SemaphoreType.DMA((count,))],
        compiler_params=pltpu.CompilerParams(collective_id=cid, has_side_effects=True),
        cost_estimate=pl.CostEstimate(flops=0, transcendentals=0, bytes_accessed=moved),
    )(*arrays)


def _gather_start_body(ring, pieces_ref, weights_ref, tens_out, dp_out, ring_send, ring_recv,
                       cross_sem, dp_send, dp_recv, local_sem):
    n_t = lax.axis_size("tensor")
    n_d = lax.axis_size("dp")
    t = lax.axis_index("tensor")
    r = lax.axis_index("dp")
    z = lax.rem(t, ring)
    base = t - z
    other = lax.rem(t + ring, n_t) - z
    cross = lax.rem(t + ring, n_t)
    right = base + lax.rem(z + 1, ring)
    left = base + lax.rem(z + ring - 1, ring)
    pair = r + 1 - 2 * lax.rem(r, 2)
    peers = n_d // 2
    barrier = pltpu.get_barrier_semaphore()
    for device in ({"tensor": cross}, {"tensor": right}, {"tensor": left}, {"dp": pair}):
        pl.semaphore_signal(barrier, inc=1, device_id=device, device_id_type=MESH_ID)
    for k in range(1, peers):
        pl.semaphore_signal(
            barrier, inc=1, device_id={"dp": lax.rem(r + 2 * k, n_d)}, device_id_type=MESH_ID
        )
    pl.semaphore_wait(barrier, 4 + peers - 1)

    def remote(src, dst, send, recv, device):
        copy = pltpu.make_async_remote_copy(
            src_ref=src, dst_ref=dst, send_sem=send, recv_sem=recv,
            device_id=device, device_id_type=MESH_ID,
        )
        copy.start()
        return copy

    waits = []
    for k in range(1, peers):
        waits.append(remote(weights_ref, dp_out.at[r], dp_send.at[0, k], dp_recv.at[0, k],
                            {"dp": lax.rem(r + 2 * k, n_d)}))
    waits.append(remote(weights_ref, dp_out.at[r], dp_send.at[0, 0], dp_recv.at[0, 0],
                        {"dp": pair}))
    crossed = remote(pieces_ref, tens_out.at[t], cross_sem.at[0], cross_sem.at[1],
                     {"tensor": cross})
    own_t = pltpu.make_async_copy(pieces_ref, tens_out.at[t], local_sem.at[0])
    own_t.start()
    own_d = pltpu.make_async_copy(weights_ref, dp_out.at[r], local_sem.at[1])
    own_d.start()
    crossed.wait()
    steps = (ring // 2, ring - 1 - ring // 2)
    moving = [None, None]
    for s in range(max(steps)):
        for d, (target, sign) in enumerate(((right, -1), (left, 1))):
            if s >= steps[d]:
                continue
            if s > 0:
                for copy in moving[d]:
                    copy.wait_recv()
            origin = lax.rem(z + sign * s + ring, ring)
            sent = []
            for h, start in enumerate((base, other)):
                slot = start + origin
                src = pieces_ref if (s == 0 and h == 0) else tens_out.at[slot]
                sent.append(remote(src, tens_out.at[slot], ring_send.at[d, s, h],
                                   ring_recv.at[d, s, h], {"tensor": target}))
            waits.extend(sent)
            moving[d] = sent
    for d in range(2):
        for copy in moving[d]:
            copy.wait_recv()
    for k in range(1, peers):
        slot = lax.rem(r + n_d - 2 * k, n_d)
        arrival = pltpu.make_async_copy(dp_out.at[slot], dp_out.at[slot], dp_recv.at[0, k])
        arrival.wait()
        waits.append(remote(dp_out.at[slot], dp_out.at[slot], dp_send.at[1, k],
                            dp_recv.at[1, k], {"dp": pair}))
    for copy in waits:
        copy.wait_send()
    pltpu.make_async_copy(dp_out.at[r], dp_out.at[r], dp_recv.at[0, 0]).wait()
    for k in range(1, peers):
        slot = lax.rem(pair + n_d - 2 * k, n_d)
        pltpu.make_async_copy(dp_out.at[slot], dp_out.at[slot], dp_recv.at[1, k]).wait()
    own_t.wait()
    own_d.wait()


def gather_start(pieces, weights, ring):
    n_t = lax.axis_size("tensor")
    n_d = lax.axis_size("dp")
    moved = 2 * (n_t * pieces.size * pieces.dtype.itemsize + n_d * weights.size * weights.dtype.itemsize)
    return pl.pallas_call(
        functools.partial(_gather_start_body, ring),
        out_shape=[
            jax.ShapeDtypeStruct((n_t,) + pieces.shape, pieces.dtype),
            jax.ShapeDtypeStruct((n_d,) + weights.shape, weights.dtype),
        ],
        in_specs=[pl.BlockSpec(memory_space=pl.ANY)] * 2,
        out_specs=[pl.BlockSpec(memory_space=pl.ANY)] * 2,
        scratch_shapes=[
            pltpu.SemaphoreType.DMA((2, ring // 2, 2)),
            pltpu.SemaphoreType.DMA((2, ring // 2, 2)),
            pltpu.SemaphoreType.DMA((2,)),
            pltpu.SemaphoreType.DMA((2, n_d // 2)),
            pltpu.SemaphoreType.DMA((2, n_d // 2)),
            pltpu.SemaphoreType.DMA((2,)),
        ],
        compiler_params=pltpu.CompilerParams(collective_id=0, has_side_effects=True),
        cost_estimate=pl.CostEstimate(flops=0, transcendentals=0, bytes_accessed=moved),
    )(pieces, weights)


def local(tokens, norm_gain, query_weight, kv_weight, out_weight, grad_out, doc_lengths):
    tensor_size = lax.axis_size("tensor")
    data_size = lax.axis_size("dp")
    tensor_index = lax.axis_index("tensor")
    sharers = tensor_size // KVH
    levels = sharers.bit_length() - 1
    contract_last = (((1,), (1,)), ((), ()))
    query_width = query_weight.shape[1]
    kv_width = kv_weight.shape[1]
    values32 = tokens.astype(jnp.float32)
    root_mean = jnp.sqrt(jnp.mean(values32 * values32, axis=-1) + epsilon)
    unit = values32 / root_mean[:, None]
    gain32 = norm_gain.astype(jnp.float32)
    normed_local = (unit * gain32).astype(jnp.bfloat16)
    rows = tokens.shape[0]
    pieces = jnp.stack([normed_local, grad_out])
    weights_local = jnp.concatenate([query_weight, kv_weight, out_weight.T], axis=1)
    tens_parts, weight_parts = gather_start(pieces, weights_local, RING)
    normed = tens_parts[:, 0].reshape(tensor_size * rows, -1)
    grad_full = tens_parts[:, 1].reshape(tensor_size * rows, -1)
    seq_length = normed.shape[0]
    weights_full = weight_parts.reshape(-1, weights_local.shape[1])
    query_full = weights_full[:, :query_width]
    kv_local = weights_full[:, query_width : query_width + kv_width]
    out_full_t = weights_full[:, query_width + kv_width :]
    queries = jnp.dot(normed, query_full, preferred_element_type=jnp.float32).astype(jnp.bfloat16)
    keyvals = jnp.dot(normed, kv_local, preferred_element_type=jnp.float32).astype(jnp.bfloat16)
    for bit_index in range(levels):
        partner = partner_2(keyvals, "tensor", bit_index)
        joined_upper_half = tensor_index >> bit_index & 1 == 1
        keyvals = jnp.concatenate(
            [
                jnp.where(joined_upper_half, partner, keyvals),
                jnp.where(joined_upper_half, keyvals, partner),
            ],
            axis=1,
        )
    key_rows = keyvals[:, :HD]
    value_rows = keyvals[:, HD:]
    out_grad = jnp.dot(grad_full, out_full_t, preferred_element_type=jnp.float32).astype(
        jnp.bfloat16
    )
    local_heads = queries.shape[1] // HD
    query_heads = queries.reshape(seq_length, local_heads, HD)
    out_heads = out_grad.reshape(seq_length, local_heads, HD)
    allowed = document_mask(doc_lengths[0], seq_length)
    scores = jnp.einsum(
        "qhd,td->hqt", query_heads, key_rows, preferred_element_type=jnp.float32
    ) / math.sqrt(HD)
    scores = jnp.where(allowed[None, :, :], scores, -1e30)
    peak = jnp.max(scores, axis=-1, keepdims=True)
    expo = jnp.exp(scores - peak)
    probs = expo / jnp.sum(expo, axis=-1, keepdims=True)
    probs_low = probs.astype(jnp.bfloat16)
    prob_grad = jnp.einsum("qhd,td->hqt", out_heads, value_rows, preferred_element_type=jnp.float32)
    inner = jnp.sum(probs * prob_grad, axis=-1, keepdims=True)
    score_grad = (probs * (prob_grad - inner) / math.sqrt(HD)).astype(jnp.bfloat16)
    query_grad = jnp.einsum("hqt,td->qhd", score_grad, key_rows, preferred_element_type=jnp.float32)
    query_grad = query_grad.astype(jnp.bfloat16).reshape(seq_length, local_heads * HD)
    key_part = jnp.einsum(
        "hqt,qhd->td", score_grad, query_heads, preferred_element_type=jnp.float32
    )
    value_part = jnp.einsum("hqt,qhd->td", probs_low, out_heads, preferred_element_type=jnp.float32)
    kv_partial = jnp.concatenate([key_part, value_part], axis=1)
    for bit_index in reversed(range(levels)):
        half_cols = kv_partial.shape[1] // 2
        upper_half = tensor_index >> bit_index & 1 == 1
        lower_cols = kv_partial[:, :half_cols]
        higher_cols = kv_partial[:, half_cols:]
        kept = jnp.where(upper_half, higher_cols, lower_cols)
        handed = jnp.where(upper_half, lower_cols, higher_cols)
        kv_partial = kept + partner_2(handed.astype(jnp.bfloat16), "tensor", bit_index).astype(
            handed.dtype
        )
    kv_grad = kv_partial.astype(jnp.bfloat16)
    from_query = lax.dot_general(
        query_grad, query_full, contract_last, preferred_element_type=jnp.float32
    )
    from_kv = lax.dot_general(kv_grad, kv_local, contract_last, preferred_element_type=jnp.float32)
    partial = (from_query + from_kv).astype(jnp.bfloat16).reshape(tensor_size, rows, -1)
    combined = jnp.concatenate([query_grad, kv_grad], axis=1)
    weight_partial = lax.dot_general(
        normed, combined, (((0,), (0,)), ((), ())), preferred_element_type=jnp.float32
    ).astype(jnp.bfloat16)
    weight_partial = weight_partial.reshape(data_size, -1, weight_partial.shape[1])
    arrived, weight_arrived = push_exchange(
        [("tensor", tensor_size, partial, True), ("dp", data_size, weight_partial, True)], 1
    )
    normed_grad = jnp.sum(arrived.astype(jnp.float32), axis=0)
    scaled = normed_grad * gain32
    correction = unit * jnp.mean(scaled * unit, axis=-1, keepdims=True)
    input_grad = (grad_out.astype(jnp.float32) + (scaled - correction) / root_mean[:, None]).astype(
        jnp.bfloat16
    )
    weight_grads = jnp.sum(weight_arrived.astype(jnp.float32), axis=0) / data_size
    return (input_grad, weight_grads[:, :query_width], weight_grads[:, query_width:])


def solution(mesh):
    placed = (
        P(("dp", "tensor"), None),
        P(),
        P("dp", "tensor"),
        P("dp", "tensor"),
        P("tensor", "dp"),
        P(("dp", "tensor"), None),
        P("dp", None),
    )
    return jax.shard_map(
        local,
        mesh=mesh,
        in_specs=placed,
        out_specs=(P(("dp", "tensor"), None), P("dp", "tensor"), P("dp", "tensor")),
        check_vma=False,
    )
```

```python
import functools
import math

import jax
import jax.numpy as jnp
from jax import lax
from jax.experimental import pallas as pl
from jax.experimental.pallas import tpu as pltpu
from jax.sharding import PartitionSpec as P

KVH = 4
HD = 128
MESH_ID = pl.DeviceIdType.MESH
RING = 8


epsilon = 1e-05


def document_mask(lengths, length_total):
    ends = jnp.cumsum(lengths)
    positions = jnp.arange(length_total, dtype=jnp.int32)
    labels = jnp.sum((ends[None, :] <= positions[:, None]).astype(jnp.int32), axis=1)
    return (labels[:, None] == labels[None, :]) & (positions[None, :] <= positions[:, None])


def _push_body(plan, *refs):
    count = len(plan)
    ins = refs[:count]
    outs = refs[count : 2 * count]
    send_sems = refs[2 * count : 3 * count]
    recv_sems = refs[3 * count : 4 * count]
    local_sem = refs[4 * count]
    barrier = pltpu.get_barrier_semaphore()
    mine = []
    expected = 0
    places = []
    for axis, n, _, stride in plan:
        index = lax.axis_index(axis)
        me = lax.rem(index // stride, n)
        offset = index - me * stride
        mine.append(me)
        places.append(functools.partial(lambda o, st, p: o + p * st, offset, stride))
        for j in range(1, n):
            pl.semaphore_signal(
                barrier,
                inc=1,
                device_id={axis: places[-1](lax.rem(me + j, n))},
                device_id_type=MESH_ID,
            )
        expected += n - 1
    pl.semaphore_wait(barrier, expected)
    local = []
    for g, (axis, n, scatter, _) in enumerate(plan):
        me = mine[g]
        src = ins[g].at[me] if scatter else ins[g]
        copy = pltpu.make_async_copy(src, outs[g].at[me], local_sem.at[g])
        copy.start()
        local.append(copy)
    remote = []
    for j in range(1, max(n for _, n, _, _ in plan)):
        for g, (axis, n, scatter, _) in enumerate(plan):
            if j >= n:
                continue
            me = mine[g]
            peer = lax.rem(me + j, n)
            copy = pltpu.make_async_remote_copy(
                src_ref=ins[g].at[peer] if scatter else ins[g],
                dst_ref=outs[g].at[me],
                send_sem=send_sems[g].at[j],
                recv_sem=recv_sems[g].at[j],
                device_id={axis: places[g](peer)},
                device_id_type=MESH_ID,
            )
            copy.start()
            remote.append(copy)
    for copy in remote:
        copy.wait()
    for copy in local:
        copy.wait()


def push_exchange(groups, cid):
    groups = [g if len(g) == 5 else g + (1,) for g in groups]
    plan = tuple((axis, n, scatter, stride) for axis, n, _, scatter, stride in groups)
    arrays = [array for _, _, array, _, _ in groups]
    out_shape = []
    moved = 0
    for _, n, array, scatter, _ in groups:
        shape = array.shape if scatter else (n,) + array.shape
        out_shape.append(jax.ShapeDtypeStruct(shape, array.dtype))
        moved += 2 * math.prod(shape) * array.dtype.itemsize
    count = len(groups)
    return pl.pallas_call(
        functools.partial(_push_body, plan),
        out_shape=out_shape,
        in_specs=[pl.BlockSpec(memory_space=pl.ANY)] * count,
        out_specs=[pl.BlockSpec(memory_space=pl.ANY)] * count,
        scratch_shapes=[pltpu.SemaphoreType.DMA((n,)) for _, n, _, _, _ in groups]
        + [pltpu.SemaphoreType.DMA((n,)) for _, n, _, _, _ in groups]
        + [pltpu.SemaphoreType.DMA((count,))],
        compiler_params=pltpu.CompilerParams(collective_id=cid, has_side_effects=True),
        cost_estimate=pl.CostEstimate(flops=0, transcendentals=0, bytes_accessed=moved),
    )(*arrays)


def _gather_start_body(ring, chunks, pieces_ref, weights_ref, tens_out, dp_out, ring_send, ring_recv,
                       cross_sem, dp_send, dp_recv, local_sem):
    n_t = lax.axis_size("tensor")
    n_d = lax.axis_size("dp")
    t = lax.axis_index("tensor")
    r = lax.axis_index("dp")
    z = lax.rem(t, ring)
    base = t - z
    other = lax.rem(t + ring, n_t) - z
    cross = lax.rem(t + ring, n_t)
    right = base + lax.rem(z + 1, ring)
    left = base + lax.rem(z + ring - 1, ring)
    pair = r + 1 - 2 * lax.rem(r, 2)
    peers = n_d // 2
    barrier = pltpu.get_barrier_semaphore()
    for device in ({"tensor": cross}, {"tensor": right}, {"tensor": left}, {"dp": pair}):
        pl.semaphore_signal(barrier, inc=1, device_id=device, device_id_type=MESH_ID)
    for k in range(1, peers):
        pl.semaphore_signal(
            barrier, inc=1, device_id={"dp": lax.rem(r + 2 * k, n_d)}, device_id_type=MESH_ID
        )
    pl.semaphore_wait(barrier, 4 + peers - 1)

    def remote(src, dst, send, recv, device):
        copy = pltpu.make_async_remote_copy(
            src_ref=src, dst_ref=dst, send_sem=send, recv_sem=recv,
            device_id=device, device_id_type=MESH_ID,
        )
        copy.start()
        return copy

    waits = []
    for k in range(1, peers):
        waits.append(remote(weights_ref, dp_out.at[r], dp_send.at[0, k], dp_recv.at[0, k],
                            {"dp": lax.rem(r + 2 * k, n_d)}))
    waits.append(remote(weights_ref, dp_out.at[r], dp_send.at[0, 0], dp_recv.at[0, 0],
                        {"dp": pair}))
    crossed = remote(pieces_ref, tens_out.at[t], cross_sem.at[0], cross_sem.at[1],
                     {"tensor": cross})
    own_t = pltpu.make_async_copy(pieces_ref, tens_out.at[t], local_sem.at[0])
    own_t.start()
    own_d = pltpu.make_async_copy(weights_ref, dp_out.at[r], local_sem.at[1])
    own_d.start()
    crossed.wait()
    steps = (ring // 2, ring - 1 - ring // 2)
    moving = [None, None]
    for s in range(max(steps)):
        for d, (target, sign) in enumerate(((right, -1), (left, 1))):
            if s >= steps[d]:
                continue
            if s > 0:
                for copy in moving[d]:
                    copy.wait_recv()
            origin = lax.rem(z + sign * s + ring, ring)
            sent = []
            for h, start in enumerate((base, other)):
                slot = start + origin
                src = pieces_ref if (s == 0 and h == 0) else tens_out.at[slot]
                step = src.shape[0] // chunks
                for c in range(chunks):
                    part = pl.ds(c * step, step)
                    sent.append(remote(src.at[part], tens_out.at[slot].at[part],
                                       ring_send.at[d, s, h * chunks + c],
                                       ring_recv.at[d, s, h * chunks + c], {"tensor": target}))
            waits.extend(sent)
            moving[d] = sent
    for d in range(2):
        for copy in moving[d]:
            copy.wait_recv()
    for k in range(1, peers):
        slot = lax.rem(r + n_d - 2 * k, n_d)
        arrival = pltpu.make_async_copy(dp_out.at[slot], dp_out.at[slot], dp_recv.at[0, k])
        arrival.wait()
        waits.append(remote(dp_out.at[slot], dp_out.at[slot], dp_send.at[1, k],
                            dp_recv.at[1, k], {"dp": pair}))
    for copy in waits:
        copy.wait_send()
    pltpu.make_async_copy(dp_out.at[r], dp_out.at[r], dp_recv.at[0, 0]).wait()
    for k in range(1, peers):
        slot = lax.rem(pair + n_d - 2 * k, n_d)
        pltpu.make_async_copy(dp_out.at[slot], dp_out.at[slot], dp_recv.at[1, k]).wait()
    own_t.wait()
    own_d.wait()


def gather_start(pieces, weights, ring, chunks=1):
    n_t = lax.axis_size("tensor")
    n_d = lax.axis_size("dp")
    moved = 2 * (n_t * pieces.size * pieces.dtype.itemsize + n_d * weights.size * weights.dtype.itemsize)
    return pl.pallas_call(
        functools.partial(_gather_start_body, ring, chunks),
        out_shape=[
            jax.ShapeDtypeStruct((n_t,) + pieces.shape, pieces.dtype),
            jax.ShapeDtypeStruct((n_d,) + weights.shape, weights.dtype),
        ],
        in_specs=[pl.BlockSpec(memory_space=pl.ANY)] * 2,
        out_specs=[pl.BlockSpec(memory_space=pl.ANY)] * 2,
        scratch_shapes=[
            pltpu.SemaphoreType.DMA((2, ring // 2, 2 * chunks)),
            pltpu.SemaphoreType.DMA((2, ring // 2, 2 * chunks)),
            pltpu.SemaphoreType.DMA((2,)),
            pltpu.SemaphoreType.DMA((2, n_d // 2)),
            pltpu.SemaphoreType.DMA((2, n_d // 2)),
            pltpu.SemaphoreType.DMA((2,)),
        ],
        compiler_params=pltpu.CompilerParams(collective_id=0, has_side_effects=True),
        cost_estimate=pl.CostEstimate(flops=0, transcendentals=0, bytes_accessed=moved),
    )(pieces, weights)


def local(tokens, norm_gain, query_weight, kv_weight, out_weight, grad_out, doc_lengths):
    tensor_size = lax.axis_size("tensor")
    data_size = lax.axis_size("dp")
    sharers = tensor_size // KVH
    contract_last = (((1,), (1,)), ((), ()))
    query_width = query_weight.shape[1]
    kv_width = kv_weight.shape[1]
    values32 = tokens.astype(jnp.float32)
    root_mean = jnp.sqrt(jnp.mean(values32 * values32, axis=-1) + epsilon)
    unit = values32 / root_mean[:, None]
    gain32 = norm_gain.astype(jnp.float32)
    normed_local = (unit * gain32).astype(jnp.bfloat16)
    rows = tokens.shape[0]
    pieces = jnp.stack([normed_local, grad_out])
    weights_local = jnp.concatenate([query_weight, kv_weight], axis=1)
    out_full_t = lax.all_gather(out_weight.T, "dp", axis=0, tiled=True)
    tens_parts, weight_parts = gather_start(pieces, weights_local, RING)
    normed = tens_parts[:, 0].reshape(tensor_size * rows, -1)
    grad_full = tens_parts[:, 1].reshape(tensor_size * rows, -1)
    seq_length = normed.shape[0]
    weights_full = weight_parts.reshape(-1, weights_local.shape[1])
    query_full = weights_full[:, :query_width]
    kv_local = weights_full[:, query_width : query_width + kv_width]
    queries = jnp.dot(normed, query_full, preferred_element_type=jnp.float32).astype(jnp.bfloat16)
    keyvals = jnp.dot(normed, kv_local, preferred_element_type=jnp.float32).astype(jnp.bfloat16)
    (shared,) = push_exchange([("tensor", sharers, keyvals, False)], 2)
    keyvals = jnp.moveaxis(shared, 0, 1).reshape(seq_length, sharers * kv_width)
    key_rows = keyvals[:, :HD]
    value_rows = keyvals[:, HD:]
    out_grad = jnp.dot(grad_full, out_full_t, preferred_element_type=jnp.float32).astype(
        jnp.bfloat16
    )
    local_heads = queries.shape[1] // HD
    query_heads = queries.reshape(seq_length, local_heads, HD)
    out_heads = out_grad.reshape(seq_length, local_heads, HD)
    allowed = document_mask(doc_lengths[0], seq_length)
    scores = jnp.einsum(
        "qhd,td->hqt", query_heads, key_rows, preferred_element_type=jnp.float32
    ) / math.sqrt(HD)
    scores = jnp.where(allowed[None, :, :], scores, -1e30)
    peak = jnp.max(scores, axis=-1, keepdims=True)
    expo = jnp.exp(scores - peak)
    probs = expo / jnp.sum(expo, axis=-1, keepdims=True)
    probs_low = probs.astype(jnp.bfloat16)
    prob_grad = jnp.einsum("qhd,td->hqt", out_heads, value_rows, preferred_element_type=jnp.float32)
    inner = jnp.sum(probs * prob_grad, axis=-1, keepdims=True)
    score_grad = (probs * (prob_grad - inner) / math.sqrt(HD)).astype(jnp.bfloat16)
    query_grad = jnp.einsum("hqt,td->qhd", score_grad, key_rows, preferred_element_type=jnp.float32)
    query_grad = query_grad.astype(jnp.bfloat16).reshape(seq_length, local_heads * HD)
    key_part = jnp.einsum(
        "hqt,qhd->td", score_grad, query_heads, preferred_element_type=jnp.float32
    )
    value_part = jnp.einsum("hqt,qhd->td", probs_low, out_heads, preferred_element_type=jnp.float32)
    kv_partial = jnp.concatenate([key_part, value_part], axis=1)
    blocks = jnp.moveaxis(kv_partial.reshape(seq_length, sharers, kv_width), 1, 0)
    (kv_arrived,) = push_exchange([("tensor", sharers, blocks.astype(jnp.bfloat16), True)], 3)
    kv_grad = jnp.sum(kv_arrived.astype(jnp.float32), axis=0).astype(jnp.bfloat16)
    from_query = lax.dot_general(
        query_grad, query_full, contract_last, preferred_element_type=jnp.float32
    )
    from_kv = lax.dot_general(kv_grad, kv_local, contract_last, preferred_element_type=jnp.float32)
    partial = (from_query + from_kv).astype(jnp.bfloat16).reshape(tensor_size, rows, -1)
    combined = jnp.concatenate([query_grad, kv_grad], axis=1)
    weight_partial = lax.dot_general(
        normed, combined, (((0,), (0,)), ((), ())), preferred_element_type=jnp.float32
    ).astype(jnp.bfloat16)
    weight_partial = weight_partial.reshape(data_size, -1, weight_partial.shape[1])
    arrived, weight_arrived = push_exchange(
        [("tensor", tensor_size, partial, True), ("dp", data_size, weight_partial, True)], 1
    )
    normed_grad = jnp.sum(arrived.astype(jnp.float32), axis=0)
    scaled = normed_grad * gain32
    correction = unit * jnp.mean(scaled * unit, axis=-1, keepdims=True)
    input_grad = (grad_out.astype(jnp.float32) + (scaled - correction) / root_mean[:, None]).astype(
        jnp.bfloat16
    )
    weight_grads = jnp.sum(weight_arrived.astype(jnp.float32), axis=0) / data_size
    return (input_grad, weight_grads[:, :query_width], weight_grads[:, query_width:])


def solution(mesh):
    placed = (
        P(("dp", "tensor"), None),
        P(),
        P("dp", "tensor"),
        P("dp", "tensor"),
        P("tensor", "dp"),
        P(("dp", "tensor"), None),
        P("dp", None),
    )
    return jax.shard_map(
        local,
        mesh=mesh,
        in_specs=placed,
        out_specs=(P(("dp", "tensor"), None), P("dp", "tensor"), P("dp", "tensor")),
        check_vma=False,
    )
```

```python
import functools
import math

import jax
import jax.numpy as jnp
from jax import lax
from jax.experimental import pallas as pl
from jax.experimental.pallas import tpu as pltpu
from jax.sharding import PartitionSpec as P

KVH = 4
HD = 128
MESH_ID = pl.DeviceIdType.MESH
RING = 8


epsilon = 1e-05


def partner_2(value, axis, bit):
    mask = 2**bit
    pairs = [(source, source ^ mask) for source in range(lax.axis_size(axis))]
    return lax.ppermute(value, axis, pairs)


def document_mask(lengths, length_total):
    ends = jnp.cumsum(lengths)
    positions = jnp.arange(length_total, dtype=jnp.int32)
    labels = jnp.sum((ends[None, :] <= positions[:, None]).astype(jnp.int32), axis=1)
    return (labels[:, None] == labels[None, :]) & (positions[None, :] <= positions[:, None])


def _push_body(plan, *refs):
    count = len(plan)
    ins = refs[:count]
    outs = refs[count : 2 * count]
    send_sems = refs[2 * count : 3 * count]
    recv_sems = refs[3 * count : 4 * count]
    local_sem = refs[4 * count]
    barrier = pltpu.get_barrier_semaphore()
    mine = []
    expected = 0
    places = []
    for axis, n, _, stride in plan:
        index = lax.axis_index(axis)
        me = lax.rem(index // stride, n)
        offset = index - me * stride
        mine.append(me)
        places.append(functools.partial(lambda o, st, p: o + p * st, offset, stride))
        for j in range(1, n):
            pl.semaphore_signal(
                barrier,
                inc=1,
                device_id={axis: places[-1](lax.rem(me + j, n))},
                device_id_type=MESH_ID,
            )
        expected += n - 1
    pl.semaphore_wait(barrier, expected)
    local = []
    for g, (axis, n, scatter, _) in enumerate(plan):
        me = mine[g]
        src = ins[g].at[me] if scatter else ins[g]
        copy = pltpu.make_async_copy(src, outs[g].at[me], local_sem.at[g])
        copy.start()
        local.append(copy)
    remote = []
    for j in range(1, max(n for _, n, _, _ in plan)):
        for g, (axis, n, scatter, _) in enumerate(plan):
            if j >= n:
                continue
            me = mine[g]
            peer = lax.rem(me + j, n)
            copy = pltpu.make_async_remote_copy(
                src_ref=ins[g].at[peer] if scatter else ins[g],
                dst_ref=outs[g].at[me],
                send_sem=send_sems[g].at[j],
                recv_sem=recv_sems[g].at[j],
                device_id={axis: places[g](peer)},
                device_id_type=MESH_ID,
            )
            copy.start()
            remote.append(copy)
    for copy in remote:
        copy.wait()
    for copy in local:
        copy.wait()


def push_exchange(groups, cid):
    groups = [g if len(g) == 5 else g + (1,) for g in groups]
    plan = tuple((axis, n, scatter, stride) for axis, n, _, scatter, stride in groups)
    arrays = [array for _, _, array, _, _ in groups]
    out_shape = []
    moved = 0
    for _, n, array, scatter, _ in groups:
        shape = array.shape if scatter else (n,) + array.shape
        out_shape.append(jax.ShapeDtypeStruct(shape, array.dtype))
        moved += 2 * math.prod(shape) * array.dtype.itemsize
    count = len(groups)
    return pl.pallas_call(
        functools.partial(_push_body, plan),
        out_shape=out_shape,
        in_specs=[pl.BlockSpec(memory_space=pl.ANY)] * count,
        out_specs=[pl.BlockSpec(memory_space=pl.ANY)] * count,
        scratch_shapes=[pltpu.SemaphoreType.DMA((n,)) for _, n, _, _, _ in groups]
        + [pltpu.SemaphoreType.DMA((n,)) for _, n, _, _, _ in groups]
        + [pltpu.SemaphoreType.DMA((count,))],
        compiler_params=pltpu.CompilerParams(collective_id=cid, has_side_effects=True),
        cost_estimate=pl.CostEstimate(flops=0, transcendentals=0, bytes_accessed=moved),
    )(*arrays)


def _gather_start_body(ring, pieces_ref, weights_ref, tens_out, dp_out, ring_send, ring_recv,
                       cross_sem, dp_send, dp_recv, local_sem):
    n_t = lax.axis_size("tensor")
    n_d = lax.axis_size("dp")
    t = lax.axis_index("tensor")
    r = lax.axis_index("dp")
    z = lax.rem(t, ring)
    base = t - z
    other = lax.rem(t + ring, n_t) - z
    cross = lax.rem(t + ring, n_t)
    right = base + lax.rem(z + 1, ring)
    left = base + lax.rem(z + ring - 1, ring)
    pair = r + 1 - 2 * lax.rem(r, 2)
    peers = n_d // 2
    barrier = pltpu.get_barrier_semaphore()
    for device in ({"tensor": cross}, {"tensor": right}, {"tensor": left}, {"dp": pair}):
        pl.semaphore_signal(barrier, inc=1, device_id=device, device_id_type=MESH_ID)
    for k in range(1, peers):
        pl.semaphore_signal(
            barrier, inc=1, device_id={"dp": lax.rem(r + 2 * k, n_d)}, device_id_type=MESH_ID
        )
    pl.semaphore_wait(barrier, 4 + peers - 1)

    def remote(src, dst, send, recv, device):
        copy = pltpu.make_async_remote_copy(
            src_ref=src, dst_ref=dst, send_sem=send, recv_sem=recv,
            device_id=device, device_id_type=MESH_ID,
        )
        copy.start()
        return copy

    waits = []
    for k in range(1, peers):
        waits.append(remote(weights_ref, dp_out.at[r], dp_send.at[0, k], dp_recv.at[0, k],
                            {"dp": lax.rem(r + 2 * k, n_d)}))
    waits.append(remote(weights_ref, dp_out.at[r], dp_send.at[0, 0], dp_recv.at[0, 0],
                        {"dp": pair}))
    crossed = remote(pieces_ref, tens_out.at[t], cross_sem.at[0], cross_sem.at[1],
                     {"tensor": cross})
    own_t = pltpu.make_async_copy(pieces_ref, tens_out.at[t], local_sem.at[0])
    own_t.start()
    own_d = pltpu.make_async_copy(weights_ref, dp_out.at[r], local_sem.at[1])
    own_d.start()
    crossed.wait()
    steps = (ring // 2, ring - 1 - ring // 2)
    moving = [None, None]
    for s in range(max(steps)):
        for d, (target, sign) in enumerate(((right, -1), (left, 1))):
            if s >= steps[d]:
                continue
            if s > 0:
                for copy in moving[d]:
                    copy.wait_recv()
            origin = lax.rem(z + sign * s + ring, ring)
            sent = []
            for h, start in enumerate((base, other)):
                slot = start + origin
                src = pieces_ref if (s == 0 and h == 0) else tens_out.at[slot]
                sent.append(remote(src, tens_out.at[slot], ring_send.at[d, s, h],
                                   ring_recv.at[d, s, h], {"tensor": target}))
            waits.extend(sent)
            moving[d] = sent
    for d in range(2):
        for copy in moving[d]:
            copy.wait_recv()
    for k in range(1, peers):
        slot = lax.rem(r + n_d - 2 * k, n_d)
        arrival = pltpu.make_async_copy(dp_out.at[slot], dp_out.at[slot], dp_recv.at[0, k])
        arrival.wait()
        waits.append(remote(dp_out.at[slot], dp_out.at[slot], dp_send.at[1, k],
                            dp_recv.at[1, k], {"dp": pair}))
    for copy in waits:
        copy.wait_send()
    pltpu.make_async_copy(dp_out.at[r], dp_out.at[r], dp_recv.at[0, 0]).wait()
    for k in range(1, peers):
        slot = lax.rem(pair + n_d - 2 * k, n_d)
        pltpu.make_async_copy(dp_out.at[slot], dp_out.at[slot], dp_recv.at[1, k]).wait()
    own_t.wait()
    own_d.wait()


def gather_start(pieces, weights, ring):
    n_t = lax.axis_size("tensor")
    n_d = lax.axis_size("dp")
    moved = 2 * (n_t * pieces.size * pieces.dtype.itemsize + n_d * weights.size * weights.dtype.itemsize)
    return pl.pallas_call(
        functools.partial(_gather_start_body, ring),
        out_shape=[
            jax.ShapeDtypeStruct((n_t,) + pieces.shape, pieces.dtype),
            jax.ShapeDtypeStruct((n_d,) + weights.shape, weights.dtype),
        ],
        in_specs=[pl.BlockSpec(memory_space=pl.ANY)] * 2,
        out_specs=[pl.BlockSpec(memory_space=pl.ANY)] * 2,
        scratch_shapes=[
            pltpu.SemaphoreType.DMA((2, ring // 2, 2)),
            pltpu.SemaphoreType.DMA((2, ring // 2, 2)),
            pltpu.SemaphoreType.DMA((2,)),
            pltpu.SemaphoreType.DMA((2, n_d // 2)),
            pltpu.SemaphoreType.DMA((2, n_d // 2)),
            pltpu.SemaphoreType.DMA((2,)),
        ],
        compiler_params=pltpu.CompilerParams(collective_id=0, has_side_effects=True),
        cost_estimate=pl.CostEstimate(flops=0, transcendentals=0, bytes_accessed=moved),
    )(pieces, weights)


def local(tokens, norm_gain, query_weight, kv_weight, out_weight, grad_out, doc_lengths):
    tensor_size = lax.axis_size("tensor")
    data_size = lax.axis_size("dp")
    tensor_index = lax.axis_index("tensor")
    sharers = tensor_size // KVH
    levels = sharers.bit_length() - 1
    contract_last = (((1,), (1,)), ((), ()))
    query_width = query_weight.shape[1]
    kv_width = kv_weight.shape[1]
    values32 = tokens.astype(jnp.float32)
    root_mean = jnp.sqrt(jnp.mean(values32 * values32, axis=-1) + epsilon)
    unit = values32 / root_mean[:, None]
    gain32 = norm_gain.astype(jnp.float32)
    normed_local = (unit * gain32).astype(jnp.bfloat16)
    rows = tokens.shape[0]
    pieces = jnp.stack([normed_local, grad_out])
    weights_local = jnp.concatenate([query_weight, kv_weight, out_weight.T], axis=1)
    tens_parts, weight_parts = gather_start(pieces, weights_local, RING)
    normed = tens_parts[:, 0].reshape(tensor_size * rows, -1)
    grad_full = tens_parts[:, 1].reshape(tensor_size * rows, -1)
    seq_length = normed.shape[0]
    weights_full = weight_parts.reshape(-1, weights_local.shape[1])
    query_full = weights_full[:, :query_width]
    kv_local = weights_full[:, query_width : query_width + kv_width]
    out_full_t = weights_full[:, query_width + kv_width :]
    queries = jnp.dot(normed, query_full, preferred_element_type=jnp.float32).astype(jnp.bfloat16)
    keyvals = jnp.dot(normed, kv_local, preferred_element_type=jnp.float32).astype(jnp.bfloat16)
    for bit_index in range(levels):
        partner = partner_2(keyvals, "tensor", bit_index)
        joined_upper_half = tensor_index >> bit_index & 1 == 1
        keyvals = jnp.concatenate(
            [
                jnp.where(joined_upper_half, partner, keyvals),
                jnp.where(joined_upper_half, keyvals, partner),
            ],
            axis=1,
        )
    key_rows = keyvals[:, :HD]
    value_rows = keyvals[:, HD:]
    out_grad = jnp.dot(grad_full, out_full_t, preferred_element_type=jnp.float32).astype(
        jnp.bfloat16
    )
    local_heads = queries.shape[1] // HD
    query_heads = queries.reshape(seq_length, local_heads, HD)
    out_heads = out_grad.reshape(seq_length, local_heads, HD)
    allowed = document_mask(doc_lengths[0], seq_length)
    scores = jnp.einsum(
        "qhd,td->hqt", query_heads, key_rows, preferred_element_type=jnp.float32
    ) / math.sqrt(HD)
    scores = jnp.where(allowed[None, :, :], scores, -1e30)
    peak = jnp.max(scores, axis=-1, keepdims=True)
    expo = jnp.exp(scores - peak)
    probs = expo / jnp.sum(expo, axis=-1, keepdims=True)
    probs_low = probs.astype(jnp.bfloat16)
    prob_grad = jnp.einsum("qhd,td->hqt", out_heads, value_rows, preferred_element_type=jnp.float32)
    inner = jnp.sum(probs * prob_grad, axis=-1, keepdims=True)
    score_grad = (probs * (prob_grad - inner) / math.sqrt(HD)).astype(jnp.bfloat16)
    query_grad = jnp.einsum("hqt,td->qhd", score_grad, key_rows, preferred_element_type=jnp.float32)
    query_grad = query_grad.astype(jnp.bfloat16).reshape(seq_length, local_heads * HD)
    key_part = jnp.einsum(
        "hqt,qhd->td", score_grad, query_heads, preferred_element_type=jnp.float32
    )
    value_part = jnp.einsum("hqt,qhd->td", probs_low, out_heads, preferred_element_type=jnp.float32)
    kv_partial = jnp.concatenate([key_part, value_part], axis=1)
    for bit_index in reversed(range(levels)):
        half_cols = kv_partial.shape[1] // 2
        upper_half = tensor_index >> bit_index & 1 == 1
        lower_cols = kv_partial[:, :half_cols]
        higher_cols = kv_partial[:, half_cols:]
        kept = jnp.where(upper_half, higher_cols, lower_cols)
        handed = jnp.where(upper_half, lower_cols, higher_cols)
        kv_partial = kept + partner_2(handed.astype(jnp.bfloat16), "tensor", bit_index).astype(
            handed.dtype
        )
    kv_grad = kv_partial.astype(jnp.bfloat16)
    from_query = lax.dot_general(
        query_grad, query_full, contract_last, preferred_element_type=jnp.float32
    )
    from_kv = lax.dot_general(kv_grad, kv_local, contract_last, preferred_element_type=jnp.float32)
    partial = (from_query + from_kv).astype(jnp.bfloat16).reshape(tensor_size, rows, -1)
    combined = jnp.concatenate([query_grad, kv_grad], axis=1)
    weight_partial = lax.dot_general(
        normed, combined, (((0,), (0,)), ((), ())), preferred_element_type=jnp.float32
    ).astype(jnp.bfloat16)
    weight_partial = weight_partial.reshape(data_size // 2, 2, -1, weight_partial.shape[1])
    parity = lax.rem(lax.axis_index("dp"), 2)
    kept = jnp.where(parity == 0, weight_partial[:, 0], weight_partial[:, 1])
    handed = jnp.where(parity == 0, weight_partial[:, 1], weight_partial[:, 0])
    swapped = lax.ppermute(handed, "dp", [(i, i ^ 1) for i in range(data_size)])
    paired = (kept.astype(jnp.float32) + swapped.astype(jnp.float32)).astype(jnp.bfloat16)
    arrived, weight_arrived = push_exchange(
        [
            ("tensor", tensor_size, partial, True),
            ("dp", data_size // 2, paired, True, 2),
        ],
        1,
    )
    normed_grad = jnp.sum(arrived.astype(jnp.float32), axis=0)
    scaled = normed_grad * gain32
    correction = unit * jnp.mean(scaled * unit, axis=-1, keepdims=True)
    input_grad = (grad_out.astype(jnp.float32) + (scaled - correction) / root_mean[:, None]).astype(
        jnp.bfloat16
    )
    weight_grads = jnp.sum(weight_arrived.astype(jnp.float32), axis=0) / data_size
    return (input_grad, weight_grads[:, :query_width], weight_grads[:, query_width:])


def solution(mesh):
    placed = (
        P(("dp", "tensor"), None),
        P(),
        P("dp", "tensor"),
        P("dp", "tensor"),
        P("tensor", "dp"),
        P(("dp", "tensor"), None),
        P("dp", None),
    )
    return jax.shard_map(
        local,
        mesh=mesh,
        in_specs=placed,
        out_specs=(P(("dp", "tensor"), None), P("dp", "tensor"), P("dp", "tensor")),
        check_vma=False,
    )
```

```python
import functools
import math

import jax
import jax.numpy as jnp
from jax import lax
from jax.experimental import pallas as pl
from jax.experimental.pallas import tpu as pltpu
from jax.sharding import PartitionSpec as P

KVH = 4
HD = 128
MESH_ID = pl.DeviceIdType.MESH
RING = 8


epsilon = 1e-05


def partner_2(value, axis, bit):
    mask = 2**bit
    pairs = [(source, source ^ mask) for source in range(lax.axis_size(axis))]
    return lax.ppermute(value, axis, pairs)


def document_mask(lengths, length_total):
    ends = jnp.cumsum(lengths)
    positions = jnp.arange(length_total, dtype=jnp.int32)
    labels = jnp.sum((ends[None, :] <= positions[:, None]).astype(jnp.int32), axis=1)
    return (labels[:, None] == labels[None, :]) & (positions[None, :] <= positions[:, None])


def _push_body(plan, *refs):
    count = len(plan)
    ins = refs[:count]
    outs = refs[count : 2 * count]
    send_sems = refs[2 * count : 3 * count]
    recv_sems = refs[3 * count : 4 * count]
    local_sem = refs[4 * count]
    barrier = pltpu.get_barrier_semaphore()
    mine = []
    expected = 0
    places = []
    for axis, n, _, stride in plan:
        index = lax.axis_index(axis)
        me = lax.rem(index // stride, n)
        offset = index - me * stride
        mine.append(me)
        places.append(functools.partial(lambda o, st, p: o + p * st, offset, stride))
        for j in range(1, n):
            pl.semaphore_signal(
                barrier,
                inc=1,
                device_id={axis: places[-1](lax.rem(me + j, n))},
                device_id_type=MESH_ID,
            )
        expected += n - 1
    pl.semaphore_wait(barrier, expected)
    local = []
    for g, (axis, n, scatter, _) in enumerate(plan):
        me = mine[g]
        src = ins[g].at[me] if scatter else ins[g]
        copy = pltpu.make_async_copy(src, outs[g].at[me], local_sem.at[g])
        copy.start()
        local.append(copy)
    remote = []
    for j in range(1, max(n for _, n, _, _ in plan)):
        for g, (axis, n, scatter, _) in enumerate(plan):
            if j >= n:
                continue
            me = mine[g]
            peer = lax.rem(me + j, n)
            copy = pltpu.make_async_remote_copy(
                src_ref=ins[g].at[peer] if scatter else ins[g],
                dst_ref=outs[g].at[me],
                send_sem=send_sems[g].at[j],
                recv_sem=recv_sems[g].at[j],
                device_id={axis: places[g](peer)},
                device_id_type=MESH_ID,
            )
            copy.start()
            remote.append(copy)
    for copy in remote:
        copy.wait()
    for copy in local:
        copy.wait()


def push_exchange(groups, cid):
    groups = [g if len(g) == 5 else g + (1,) for g in groups]
    plan = tuple((axis, n, scatter, stride) for axis, n, _, scatter, stride in groups)
    arrays = [array for _, _, array, _, _ in groups]
    out_shape = []
    moved = 0
    for _, n, array, scatter, _ in groups:
        shape = array.shape if scatter else (n,) + array.shape
        out_shape.append(jax.ShapeDtypeStruct(shape, array.dtype))
        moved += 2 * math.prod(shape) * array.dtype.itemsize
    count = len(groups)
    return pl.pallas_call(
        functools.partial(_push_body, plan),
        out_shape=out_shape,
        in_specs=[pl.BlockSpec(memory_space=pl.ANY)] * count,
        out_specs=[pl.BlockSpec(memory_space=pl.ANY)] * count,
        scratch_shapes=[pltpu.SemaphoreType.DMA((n,)) for _, n, _, _, _ in groups]
        + [pltpu.SemaphoreType.DMA((n,)) for _, n, _, _, _ in groups]
        + [pltpu.SemaphoreType.DMA((count,))],
        compiler_params=pltpu.CompilerParams(collective_id=cid, has_side_effects=True),
        cost_estimate=pl.CostEstimate(flops=0, transcendentals=0, bytes_accessed=moved),
    )(*arrays)


def _gather_start_body(ring, pieces_ref, weights_ref, tens_out, dp_out, ring_send, ring_recv,
                       cross_sem, dp_send, dp_recv, local_sem):
    n_t = lax.axis_size("tensor")
    n_d = lax.axis_size("dp")
    t = lax.axis_index("tensor")
    r = lax.axis_index("dp")
    z = lax.rem(t, ring)
    base = t - z
    other = lax.rem(t + ring, n_t) - z
    cross = lax.rem(t + ring, n_t)
    right = base + lax.rem(z + 1, ring)
    left = base + lax.rem(z + ring - 1, ring)
    pair = r + 1 - 2 * lax.rem(r, 2)
    peers = n_d // 2
    barrier = pltpu.get_barrier_semaphore()
    for device in ({"tensor": cross}, {"tensor": right}, {"tensor": left}, {"dp": pair}):
        pl.semaphore_signal(barrier, inc=1, device_id=device, device_id_type=MESH_ID)
    for k in range(1, peers):
        pl.semaphore_signal(
            barrier, inc=1, device_id={"dp": lax.rem(r + 2 * k, n_d)}, device_id_type=MESH_ID
        )
    pl.semaphore_wait(barrier, 4 + peers - 1)

    def remote(src, dst, send, recv, device):
        copy = pltpu.make_async_remote_copy(
            src_ref=src, dst_ref=dst, send_sem=send, recv_sem=recv,
            device_id=device, device_id_type=MESH_ID,
        )
        copy.start()
        return copy

    waits = []
    for k in range(1, peers):
        waits.append(remote(weights_ref, dp_out.at[r], dp_send.at[0, k], dp_recv.at[0, k],
                            {"dp": lax.rem(r + 2 * k, n_d)}))
    waits.append(remote(weights_ref, dp_out.at[r], dp_send.at[0, 0], dp_recv.at[0, 0],
                        {"dp": pair}))
    crossed = remote(pieces_ref, tens_out.at[t], cross_sem.at[0], cross_sem.at[1],
                     {"tensor": cross})
    own_t = pltpu.make_async_copy(pieces_ref, tens_out.at[t], local_sem.at[0])
    own_t.start()
    own_d = pltpu.make_async_copy(weights_ref, dp_out.at[r], local_sem.at[1])
    own_d.start()
    crossed.wait()
    steps = (ring // 2, ring - 1 - ring // 2)
    moving = [None, None]
    for s in range(max(steps)):
        for d, (target, sign) in enumerate(((right, -1), (left, 1))):
            if s >= steps[d]:
                continue
            if s > 0:
                for copy in moving[d]:
                    copy.wait_recv()
            origin = lax.rem(z + sign * s + ring, ring)
            sent = []
            for h, start in enumerate((base, other)):
                slot = start + origin
                src = pieces_ref if (s == 0 and h == 0) else tens_out.at[slot]
                sent.append(remote(src, tens_out.at[slot], ring_send.at[d, s, h],
                                   ring_recv.at[d, s, h], {"tensor": target}))
            waits.extend(sent)
            moving[d] = sent
    for d in range(2):
        for copy in moving[d]:
            copy.wait_recv()
    for k in range(1, peers):
        slot = lax.rem(r + n_d - 2 * k, n_d)
        arrival = pltpu.make_async_copy(dp_out.at[slot], dp_out.at[slot], dp_recv.at[0, k])
        arrival.wait()
        waits.append(remote(dp_out.at[slot], dp_out.at[slot], dp_send.at[1, k],
                            dp_recv.at[1, k], {"dp": pair}))
    for copy in waits:
        copy.wait_send()
    pltpu.make_async_copy(dp_out.at[r], dp_out.at[r], dp_recv.at[0, 0]).wait()
    for k in range(1, peers):
        slot = lax.rem(pair + n_d - 2 * k, n_d)
        pltpu.make_async_copy(dp_out.at[slot], dp_out.at[slot], dp_recv.at[1, k]).wait()
    own_t.wait()
    own_d.wait()


def gather_start(pieces, weights, ring):
    n_t = lax.axis_size("tensor")
    n_d = lax.axis_size("dp")
    moved = 2 * (n_t * pieces.size * pieces.dtype.itemsize + n_d * weights.size * weights.dtype.itemsize)
    return pl.pallas_call(
        functools.partial(_gather_start_body, ring),
        out_shape=[
            jax.ShapeDtypeStruct((n_t,) + pieces.shape, pieces.dtype),
            jax.ShapeDtypeStruct((n_d,) + weights.shape, weights.dtype),
        ],
        in_specs=[pl.BlockSpec(memory_space=pl.ANY)] * 2,
        out_specs=[pl.BlockSpec(memory_space=pl.ANY)] * 2,
        scratch_shapes=[
            pltpu.SemaphoreType.DMA((2, ring // 2, 2)),
            pltpu.SemaphoreType.DMA((2, ring // 2, 2)),
            pltpu.SemaphoreType.DMA((2,)),
            pltpu.SemaphoreType.DMA((2, n_d // 2)),
            pltpu.SemaphoreType.DMA((2, n_d // 2)),
            pltpu.SemaphoreType.DMA((2,)),
        ],
        compiler_params=pltpu.CompilerParams(collective_id=0, has_side_effects=True),
        cost_estimate=pl.CostEstimate(flops=0, transcendentals=0, bytes_accessed=moved),
    )(pieces, weights)


def _pair_body(x_ref, o_ref, mine, theirs, send_sem, recv_sem, local_sem):
    r = lax.axis_index("dp")
    parity = lax.rem(r, 2)
    pair = r + 1 - 2 * parity
    slots, _, width = mine.shape
    barrier = pltpu.get_barrier_semaphore()
    pl.semaphore_signal(barrier, inc=1, device_id={"dp": pair}, device_id_type=MESH_ID)
    pl.semaphore_wait(barrier, 1)
    sent = []
    kept = []
    for i in range(slots):
        give = pl.ds(pl.multiple_of((2 * i + 1 - parity) * width, width), width)
        keep = pl.ds(pl.multiple_of((2 * i + parity) * width, width), width)
        copy = pltpu.make_async_remote_copy(
            src_ref=x_ref.at[:, give], dst_ref=theirs.at[i], send_sem=send_sem.at[i],
            recv_sem=recv_sem.at[i], device_id={"dp": pair}, device_id_type=MESH_ID,
        )
        copy.start()
        sent.append(copy)
        own = pltpu.make_async_copy(x_ref.at[:, keep], mine.at[i], local_sem.at[i])
        own.start()
        kept.append(own)
    for copy in sent:
        copy.wait()
    for copy in kept:
        copy.wait()
    o_ref[...] = (mine[...].astype(jnp.float32) + theirs[...].astype(jnp.float32)).astype(o_ref.dtype)


def pair_sum(x, width):
    rows, cols = x.shape
    slots = cols // width // 2
    shape = (slots, rows, width)
    return pl.pallas_call(
        _pair_body,
        out_shape=jax.ShapeDtypeStruct(shape, x.dtype),
        in_specs=[pl.BlockSpec(memory_space=pl.ANY)],
        out_specs=pl.BlockSpec(memory_space=pltpu.VMEM),
        scratch_shapes=[
            pltpu.VMEM(shape, x.dtype),
            pltpu.VMEM(shape, x.dtype),
            pltpu.SemaphoreType.DMA((slots,)),
            pltpu.SemaphoreType.DMA((slots,)),
            pltpu.SemaphoreType.DMA((slots,)),
        ],
        compiler_params=pltpu.CompilerParams(collective_id=4, has_side_effects=True),
        cost_estimate=pl.CostEstimate(
            flops=x.size // 2, transcendentals=0, bytes_accessed=2 * x.size * x.dtype.itemsize
        ),
    )(x)


def local(tokens, norm_gain, query_weight, kv_weight, out_weight, grad_out, doc_lengths):
    tensor_size = lax.axis_size("tensor")
    data_size = lax.axis_size("dp")
    tensor_index = lax.axis_index("tensor")
    sharers = tensor_size // KVH
    levels = sharers.bit_length() - 1
    contract_last = (((1,), (1,)), ((), ()))
    query_width = query_weight.shape[1]
    kv_width = kv_weight.shape[1]
    values32 = tokens.astype(jnp.float32)
    root_mean = jnp.sqrt(jnp.mean(values32 * values32, axis=-1) + epsilon)
    unit = values32 / root_mean[:, None]
    gain32 = norm_gain.astype(jnp.float32)
    normed_local = (unit * gain32).astype(jnp.bfloat16)
    rows = tokens.shape[0]
    pieces = jnp.stack([normed_local, grad_out])
    weights_local = jnp.concatenate([query_weight, kv_weight, out_weight.T], axis=1)
    tens_parts, weight_parts = gather_start(pieces, weights_local, RING)
    normed = tens_parts[:, 0].reshape(tensor_size * rows, -1)
    grad_full = tens_parts[:, 1].reshape(tensor_size * rows, -1)
    seq_length = normed.shape[0]
    weights_full = weight_parts.reshape(-1, weights_local.shape[1])
    query_full = weights_full[:, :query_width]
    kv_local = weights_full[:, query_width : query_width + kv_width]
    out_full_t = weights_full[:, query_width + kv_width :]
    queries = jnp.dot(normed, query_full, preferred_element_type=jnp.float32).astype(jnp.bfloat16)
    keyvals = jnp.dot(normed, kv_local, preferred_element_type=jnp.float32).astype(jnp.bfloat16)
    for bit_index in range(levels):
        partner = partner_2(keyvals, "tensor", bit_index)
        joined_upper_half = tensor_index >> bit_index & 1 == 1
        keyvals = jnp.concatenate(
            [
                jnp.where(joined_upper_half, partner, keyvals),
                jnp.where(joined_upper_half, keyvals, partner),
            ],
            axis=1,
        )
    key_rows = keyvals[:, :HD]
    value_rows = keyvals[:, HD:]
    out_grad = jnp.dot(grad_full, out_full_t, preferred_element_type=jnp.float32).astype(
        jnp.bfloat16
    )
    local_heads = queries.shape[1] // HD
    query_heads = queries.reshape(seq_length, local_heads, HD)
    out_heads = out_grad.reshape(seq_length, local_heads, HD)
    allowed = document_mask(doc_lengths[0], seq_length)
    scores = jnp.einsum(
        "qhd,td->hqt", query_heads, key_rows, preferred_element_type=jnp.float32
    ) / math.sqrt(HD)
    scores = jnp.where(allowed[None, :, :], scores, -1e30)
    peak = jnp.max(scores, axis=-1, keepdims=True)
    expo = jnp.exp(scores - peak)
    probs = expo / jnp.sum(expo, axis=-1, keepdims=True)
    probs_low = probs.astype(jnp.bfloat16)
    prob_grad = jnp.einsum("qhd,td->hqt", out_heads, value_rows, preferred_element_type=jnp.float32)
    inner = jnp.sum(probs * prob_grad, axis=-1, keepdims=True)
    score_grad = (probs * (prob_grad - inner) / math.sqrt(HD)).astype(jnp.bfloat16)
    query_grad = jnp.einsum("hqt,td->qhd", score_grad, key_rows, preferred_element_type=jnp.float32)
    query_grad = query_grad.astype(jnp.bfloat16).reshape(seq_length, local_heads * HD)
    key_part = jnp.einsum(
        "hqt,qhd->td", score_grad, query_heads, preferred_element_type=jnp.float32
    )
    value_part = jnp.einsum("hqt,qhd->td", probs_low, out_heads, preferred_element_type=jnp.float32)
    kv_partial = jnp.concatenate([key_part, value_part], axis=1)
    for bit_index in reversed(range(levels)):
        half_cols = kv_partial.shape[1] // 2
        upper_half = tensor_index >> bit_index & 1 == 1
        lower_cols = kv_partial[:, :half_cols]
        higher_cols = kv_partial[:, half_cols:]
        kept = jnp.where(upper_half, higher_cols, lower_cols)
        handed = jnp.where(upper_half, lower_cols, higher_cols)
        kv_partial = kept + partner_2(handed.astype(jnp.bfloat16), "tensor", bit_index).astype(
            handed.dtype
        )
    kv_grad = kv_partial.astype(jnp.bfloat16)
    from_query = lax.dot_general(
        query_grad, query_full, contract_last, preferred_element_type=jnp.float32
    )
    from_kv = lax.dot_general(kv_grad, kv_local, contract_last, preferred_element_type=jnp.float32)
    partial = (from_query + from_kv).astype(jnp.bfloat16).reshape(tensor_size, rows, -1)
    combined = jnp.concatenate([query_grad, kv_grad], axis=1)
    weight_partial = lax.dot_general(
        combined, normed, (((0,), (0,)), ((), ())), preferred_element_type=jnp.float32
    ).astype(jnp.bfloat16)
    block = weight_partial.shape[1] // data_size
    paired = pair_sum(weight_partial, block)
    arrived, weight_arrived = push_exchange(
        [
            ("tensor", tensor_size, partial, True),
            ("dp", data_size // 2, paired, True, 2),
        ],
        1,
    )
    normed_grad = jnp.sum(arrived.astype(jnp.float32), axis=0)
    scaled = normed_grad * gain32
    correction = unit * jnp.mean(scaled * unit, axis=-1, keepdims=True)
    input_grad = (grad_out.astype(jnp.float32) + (scaled - correction) / root_mean[:, None]).astype(
        jnp.bfloat16
    )
    weight_grads = (jnp.sum(weight_arrived.astype(jnp.float32), axis=0) / data_size).T
    return (input_grad, weight_grads[:, :query_width], weight_grads[:, query_width:])


def solution(mesh):
    placed = (
        P(("dp", "tensor"), None),
        P(),
        P("dp", "tensor"),
        P("dp", "tensor"),
        P("tensor", "dp"),
        P(("dp", "tensor"), None),
        P("dp", None),
    )
    return jax.shard_map(
        local,
        mesh=mesh,
        in_specs=placed,
        out_specs=(P(("dp", "tensor"), None), P("dp", "tensor"), P("dp", "tensor")),
        check_vma=False,
    )
```

```python
import functools
import math

import jax
import jax.numpy as jnp
from jax import lax
from jax.experimental import pallas as pl
from jax.experimental.pallas import tpu as pltpu
from jax.sharding import PartitionSpec as P

KVH = 4
HD = 128
MESH_ID = pl.DeviceIdType.MESH
RING = 8


epsilon = 1e-05


def partner_2(value, axis, bit):
    mask = 2**bit
    pairs = [(source, source ^ mask) for source in range(lax.axis_size(axis))]
    return lax.ppermute(value, axis, pairs)


def document_mask(lengths, length_total):
    ends = jnp.cumsum(lengths)
    positions = jnp.arange(length_total, dtype=jnp.int32)
    labels = jnp.sum((ends[None, :] <= positions[:, None]).astype(jnp.int32), axis=1)
    return (labels[:, None] == labels[None, :]) & (positions[None, :] <= positions[:, None])


def _push_body(plan, *refs):
    count = len(plan)
    ins = refs[:count]
    outs = refs[count : 2 * count]
    send_sems = refs[2 * count : 3 * count]
    recv_sems = refs[3 * count : 4 * count]
    local_sem = refs[4 * count]
    barrier = pltpu.get_barrier_semaphore()
    mine = []
    expected = 0
    places = []
    for axis, n, _, stride in plan:
        index = lax.axis_index(axis)
        me = lax.rem(index // stride, n)
        offset = index - me * stride
        mine.append(me)
        places.append(functools.partial(lambda o, st, p: o + p * st, offset, stride))
        for j in range(1, n):
            pl.semaphore_signal(
                barrier,
                inc=1,
                device_id={axis: places[-1](lax.rem(me + j, n))},
                device_id_type=MESH_ID,
            )
        expected += n - 1
    pl.semaphore_wait(barrier, expected)
    local = []
    for g, (axis, n, scatter, _) in enumerate(plan):
        me = mine[g]
        src = ins[g].at[me] if scatter else ins[g]
        copy = pltpu.make_async_copy(src, outs[g].at[me], local_sem.at[g])
        copy.start()
        local.append(copy)
    remote = []
    for j in range(1, max(n for _, n, _, _ in plan)):
        for g, (axis, n, scatter, _) in enumerate(plan):
            if j >= n:
                continue
            me = mine[g]
            peer = lax.rem(me + j, n)
            copy = pltpu.make_async_remote_copy(
                src_ref=ins[g].at[peer] if scatter else ins[g],
                dst_ref=outs[g].at[me],
                send_sem=send_sems[g].at[j],
                recv_sem=recv_sems[g].at[j],
                device_id={axis: places[g](peer)},
                device_id_type=MESH_ID,
            )
            copy.start()
            remote.append(copy)
    for copy in remote:
        copy.wait()
    for copy in local:
        copy.wait()


def push_exchange(groups, cid):
    groups = [g if len(g) == 5 else g + (1,) for g in groups]
    plan = tuple((axis, n, scatter, stride) for axis, n, _, scatter, stride in groups)
    arrays = [array for _, _, array, _, _ in groups]
    out_shape = []
    moved = 0
    for _, n, array, scatter, _ in groups:
        shape = array.shape if scatter else (n,) + array.shape
        out_shape.append(jax.ShapeDtypeStruct(shape, array.dtype))
        moved += 2 * math.prod(shape) * array.dtype.itemsize
    count = len(groups)
    return pl.pallas_call(
        functools.partial(_push_body, plan),
        out_shape=out_shape,
        in_specs=[pl.BlockSpec(memory_space=pl.ANY)] * count,
        out_specs=[pl.BlockSpec(memory_space=pl.ANY)] * count,
        scratch_shapes=[pltpu.SemaphoreType.DMA((n,)) for _, n, _, _, _ in groups]
        + [pltpu.SemaphoreType.DMA((n,)) for _, n, _, _, _ in groups]
        + [pltpu.SemaphoreType.DMA((count,))],
        compiler_params=pltpu.CompilerParams(collective_id=cid, has_side_effects=True),
        cost_estimate=pl.CostEstimate(flops=0, transcendentals=0, bytes_accessed=moved),
    )(*arrays)


def _gather_start_body(ring, pieces_ref, weights_ref, tens_out, dp_out, t_send, t_recv, t_cross,
                       d_send, d_recv, d_cross, pair_send, pair_recv, local_sem):
    n_t = lax.axis_size("tensor")
    n_d = lax.axis_size("dp")
    t = lax.axis_index("tensor")
    r = lax.axis_index("dp")
    z = lax.rem(t, ring)
    t_base = t - z
    t_other = lax.rem(t + ring, n_t) - z
    t_far = lax.rem(t + ring, n_t)
    d_ring = n_d // 4
    core = lax.rem(r, 2)
    y = lax.rem(r // 2, d_ring)
    x = r // (2 * d_ring)
    d_base = x * 2 * d_ring + core
    d_other = (1 - x) * 2 * d_ring + core
    d_far = d_other + 2 * y
    pair = r + 1 - 2 * core
    rings = (
        ("tensor", tens_out, pieces_ref, z, (t_base, t_other), 1, ring, t_send, t_recv),
        ("dp", dp_out, weights_ref, y, (d_base, d_other), 2, d_ring, d_send, d_recv),
    )

    def neighbours(pos, bases, stride, n):
        return (bases[0] + lax.rem(pos + 1, n) * stride, bases[0] + lax.rem(pos + n - 1, n) * stride)

    barrier = pltpu.get_barrier_semaphore()
    targets = [{"tensor": t_far}, {"dp": pair}, {"dp": d_far}]
    for axis, _, _, pos, bases, stride, n, _, _ in rings:
        targets.extend({axis: v} for v in neighbours(pos, bases, stride, n))
    for device in targets:
        pl.semaphore_signal(barrier, inc=1, device_id=device, device_id_type=MESH_ID)
    pl.semaphore_wait(barrier, len(targets))

    def remote(src, dst, send, recv, device):
        copy = pltpu.make_async_remote_copy(
            src_ref=src, dst_ref=dst, send_sem=send, recv_sem=recv,
            device_id=device, device_id_type=MESH_ID,
        )
        copy.start()
        return copy

    waits = []
    forwarded = [0]

    def forward(src, slot):
        f = forwarded[0]
        waits.append(remote(src, dp_out.at[slot], pair_send.at[f], pair_recv.at[f], {"dp": pair}))
        forwarded[0] = f + 1

    forward(weights_ref, r)
    t_crossed = remote(pieces_ref, tens_out.at[t], t_cross.at[0], t_cross.at[1], {"tensor": t_far})
    d_crossed = remote(weights_ref, dp_out.at[r], d_cross.at[0], d_cross.at[1], {"dp": d_far})
    own_t = pltpu.make_async_copy(pieces_ref, tens_out.at[t], local_sem.at[0])
    own_t.start()
    own_d = pltpu.make_async_copy(weights_ref, dp_out.at[r], local_sem.at[1])
    own_d.start()
    t_crossed.wait()
    d_crossed.wait()
    forward(dp_out.at[d_far], d_far)
    moving = {}
    for s in range(max(ring, d_ring) // 2):
        for k, (axis, out, own, pos, bases, stride, n, send, recv) in enumerate(rings):
            right, left = neighbours(pos, bases, stride, n)
            steps = (n // 2, n - 1 - n // 2)
            for d, (target, sign) in enumerate(((right, -1), (left, 1))):
                if s >= steps[d]:
                    continue
                origin = lax.rem(pos + sign * s + n, n)
                if s > 0:
                    for copy in moving[k, d]:
                        copy.wait_recv()
                    if k == 1:
                        for start in bases:
                            slot = start + origin * stride
                            forward(out.at[slot], slot)
                sent = []
                for h, start in enumerate(bases):
                    slot = start + origin * stride
                    src = own if (s == 0 and h == 0) else out.at[slot]
                    sent.append(remote(src, out.at[slot], send.at[d, s, h], recv.at[d, s, h],
                                       {axis: target}))
                waits.extend(sent)
                moving[k, d] = sent
    for k, (axis, out, own, pos, bases, stride, n, send, recv) in enumerate(rings):
        steps = (n // 2, n - 1 - n // 2)
        for d, sign in enumerate((-1, 1)):
            for copy in moving[k, d]:
                copy.wait_recv()
            if k == 1:
                origin = lax.rem(pos + sign * steps[d] + n, n)
                for start in bases:
                    slot = start + origin * stride
                    forward(out.at[slot], slot)
    for copy in waits:
        copy.wait_send()
    for f in range(forwarded[0]):
        pltpu.make_async_copy(dp_out.at[0], dp_out.at[0], pair_recv.at[f]).wait()
    own_t.wait()
    own_d.wait()


def gather_start(pieces, weights, ring):
    n_t = lax.axis_size("tensor")
    n_d = lax.axis_size("dp")
    d_ring = n_d // 4
    moved = 2 * (n_t * pieces.size * pieces.dtype.itemsize + n_d * weights.size * weights.dtype.itemsize)
    return pl.pallas_call(
        functools.partial(_gather_start_body, ring),
        out_shape=[
            jax.ShapeDtypeStruct((n_t,) + pieces.shape, pieces.dtype),
            jax.ShapeDtypeStruct((n_d,) + weights.shape, weights.dtype),
        ],
        in_specs=[pl.BlockSpec(memory_space=pl.ANY)] * 2,
        out_specs=[pl.BlockSpec(memory_space=pl.ANY)] * 2,
        scratch_shapes=[
            pltpu.SemaphoreType.DMA((2, ring // 2, 2)),
            pltpu.SemaphoreType.DMA((2, ring // 2, 2)),
            pltpu.SemaphoreType.DMA((2,)),
            pltpu.SemaphoreType.DMA((2, d_ring // 2, 2)),
            pltpu.SemaphoreType.DMA((2, d_ring // 2, 2)),
            pltpu.SemaphoreType.DMA((2,)),
            pltpu.SemaphoreType.DMA((2 * d_ring,)),
            pltpu.SemaphoreType.DMA((2 * d_ring,)),
            pltpu.SemaphoreType.DMA((2,)),
        ],
        compiler_params=pltpu.CompilerParams(collective_id=0, has_side_effects=True),
        cost_estimate=pl.CostEstimate(flops=0, transcendentals=0, bytes_accessed=moved),
    )(pieces, weights)


def _pair_body(x_ref, o_ref, mine, theirs, send_sem, recv_sem, local_sem):
    r = lax.axis_index("dp")
    parity = lax.rem(r, 2)
    pair = r + 1 - 2 * parity
    slots, _, width = mine.shape
    barrier = pltpu.get_barrier_semaphore()
    pl.semaphore_signal(barrier, inc=1, device_id={"dp": pair}, device_id_type=MESH_ID)
    pl.semaphore_wait(barrier, 1)
    sent = []
    kept = []
    for i in range(slots):
        give = pl.ds(pl.multiple_of((2 * i + 1 - parity) * width, width), width)
        keep = pl.ds(pl.multiple_of((2 * i + parity) * width, width), width)
        copy = pltpu.make_async_remote_copy(
            src_ref=x_ref.at[:, give], dst_ref=theirs.at[i], send_sem=send_sem.at[i],
            recv_sem=recv_sem.at[i], device_id={"dp": pair}, device_id_type=MESH_ID,
        )
        copy.start()
        sent.append(copy)
        own = pltpu.make_async_copy(x_ref.at[:, keep], mine.at[i], local_sem.at[i])
        own.start()
        kept.append(own)
    for copy in sent:
        copy.wait()
    for copy in kept:
        copy.wait()
    o_ref[...] = (mine[...].astype(jnp.float32) + theirs[...].astype(jnp.float32)).astype(o_ref.dtype)


def pair_sum(x, width):
    rows, cols = x.shape
    slots = cols // width // 2
    shape = (slots, rows, width)
    return pl.pallas_call(
        _pair_body,
        out_shape=jax.ShapeDtypeStruct(shape, x.dtype),
        in_specs=[pl.BlockSpec(memory_space=pl.ANY)],
        out_specs=pl.BlockSpec(memory_space=pltpu.VMEM),
        scratch_shapes=[
            pltpu.VMEM(shape, x.dtype),
            pltpu.VMEM(shape, x.dtype),
            pltpu.SemaphoreType.DMA((slots,)),
            pltpu.SemaphoreType.DMA((slots,)),
            pltpu.SemaphoreType.DMA((slots,)),
        ],
        compiler_params=pltpu.CompilerParams(collective_id=4, has_side_effects=True),
        cost_estimate=pl.CostEstimate(
            flops=x.size // 2, transcendentals=0, bytes_accessed=2 * x.size * x.dtype.itemsize
        ),
    )(x)


def local(tokens, norm_gain, query_weight, kv_weight, out_weight, grad_out, doc_lengths):
    tensor_size = lax.axis_size("tensor")
    data_size = lax.axis_size("dp")
    tensor_index = lax.axis_index("tensor")
    sharers = tensor_size // KVH
    levels = sharers.bit_length() - 1
    contract_last = (((1,), (1,)), ((), ()))
    query_width = query_weight.shape[1]
    kv_width = kv_weight.shape[1]
    values32 = tokens.astype(jnp.float32)
    root_mean = jnp.sqrt(jnp.mean(values32 * values32, axis=-1) + epsilon)
    unit = values32 / root_mean[:, None]
    gain32 = norm_gain.astype(jnp.float32)
    normed_local = (unit * gain32).astype(jnp.bfloat16)
    rows = tokens.shape[0]
    pieces = jnp.stack([normed_local, grad_out])
    weights_local = jnp.concatenate([query_weight, kv_weight, out_weight.T], axis=1)
    tens_parts, weight_parts = gather_start(pieces, weights_local, RING)
    normed = tens_parts[:, 0].reshape(tensor_size * rows, -1)
    grad_full = tens_parts[:, 1].reshape(tensor_size * rows, -1)
    seq_length = normed.shape[0]
    weights_full = weight_parts.reshape(-1, weights_local.shape[1])
    query_full = weights_full[:, :query_width]
    kv_local = weights_full[:, query_width : query_width + kv_width]
    out_full_t = weights_full[:, query_width + kv_width :]
    queries = jnp.dot(normed, query_full, preferred_element_type=jnp.float32).astype(jnp.bfloat16)
    keyvals = jnp.dot(normed, kv_local, preferred_element_type=jnp.float32).astype(jnp.bfloat16)
    for bit_index in range(levels):
        partner = partner_2(keyvals, "tensor", bit_index)
        joined_upper_half = tensor_index >> bit_index & 1 == 1
        keyvals = jnp.concatenate(
            [
                jnp.where(joined_upper_half, partner, keyvals),
                jnp.where(joined_upper_half, keyvals, partner),
            ],
            axis=1,
        )
    key_rows = keyvals[:, :HD]
    value_rows = keyvals[:, HD:]
    out_grad = jnp.dot(grad_full, out_full_t, preferred_element_type=jnp.float32).astype(
        jnp.bfloat16
    )
    local_heads = queries.shape[1] // HD
    query_heads = queries.reshape(seq_length, local_heads, HD)
    out_heads = out_grad.reshape(seq_length, local_heads, HD)
    allowed = document_mask(doc_lengths[0], seq_length)
    scores = jnp.einsum(
        "qhd,td->hqt", query_heads, key_rows, preferred_element_type=jnp.float32
    ) / math.sqrt(HD)
    scores = jnp.where(allowed[None, :, :], scores, -1e30)
    peak = jnp.max(scores, axis=-1, keepdims=True)
    expo = jnp.exp(scores - peak)
    probs = expo / jnp.sum(expo, axis=-1, keepdims=True)
    probs_low = probs.astype(jnp.bfloat16)
    prob_grad = jnp.einsum("qhd,td->hqt", out_heads, value_rows, preferred_element_type=jnp.float32)
    inner = jnp.sum(probs * prob_grad, axis=-1, keepdims=True)
    score_grad = (probs * (prob_grad - inner) / math.sqrt(HD)).astype(jnp.bfloat16)
    query_grad = jnp.einsum("hqt,td->qhd", score_grad, key_rows, preferred_element_type=jnp.float32)
    query_grad = query_grad.astype(jnp.bfloat16).reshape(seq_length, local_heads * HD)
    key_part = jnp.einsum(
        "hqt,qhd->td", score_grad, query_heads, preferred_element_type=jnp.float32
    )
    value_part = jnp.einsum("hqt,qhd->td", probs_low, out_heads, preferred_element_type=jnp.float32)
    kv_partial = jnp.concatenate([key_part, value_part], axis=1)
    for bit_index in reversed(range(levels)):
        half_cols = kv_partial.shape[1] // 2
        upper_half = tensor_index >> bit_index & 1 == 1
        lower_cols = kv_partial[:, :half_cols]
        higher_cols = kv_partial[:, half_cols:]
        kept = jnp.where(upper_half, higher_cols, lower_cols)
        handed = jnp.where(upper_half, lower_cols, higher_cols)
        kv_partial = kept + partner_2(handed.astype(jnp.bfloat16), "tensor", bit_index).astype(
            handed.dtype
        )
    kv_grad = kv_partial.astype(jnp.bfloat16)
    from_query = lax.dot_general(
        query_grad, query_full, contract_last, preferred_element_type=jnp.float32
    )
    from_kv = lax.dot_general(kv_grad, kv_local, contract_last, preferred_element_type=jnp.float32)
    partial = (from_query + from_kv).astype(jnp.bfloat16).reshape(tensor_size, rows, -1)
    combined = jnp.concatenate([query_grad, kv_grad], axis=1)
    weight_partial = lax.dot_general(
        combined, normed, (((0,), (0,)), ((), ())), preferred_element_type=jnp.float32
    ).astype(jnp.bfloat16)
    block = weight_partial.shape[1] // data_size
    paired = pair_sum(weight_partial, block)
    arrived, weight_arrived = push_exchange(
        [
            ("tensor", tensor_size, partial, True),
            ("dp", data_size // 2, paired, True, 2),
        ],
        1,
    )
    normed_grad = jnp.sum(arrived.astype(jnp.float32), axis=0)
    scaled = normed_grad * gain32
    correction = unit * jnp.mean(scaled * unit, axis=-1, keepdims=True)
    input_grad = (grad_out.astype(jnp.float32) + (scaled - correction) / root_mean[:, None]).astype(
        jnp.bfloat16
    )
    weight_grads = (jnp.sum(weight_arrived.astype(jnp.float32), axis=0) / data_size).T
    return (input_grad, weight_grads[:, :query_width], weight_grads[:, query_width:])


def solution(mesh):
    placed = (
        P(("dp", "tensor"), None),
        P(),
        P("dp", "tensor"),
        P("dp", "tensor"),
        P("tensor", "dp"),
        P(("dp", "tensor"), None),
        P("dp", None),
    )
    return jax.shard_map(
        local,
        mesh=mesh,
        in_specs=placed,
        out_specs=(P(("dp", "tensor"), None), P("dp", "tensor"), P("dp", "tensor")),
        check_vma=False,
    )
```

```python
import functools
import math

import jax
import jax.numpy as jnp
from jax import lax
from jax.experimental import pallas as pl
from jax.experimental.pallas import tpu as pltpu
from jax.sharding import PartitionSpec as P

KVH = 4
HD = 128
MESH_ID = pl.DeviceIdType.MESH
RING = 8


epsilon = 1e-05


def partner_2(value, axis, bit):
    mask = 2**bit
    pairs = [(source, source ^ mask) for source in range(lax.axis_size(axis))]
    return lax.ppermute(value, axis, pairs)


def document_mask(lengths, length_total):
    ends = jnp.cumsum(lengths)
    positions = jnp.arange(length_total, dtype=jnp.int32)
    labels = jnp.sum((ends[None, :] <= positions[:, None]).astype(jnp.int32), axis=1)
    return (labels[:, None] == labels[None, :]) & (positions[None, :] <= positions[:, None])


def _push_body(plan, *refs):
    count = len(plan)
    ins = refs[:count]
    outs = refs[count : 2 * count]
    send_sems = refs[2 * count : 3 * count]
    recv_sems = refs[3 * count : 4 * count]
    local_sem = refs[4 * count]
    barrier = pltpu.get_barrier_semaphore()
    mine = []
    expected = 0
    places = []
    for axis, n, _, stride in plan:
        index = lax.axis_index(axis)
        me = lax.rem(index // stride, n)
        offset = index - me * stride
        mine.append(me)
        places.append(functools.partial(lambda o, st, p: o + p * st, offset, stride))
        for j in range(1, n):
            pl.semaphore_signal(
                barrier,
                inc=1,
                device_id={axis: places[-1](lax.rem(me + j, n))},
                device_id_type=MESH_ID,
            )
        expected += n - 1
    pl.semaphore_wait(barrier, expected)
    local = []
    for g, (axis, n, scatter, _) in enumerate(plan):
        me = mine[g]
        src = ins[g].at[me] if scatter else ins[g]
        copy = pltpu.make_async_copy(src, outs[g].at[me], local_sem.at[g])
        copy.start()
        local.append(copy)
    remote = []
    for j in range(1, max(n for _, n, _, _ in plan)):
        for g, (axis, n, scatter, _) in enumerate(plan):
            if j >= n:
                continue
            me = mine[g]
            peer = lax.rem(me + j, n)
            copy = pltpu.make_async_remote_copy(
                src_ref=ins[g].at[peer] if scatter else ins[g],
                dst_ref=outs[g].at[me],
                send_sem=send_sems[g].at[j],
                recv_sem=recv_sems[g].at[j],
                device_id={axis: places[g](peer)},
                device_id_type=MESH_ID,
            )
            copy.start()
            remote.append(copy)
    for copy in remote:
        copy.wait()
    for copy in local:
        copy.wait()


def push_exchange(groups, cid):
    groups = [g if len(g) == 5 else g + (1,) for g in groups]
    plan = tuple((axis, n, scatter, stride) for axis, n, _, scatter, stride in groups)
    arrays = [array for _, _, array, _, _ in groups]
    out_shape = []
    moved = 0
    for _, n, array, scatter, _ in groups:
        shape = array.shape if scatter else (n,) + array.shape
        out_shape.append(jax.ShapeDtypeStruct(shape, array.dtype))
        moved += 2 * math.prod(shape) * array.dtype.itemsize
    count = len(groups)
    return pl.pallas_call(
        functools.partial(_push_body, plan),
        out_shape=out_shape,
        in_specs=[pl.BlockSpec(memory_space=pl.ANY)] * count,
        out_specs=[pl.BlockSpec(memory_space=pl.ANY)] * count,
        scratch_shapes=[pltpu.SemaphoreType.DMA((n,)) for _, n, _, _, _ in groups]
        + [pltpu.SemaphoreType.DMA((n,)) for _, n, _, _, _ in groups]
        + [pltpu.SemaphoreType.DMA((count,))],
        compiler_params=pltpu.CompilerParams(collective_id=cid, has_side_effects=True),
        cost_estimate=pl.CostEstimate(flops=0, transcendentals=0, bytes_accessed=moved),
    )(*arrays)


def _gather_start_body(ring, pieces_ref, weights_ref, tens_out, dp_out, t_send, t_recv, t_cross,
                       d_send, d_recv, d_cross, pair_send, pair_recv, local_sem):
    n_t = lax.axis_size("tensor")
    n_d = lax.axis_size("dp")
    t = lax.axis_index("tensor")
    r = lax.axis_index("dp")
    z = lax.rem(t, ring)
    t_base = t - z
    t_other = lax.rem(t + ring, n_t) - z
    t_far = lax.rem(t + ring, n_t)
    d_ring = n_d // 4
    core = lax.rem(r, 2)
    y = lax.rem(r // 2, d_ring)
    x = r // (2 * d_ring)
    d_base = x * 2 * d_ring + core
    d_other = (1 - x) * 2 * d_ring + core
    d_far = d_other + 2 * y
    pair = r + 1 - 2 * core
    rings = (
        ("tensor", tens_out, pieces_ref, z, (t_base, t_other), 1, ring, t_send, t_recv),
        ("dp", dp_out, weights_ref, y, (d_base, d_other), 2, d_ring, d_send, d_recv),
    )

    def neighbours(pos, bases, stride, n):
        return (bases[0] + lax.rem(pos + 1, n) * stride, bases[0] + lax.rem(pos + n - 1, n) * stride)

    barrier = pltpu.get_barrier_semaphore()
    targets = [{"tensor": t_far}, {"dp": pair}, {"dp": d_far}]
    for axis, _, _, pos, bases, stride, n, _, _ in rings:
        targets.extend({axis: v} for v in neighbours(pos, bases, stride, n))
    for device in targets:
        pl.semaphore_signal(barrier, inc=1, device_id=device, device_id_type=MESH_ID)
    pl.semaphore_wait(barrier, len(targets))

    def remote(src, dst, send, recv, device):
        copy = pltpu.make_async_remote_copy(
            src_ref=src, dst_ref=dst, send_sem=send, recv_sem=recv,
            device_id=device, device_id_type=MESH_ID,
        )
        copy.start()
        return copy

    waits = []
    forwarded = [0]

    def forward(src, slot):
        f = forwarded[0]
        waits.append(remote(src, dp_out.at[slot], pair_send.at[f], pair_recv.at[f], {"dp": pair}))
        forwarded[0] = f + 1

    forward(weights_ref, r)
    t_crossed = remote(pieces_ref, tens_out.at[t], t_cross.at[0], t_cross.at[1], {"tensor": t_far})
    d_crossed = remote(weights_ref, dp_out.at[r], d_cross.at[0], d_cross.at[1], {"dp": d_far})
    own_t = pltpu.make_async_copy(pieces_ref, tens_out.at[t], local_sem.at[0])
    own_t.start()
    own_d = pltpu.make_async_copy(weights_ref, dp_out.at[r], local_sem.at[1])
    own_d.start()
    t_crossed.wait()
    d_crossed.wait()
    forward(dp_out.at[d_far], d_far)
    moving = {}
    for s in range(max(ring, d_ring) // 2):
        for k, (axis, out, own, pos, bases, stride, n, send, recv) in enumerate(rings):
            right, left = neighbours(pos, bases, stride, n)
            steps = (n // 2, n - 1 - n // 2)
            for d, (target, sign) in enumerate(((right, -1), (left, 1))):
                if s >= steps[d]:
                    continue
                origin = lax.rem(pos + sign * s + n, n)
                if s > 0:
                    for copy in moving[k, d]:
                        copy.wait_recv()
                    if k == 1:
                        for start in bases:
                            slot = start + origin * stride
                            forward(out.at[slot], slot)
                sent = []
                for h, start in enumerate(bases):
                    slot = start + origin * stride
                    src = own if (s == 0 and h == 0) else out.at[slot]
                    sent.append(remote(src, out.at[slot], send.at[d, s, h], recv.at[d, s, h],
                                       {axis: target}))
                waits.extend(sent)
                moving[k, d] = sent
    for k, (axis, out, own, pos, bases, stride, n, send, recv) in enumerate(rings):
        steps = (n // 2, n - 1 - n // 2)
        for d, sign in enumerate((-1, 1)):
            for copy in moving[k, d]:
                copy.wait_recv()
            if k == 1:
                origin = lax.rem(pos + sign * steps[d] + n, n)
                for start in bases:
                    slot = start + origin * stride
                    forward(out.at[slot], slot)
    for copy in waits:
        copy.wait_send()
    for f in range(forwarded[0]):
        pltpu.make_async_copy(dp_out.at[0], dp_out.at[0], pair_recv.at[f]).wait()
    own_t.wait()
    own_d.wait()


def gather_start(pieces, weights, ring):
    n_t = lax.axis_size("tensor")
    n_d = lax.axis_size("dp")
    d_ring = n_d // 4
    moved = 2 * (n_t * pieces.size * pieces.dtype.itemsize + n_d * weights.size * weights.dtype.itemsize)
    return pl.pallas_call(
        functools.partial(_gather_start_body, ring),
        out_shape=[
            jax.ShapeDtypeStruct((n_t,) + pieces.shape, pieces.dtype),
            jax.ShapeDtypeStruct((n_d,) + weights.shape, weights.dtype),
        ],
        in_specs=[pl.BlockSpec(memory_space=pl.ANY)] * 2,
        out_specs=[pl.BlockSpec(memory_space=pl.ANY)] * 2,
        scratch_shapes=[
            pltpu.SemaphoreType.DMA((2, ring // 2, 2)),
            pltpu.SemaphoreType.DMA((2, ring // 2, 2)),
            pltpu.SemaphoreType.DMA((2,)),
            pltpu.SemaphoreType.DMA((2, d_ring // 2, 2)),
            pltpu.SemaphoreType.DMA((2, d_ring // 2, 2)),
            pltpu.SemaphoreType.DMA((2,)),
            pltpu.SemaphoreType.DMA((2 * d_ring,)),
            pltpu.SemaphoreType.DMA((2 * d_ring,)),
            pltpu.SemaphoreType.DMA((2,)),
        ],
        compiler_params=pltpu.CompilerParams(collective_id=0, has_side_effects=True),
        cost_estimate=pl.CostEstimate(flops=0, transcendentals=0, bytes_accessed=moved),
    )(pieces, weights)


def _pair_body(x_ref, o_ref, mine, theirs, send_sem, recv_sem, local_sem):
    r = lax.axis_index("dp")
    parity = lax.rem(r, 2)
    pair = r + 1 - 2 * parity
    slots, _, width = mine.shape
    barrier = pltpu.get_barrier_semaphore()
    pl.semaphore_signal(barrier, inc=1, device_id={"dp": pair}, device_id_type=MESH_ID)
    pl.semaphore_wait(barrier, 1)
    sent = []
    kept = []
    for i in range(slots):
        give = pl.ds(pl.multiple_of((2 * i + 1 - parity) * width, width), width)
        keep = pl.ds(pl.multiple_of((2 * i + parity) * width, width), width)
        copy = pltpu.make_async_remote_copy(
            src_ref=x_ref.at[:, give], dst_ref=theirs.at[i], send_sem=send_sem.at[i],
            recv_sem=recv_sem.at[i], device_id={"dp": pair}, device_id_type=MESH_ID,
        )
        copy.start()
        sent.append(copy)
        own = pltpu.make_async_copy(x_ref.at[:, keep], mine.at[i], local_sem.at[i])
        own.start()
        kept.append(own)
    for copy in sent:
        copy.wait()
    for copy in kept:
        copy.wait()
    o_ref[...] = (mine[...].astype(jnp.float32) + theirs[...].astype(jnp.float32)).astype(o_ref.dtype)


def pair_sum(x, width):
    rows, cols = x.shape
    slots = cols // width // 2
    shape = (slots, rows, width)
    return pl.pallas_call(
        _pair_body,
        out_shape=jax.ShapeDtypeStruct(shape, x.dtype),
        in_specs=[pl.BlockSpec(memory_space=pl.ANY)],
        out_specs=pl.BlockSpec(memory_space=pltpu.VMEM),
        scratch_shapes=[
            pltpu.VMEM(shape, x.dtype),
            pltpu.VMEM(shape, x.dtype),
            pltpu.SemaphoreType.DMA((slots,)),
            pltpu.SemaphoreType.DMA((slots,)),
            pltpu.SemaphoreType.DMA((slots,)),
        ],
        compiler_params=pltpu.CompilerParams(collective_id=4, has_side_effects=True),
        cost_estimate=pl.CostEstimate(
            flops=x.size // 2, transcendentals=0, bytes_accessed=2 * x.size * x.dtype.itemsize
        ),
    )(x)


def _end_body(ring, x_ref, w_ref, o_ref, w_out, send_buf, recv_buf, cross_buf, cross_in,
              t_send, t_recv, c_sem, w_send, w_recv, local_sem):
    n_t = lax.axis_size("tensor")
    n_d = lax.axis_size("dp")
    t = lax.axis_index("tensor")
    r = lax.axis_index("dp")
    z = lax.rem(t, ring)
    t_base = t - z
    t_other = lax.rem(t + ring, n_t) - z
    t_far = lax.rem(t + ring, n_t)
    right = t_base + lax.rem(z + 1, ring)
    left = t_base + lax.rem(z + ring - 1, ring)
    parity = lax.rem(r, 2)
    n_w = n_d // 2
    me_w = r // 2
    barrier = pltpu.get_barrier_semaphore()
    for device in ({"tensor": t_far}, {"tensor": right}, {"tensor": left}):
        pl.semaphore_signal(barrier, inc=1, device_id=device, device_id_type=MESH_ID)
    for j in range(1, n_w):
        peer = 2 * lax.rem(me_w + j, n_w) + parity
        pl.semaphore_signal(barrier, inc=1, device_id={"dp": peer}, device_id_type=MESH_ID)
    pl.semaphore_wait(barrier, 3 + n_w - 1)

    def remote(src, dst, send, recv, device):
        copy = pltpu.make_async_remote_copy(
            src_ref=src, dst_ref=dst, send_sem=send, recv_sem=recv,
            device_id=device, device_id_type=MESH_ID,
        )
        copy.start()
        return copy

    waits = []
    for j in range(1, n_w):
        peer = lax.rem(me_w + j, n_w)
        waits.append(remote(w_ref.at[peer], w_out.at[me_w], w_send.at[j], w_recv.at[j],
                            {"dp": 2 * peer + parity}))
    own_w = pltpu.make_async_copy(w_ref.at[me_w], w_out.at[me_w], local_sem.at[0])
    own_w.start()
    steps = (ring // 2, ring - 1 - ring // 2)
    moving = [None, None]
    for s in range(max(steps)):
        for d, (target, sign) in enumerate(((right, -1), (left, 1))):
            if s >= steps[d]:
                continue
            q = lax.rem(z - sign * (steps[d] - s) + 2 * ring, ring)
            sent = []
            for h, start in enumerate((t_base, t_other)):
                slot = start + q
                if s == 0:
                    src = x_ref.at[slot]
                else:
                    moving[d][h].wait_recv()
                    send_buf[d, s, h] = (
                        recv_buf[d, s - 1, h].astype(jnp.float32) + x_ref[slot].astype(jnp.float32)
                    ).astype(send_buf.dtype)
                    src = send_buf.at[d, s, h]
                sent.append(remote(src, recv_buf.at[d, s, h], t_send.at[d, s, h],
                                   t_recv.at[d, s, h], {"tensor": target}))
            waits.extend(sent)
            moving[d] = sent
    for d in range(2):
        for copy in moving[d]:
            copy.wait_recv()
    plus, minus = steps[0] - 1, steps[1] - 1
    cross_buf[...] = (
        x_ref[t_far].astype(jnp.float32)
        + recv_buf[0, plus, 1].astype(jnp.float32)
        + recv_buf[1, minus, 1].astype(jnp.float32)
    ).astype(cross_buf.dtype)
    crossed = remote(cross_buf, cross_in, c_sem.at[0], c_sem.at[1], {"tensor": t_far})
    crossed.wait()
    o_ref[...] = (
        x_ref[t].astype(jnp.float32)
        + recv_buf[0, plus, 0].astype(jnp.float32)
        + recv_buf[1, minus, 0].astype(jnp.float32)
        + cross_in[...].astype(jnp.float32)
    )
    for copy in waits:
        copy.wait_send()
    for j in range(1, n_w):
        pltpu.make_async_copy(w_out.at[0], w_out.at[0], w_recv.at[j]).wait()
    own_w.wait()


def end_exchange(partial, paired, ring):
    n_t, rows, cols = partial.shape
    n_w = paired.shape[0]
    piece = (rows, cols)
    moved = 2 * (partial.size * partial.dtype.itemsize + paired.size * paired.dtype.itemsize)
    return pl.pallas_call(
        functools.partial(_end_body, ring),
        out_shape=[
            jax.ShapeDtypeStruct(piece, jnp.float32),
            jax.ShapeDtypeStruct(paired.shape, paired.dtype),
        ],
        in_specs=[pl.BlockSpec(memory_space=pltpu.VMEM), pl.BlockSpec(memory_space=pl.ANY)],
        out_specs=[pl.BlockSpec(memory_space=pltpu.VMEM), pl.BlockSpec(memory_space=pl.ANY)],
        scratch_shapes=[
            pltpu.VMEM((2, ring // 2, 2) + piece, partial.dtype),
            pltpu.VMEM((2, ring // 2, 2) + piece, partial.dtype),
            pltpu.VMEM(piece, partial.dtype),
            pltpu.VMEM(piece, partial.dtype),
            pltpu.SemaphoreType.DMA((2, ring // 2, 2)),
            pltpu.SemaphoreType.DMA((2, ring // 2, 2)),
            pltpu.SemaphoreType.DMA((2,)),
            pltpu.SemaphoreType.DMA((n_w,)),
            pltpu.SemaphoreType.DMA((n_w,)),
            pltpu.SemaphoreType.DMA((1,)),
        ],
        compiler_params=pltpu.CompilerParams(collective_id=1, has_side_effects=True),
        cost_estimate=pl.CostEstimate(flops=4 * partial.size, transcendentals=0, bytes_accessed=moved),
    )(partial, paired)


def local(tokens, norm_gain, query_weight, kv_weight, out_weight, grad_out, doc_lengths):
    tensor_size = lax.axis_size("tensor")
    data_size = lax.axis_size("dp")
    tensor_index = lax.axis_index("tensor")
    sharers = tensor_size // KVH
    levels = sharers.bit_length() - 1
    contract_last = (((1,), (1,)), ((), ()))
    query_width = query_weight.shape[1]
    kv_width = kv_weight.shape[1]
    values32 = tokens.astype(jnp.float32)
    root_mean = jnp.sqrt(jnp.mean(values32 * values32, axis=-1) + epsilon)
    unit = values32 / root_mean[:, None]
    gain32 = norm_gain.astype(jnp.float32)
    normed_local = (unit * gain32).astype(jnp.bfloat16)
    rows = tokens.shape[0]
    pieces = jnp.stack([normed_local, grad_out])
    weights_local = jnp.concatenate([query_weight, kv_weight, out_weight.T], axis=1)
    tens_parts, weight_parts = gather_start(pieces, weights_local, RING)
    normed = tens_parts[:, 0].reshape(tensor_size * rows, -1)
    grad_full = tens_parts[:, 1].reshape(tensor_size * rows, -1)
    seq_length = normed.shape[0]
    weights_full = weight_parts.reshape(-1, weights_local.shape[1])
    query_full = weights_full[:, :query_width]
    kv_local = weights_full[:, query_width : query_width + kv_width]
    out_full_t = weights_full[:, query_width + kv_width :]
    queries = jnp.dot(normed, query_full, preferred_element_type=jnp.float32).astype(jnp.bfloat16)
    keyvals = jnp.dot(normed, kv_local, preferred_element_type=jnp.float32).astype(jnp.bfloat16)
    for bit_index in range(levels):
        partner = partner_2(keyvals, "tensor", bit_index)
        joined_upper_half = tensor_index >> bit_index & 1 == 1
        keyvals = jnp.concatenate(
            [
                jnp.where(joined_upper_half, partner, keyvals),
                jnp.where(joined_upper_half, keyvals, partner),
            ],
            axis=1,
        )
    key_rows = keyvals[:, :HD]
    value_rows = keyvals[:, HD:]
    out_grad = jnp.dot(grad_full, out_full_t, preferred_element_type=jnp.float32).astype(
        jnp.bfloat16
    )
    local_heads = queries.shape[1] // HD
    query_heads = queries.reshape(seq_length, local_heads, HD)
    out_heads = out_grad.reshape(seq_length, local_heads, HD)
    allowed = document_mask(doc_lengths[0], seq_length)
    scores = jnp.einsum(
        "qhd,td->hqt", query_heads, key_rows, preferred_element_type=jnp.float32
    ) / math.sqrt(HD)
    scores = jnp.where(allowed[None, :, :], scores, -1e30)
    peak = jnp.max(scores, axis=-1, keepdims=True)
    expo = jnp.exp(scores - peak)
    probs = expo / jnp.sum(expo, axis=-1, keepdims=True)
    probs_low = probs.astype(jnp.bfloat16)
    prob_grad = jnp.einsum("qhd,td->hqt", out_heads, value_rows, preferred_element_type=jnp.float32)
    inner = jnp.sum(probs * prob_grad, axis=-1, keepdims=True)
    score_grad = (probs * (prob_grad - inner) / math.sqrt(HD)).astype(jnp.bfloat16)
    query_grad = jnp.einsum("hqt,td->qhd", score_grad, key_rows, preferred_element_type=jnp.float32)
    query_grad = query_grad.astype(jnp.bfloat16).reshape(seq_length, local_heads * HD)
    key_part = jnp.einsum(
        "hqt,qhd->td", score_grad, query_heads, preferred_element_type=jnp.float32
    )
    value_part = jnp.einsum("hqt,qhd->td", probs_low, out_heads, preferred_element_type=jnp.float32)
    kv_partial = jnp.concatenate([key_part, value_part], axis=1)
    for bit_index in reversed(range(levels)):
        half_cols = kv_partial.shape[1] // 2
        upper_half = tensor_index >> bit_index & 1 == 1
        lower_cols = kv_partial[:, :half_cols]
        higher_cols = kv_partial[:, half_cols:]
        kept = jnp.where(upper_half, higher_cols, lower_cols)
        handed = jnp.where(upper_half, lower_cols, higher_cols)
        kv_partial = kept + partner_2(handed.astype(jnp.bfloat16), "tensor", bit_index).astype(
            handed.dtype
        )
    kv_grad = kv_partial.astype(jnp.bfloat16)
    from_query = lax.dot_general(
        query_grad, query_full, contract_last, preferred_element_type=jnp.float32
    )
    from_kv = lax.dot_general(kv_grad, kv_local, contract_last, preferred_element_type=jnp.float32)
    partial = (from_query + from_kv).astype(jnp.bfloat16).reshape(tensor_size, rows, -1)
    combined = jnp.concatenate([query_grad, kv_grad], axis=1)
    weight_partial = lax.dot_general(
        combined, normed, (((0,), (0,)), ((), ())), preferred_element_type=jnp.float32
    ).astype(jnp.bfloat16)
    block = weight_partial.shape[1] // data_size
    paired = pair_sum(weight_partial, block)
    normed_grad, weight_arrived = end_exchange(partial, paired, RING)
    scaled = normed_grad * gain32
    correction = unit * jnp.mean(scaled * unit, axis=-1, keepdims=True)
    input_grad = (grad_out.astype(jnp.float32) + (scaled - correction) / root_mean[:, None]).astype(
        jnp.bfloat16
    )
    weight_grads = (jnp.sum(weight_arrived.astype(jnp.float32), axis=0) / data_size).T
    return (input_grad, weight_grads[:, :query_width], weight_grads[:, query_width:])


def solution(mesh):
    placed = (
        P(("dp", "tensor"), None),
        P(),
        P("dp", "tensor"),
        P("dp", "tensor"),
        P("tensor", "dp"),
        P(("dp", "tensor"), None),
        P("dp", None),
    )
    return jax.shard_map(
        local,
        mesh=mesh,
        in_specs=placed,
        out_specs=(P(("dp", "tensor"), None), P("dp", "tensor"), P("dp", "tensor")),
        check_vma=False,
    )
```

```python
import functools
import math

import jax
import jax.numpy as jnp
from jax import lax
from jax.experimental import pallas as pl
from jax.experimental.pallas import tpu as pltpu
from jax.sharding import PartitionSpec as P

KVH = 4
HD = 128
MESH_ID = pl.DeviceIdType.MESH
RING = 8


epsilon = 1e-05


def partner_2(value, axis, bit):
    mask = 2**bit
    pairs = [(source, source ^ mask) for source in range(lax.axis_size(axis))]
    return lax.ppermute(value, axis, pairs)


def document_mask(lengths, length_total):
    ends = jnp.cumsum(lengths)
    positions = jnp.arange(length_total, dtype=jnp.int32)
    labels = jnp.sum((ends[None, :] <= positions[:, None]).astype(jnp.int32), axis=1)
    return (labels[:, None] == labels[None, :]) & (positions[None, :] <= positions[:, None])


def _push_body(plan, *refs):
    count = len(plan)
    ins = refs[:count]
    outs = refs[count : 2 * count]
    send_sems = refs[2 * count : 3 * count]
    recv_sems = refs[3 * count : 4 * count]
    local_sem = refs[4 * count]
    barrier = pltpu.get_barrier_semaphore()
    mine = []
    expected = 0
    places = []
    for axis, n, _, stride in plan:
        index = lax.axis_index(axis)
        me = lax.rem(index // stride, n)
        offset = index - me * stride
        mine.append(me)
        places.append(functools.partial(lambda o, st, p: o + p * st, offset, stride))
        for j in range(1, n):
            pl.semaphore_signal(
                barrier,
                inc=1,
                device_id={axis: places[-1](lax.rem(me + j, n))},
                device_id_type=MESH_ID,
            )
        expected += n - 1
    pl.semaphore_wait(barrier, expected)
    local = []
    for g, (axis, n, scatter, _) in enumerate(plan):
        me = mine[g]
        src = ins[g].at[me] if scatter else ins[g]
        copy = pltpu.make_async_copy(src, outs[g].at[me], local_sem.at[g])
        copy.start()
        local.append(copy)
    remote = []
    for j in range(1, max(n for _, n, _, _ in plan)):
        for g, (axis, n, scatter, _) in enumerate(plan):
            if j >= n:
                continue
            me = mine[g]
            peer = lax.rem(me + j, n)
            copy = pltpu.make_async_remote_copy(
                src_ref=ins[g].at[peer] if scatter else ins[g],
                dst_ref=outs[g].at[me],
                send_sem=send_sems[g].at[j],
                recv_sem=recv_sems[g].at[j],
                device_id={axis: places[g](peer)},
                device_id_type=MESH_ID,
            )
            copy.start()
            remote.append(copy)
    for copy in remote:
        copy.wait()
    for copy in local:
        copy.wait()


def push_exchange(groups, cid):
    groups = [g if len(g) == 5 else g + (1,) for g in groups]
    plan = tuple((axis, n, scatter, stride) for axis, n, _, scatter, stride in groups)
    arrays = [array for _, _, array, _, _ in groups]
    out_shape = []
    moved = 0
    for _, n, array, scatter, _ in groups:
        shape = array.shape if scatter else (n,) + array.shape
        out_shape.append(jax.ShapeDtypeStruct(shape, array.dtype))
        moved += 2 * math.prod(shape) * array.dtype.itemsize
    count = len(groups)
    return pl.pallas_call(
        functools.partial(_push_body, plan),
        out_shape=out_shape,
        in_specs=[pl.BlockSpec(memory_space=pl.ANY)] * count,
        out_specs=[pl.BlockSpec(memory_space=pl.ANY)] * count,
        scratch_shapes=[pltpu.SemaphoreType.DMA((n,)) for _, n, _, _, _ in groups]
        + [pltpu.SemaphoreType.DMA((n,)) for _, n, _, _, _ in groups]
        + [pltpu.SemaphoreType.DMA((count,))],
        compiler_params=pltpu.CompilerParams(collective_id=cid, has_side_effects=True),
        cost_estimate=pl.CostEstimate(flops=0, transcendentals=0, bytes_accessed=moved),
    )(*arrays)


def _gather_start_body(ring, pieces_ref, weights_ref, tens_out, dp_out, t_send, t_recv, t_cross,
                       d_send, d_recv, d_cross, pair_send, pair_recv, local_sem):
    n_t = lax.axis_size("tensor")
    n_d = lax.axis_size("dp")
    t = lax.axis_index("tensor")
    r = lax.axis_index("dp")
    z = lax.rem(t, ring)
    t_base = t - z
    t_other = lax.rem(t + ring, n_t) - z
    t_far = lax.rem(t + ring, n_t)
    d_ring = n_d // 4
    core = lax.rem(r, 2)
    y = lax.rem(r // 2, d_ring)
    x = r // (2 * d_ring)
    d_base = x * 2 * d_ring + core
    d_other = (1 - x) * 2 * d_ring + core
    d_far = d_other + 2 * y
    pair = r + 1 - 2 * core
    rings = (
        ("tensor", tens_out, pieces_ref, z, (t_base, t_other), 1, ring, t_send, t_recv),
        ("dp", dp_out, weights_ref, y, (d_base, d_other), 2, d_ring, d_send, d_recv),
    )

    def neighbours(pos, bases, stride, n):
        return (bases[0] + lax.rem(pos + 1, n) * stride, bases[0] + lax.rem(pos + n - 1, n) * stride)

    barrier = pltpu.get_barrier_semaphore()
    targets = [{"tensor": t_far}, {"dp": pair}, {"dp": d_far}]
    for axis, _, _, pos, bases, stride, n, _, _ in rings:
        targets.extend({axis: v} for v in neighbours(pos, bases, stride, n))
    for device in targets:
        pl.semaphore_signal(barrier, inc=1, device_id=device, device_id_type=MESH_ID)
    pl.semaphore_wait(barrier, len(targets))

    def remote(src, dst, send, recv, device):
        copy = pltpu.make_async_remote_copy(
            src_ref=src, dst_ref=dst, send_sem=send, recv_sem=recv,
            device_id=device, device_id_type=MESH_ID,
        )
        copy.start()
        return copy

    waits = []
    forwarded = [0]

    def forward(src, slot):
        f = forwarded[0]
        waits.append(remote(src, dp_out.at[slot], pair_send.at[f], pair_recv.at[f], {"dp": pair}))
        forwarded[0] = f + 1

    forward(weights_ref, r)
    t_crossed = remote(pieces_ref, tens_out.at[t], t_cross.at[0], t_cross.at[1], {"tensor": t_far})
    d_crossed = remote(weights_ref, dp_out.at[r], d_cross.at[0], d_cross.at[1], {"dp": d_far})
    own_t = pltpu.make_async_copy(pieces_ref, tens_out.at[t], local_sem.at[0])
    own_t.start()
    own_d = pltpu.make_async_copy(weights_ref, dp_out.at[r], local_sem.at[1])
    own_d.start()
    t_crossed.wait()
    d_crossed.wait()
    forward(dp_out.at[d_far], d_far)
    moving = {}
    for s in range(max(ring, d_ring) // 2):
        for k, (axis, out, own, pos, bases, stride, n, send, recv) in enumerate(rings):
            right, left = neighbours(pos, bases, stride, n)
            steps = (n // 2, n - 1 - n // 2)
            for d, (target, sign) in enumerate(((right, -1), (left, 1))):
                if s >= steps[d]:
                    continue
                origin = lax.rem(pos + sign * s + n, n)
                if s > 0:
                    for copy in moving[k, d]:
                        copy.wait_recv()
                    if k == 1:
                        for start in bases:
                            slot = start + origin * stride
                            forward(out.at[slot], slot)
                sent = []
                for h, start in enumerate(bases):
                    slot = start + origin * stride
                    src = own if (s == 0 and h == 0) else out.at[slot]
                    sent.append(remote(src, out.at[slot], send.at[d, s, h], recv.at[d, s, h],
                                       {axis: target}))
                waits.extend(sent)
                moving[k, d] = sent
    for k, (axis, out, own, pos, bases, stride, n, send, recv) in enumerate(rings):
        steps = (n // 2, n - 1 - n // 2)
        for d, sign in enumerate((-1, 1)):
            for copy in moving[k, d]:
                copy.wait_recv()
            if k == 1:
                origin = lax.rem(pos + sign * steps[d] + n, n)
                for start in bases:
                    slot = start + origin * stride
                    forward(out.at[slot], slot)
    for copy in waits:
        copy.wait_send()
    for f in range(forwarded[0]):
        pltpu.make_async_copy(dp_out.at[0], dp_out.at[0], pair_recv.at[f]).wait()
    own_t.wait()
    own_d.wait()


def gather_start(pieces, weights, ring):
    n_t = lax.axis_size("tensor")
    n_d = lax.axis_size("dp")
    d_ring = n_d // 4
    moved = 2 * (n_t * pieces.size * pieces.dtype.itemsize + n_d * weights.size * weights.dtype.itemsize)
    return pl.pallas_call(
        functools.partial(_gather_start_body, ring),
        out_shape=[
            jax.ShapeDtypeStruct((n_t,) + pieces.shape, pieces.dtype),
            jax.ShapeDtypeStruct((n_d,) + weights.shape, weights.dtype),
        ],
        in_specs=[pl.BlockSpec(memory_space=pl.ANY)] * 2,
        out_specs=[pl.BlockSpec(memory_space=pl.ANY)] * 2,
        scratch_shapes=[
            pltpu.SemaphoreType.DMA((2, ring // 2, 2)),
            pltpu.SemaphoreType.DMA((2, ring // 2, 2)),
            pltpu.SemaphoreType.DMA((2,)),
            pltpu.SemaphoreType.DMA((2, d_ring // 2, 2)),
            pltpu.SemaphoreType.DMA((2, d_ring // 2, 2)),
            pltpu.SemaphoreType.DMA((2,)),
            pltpu.SemaphoreType.DMA((2 * d_ring,)),
            pltpu.SemaphoreType.DMA((2 * d_ring,)),
            pltpu.SemaphoreType.DMA((2,)),
        ],
        compiler_params=pltpu.CompilerParams(collective_id=0, has_side_effects=True),
        cost_estimate=pl.CostEstimate(flops=0, transcendentals=0, bytes_accessed=moved),
    )(pieces, weights)


def _pair_body(x_ref, o_ref, mine, theirs, send_sem, recv_sem, local_sem):
    r = lax.axis_index("dp")
    parity = lax.rem(r, 2)
    pair = r + 1 - 2 * parity
    slots, _, width = mine.shape
    barrier = pltpu.get_barrier_semaphore()
    pl.semaphore_signal(barrier, inc=1, device_id={"dp": pair}, device_id_type=MESH_ID)
    pl.semaphore_wait(barrier, 1)
    sent = []
    kept = []
    for i in range(slots):
        give = pl.ds(pl.multiple_of((2 * i + 1 - parity) * width, width), width)
        keep = pl.ds(pl.multiple_of((2 * i + parity) * width, width), width)
        copy = pltpu.make_async_remote_copy(
            src_ref=x_ref.at[:, give], dst_ref=theirs.at[i], send_sem=send_sem.at[i],
            recv_sem=recv_sem.at[i], device_id={"dp": pair}, device_id_type=MESH_ID,
        )
        copy.start()
        sent.append(copy)
        own = pltpu.make_async_copy(x_ref.at[:, keep], mine.at[i], local_sem.at[i])
        own.start()
        kept.append(own)
    for copy in sent:
        copy.wait()
    for copy in kept:
        copy.wait()
    o_ref[...] = (mine[...].astype(jnp.float32) + theirs[...].astype(jnp.float32)).astype(o_ref.dtype)


def pair_sum(x, width):
    rows, cols = x.shape
    slots = cols // width // 2
    shape = (slots, rows, width)
    return pl.pallas_call(
        _pair_body,
        out_shape=jax.ShapeDtypeStruct(shape, x.dtype),
        in_specs=[pl.BlockSpec(memory_space=pl.ANY)],
        out_specs=pl.BlockSpec(memory_space=pltpu.VMEM),
        scratch_shapes=[
            pltpu.VMEM(shape, x.dtype),
            pltpu.VMEM(shape, x.dtype),
            pltpu.SemaphoreType.DMA((slots,)),
            pltpu.SemaphoreType.DMA((slots,)),
            pltpu.SemaphoreType.DMA((slots,)),
        ],
        compiler_params=pltpu.CompilerParams(collective_id=4, has_side_effects=True),
        cost_estimate=pl.CostEstimate(
            flops=x.size // 2, transcendentals=0, bytes_accessed=2 * x.size * x.dtype.itemsize
        ),
    )(x)


def _end_body(ring, x_ref, w_ref, o_ref, w_out, send_buf, recv_buf, cross_buf, cross_in,
              t_send, t_recv, c_sem, w_send, w_recv, local_sem):
    n_t = lax.axis_size("tensor")
    n_d = lax.axis_size("dp")
    t = lax.axis_index("tensor")
    r = lax.axis_index("dp")
    z = lax.rem(t, ring)
    t_base = t - z
    t_other = lax.rem(t + ring, n_t) - z
    t_far = lax.rem(t + ring, n_t)
    right = t_base + lax.rem(z + 1, ring)
    left = t_base + lax.rem(z + ring - 1, ring)
    parity = lax.rem(r, 2)
    n_w = n_d // 2
    me_w = r // 2
    barrier = pltpu.get_barrier_semaphore()
    for device in ({"tensor": t_far}, {"tensor": right}, {"tensor": left}):
        pl.semaphore_signal(barrier, inc=1, device_id=device, device_id_type=MESH_ID)
    for j in range(1, n_w):
        peer = 2 * lax.rem(me_w + j, n_w) + parity
        pl.semaphore_signal(barrier, inc=1, device_id={"dp": peer}, device_id_type=MESH_ID)
    pl.semaphore_wait(barrier, 3 + n_w - 1)

    def remote(src, dst, send, recv, device):
        copy = pltpu.make_async_remote_copy(
            src_ref=src, dst_ref=dst, send_sem=send, recv_sem=recv,
            device_id=device, device_id_type=MESH_ID,
        )
        copy.start()
        return copy

    waits = []
    for j in range(1, n_w):
        peer = lax.rem(me_w + j, n_w)
        waits.append(remote(w_ref.at[peer], w_out.at[me_w], w_send.at[j], w_recv.at[j],
                            {"dp": 2 * peer + parity}))
    own_w = pltpu.make_async_copy(w_ref.at[me_w], w_out.at[me_w], local_sem.at[0])
    own_w.start()
    steps = (ring // 2, ring - 1 - ring // 2)
    moving = [None, None]
    for s in range(max(steps)):
        for d, (target, sign) in enumerate(((right, -1), (left, 1))):
            if s >= steps[d]:
                continue
            q = lax.rem(z - sign * (steps[d] - s) + 2 * ring, ring)
            sent = []
            for h, start in enumerate((t_base, t_other)):
                slot = start + q
                if s == 0:
                    src = x_ref.at[slot]
                else:
                    moving[d][h].wait_recv()
                    send_buf[d, s, h] = (
                        recv_buf[d, s - 1, h].astype(jnp.float32) + x_ref[slot].astype(jnp.float32)
                    ).astype(send_buf.dtype)
                    src = send_buf.at[d, s, h]
                sent.append(remote(src, recv_buf.at[d, s, h], t_send.at[d, s, h],
                                   t_recv.at[d, s, h], {"tensor": target}))
            waits.extend(sent)
            moving[d] = sent
    for d in range(2):
        for copy in moving[d]:
            copy.wait_recv()
    plus, minus = steps[0] - 1, steps[1] - 1
    cross_buf[...] = (
        x_ref[t_far].astype(jnp.float32)
        + recv_buf[0, plus, 1].astype(jnp.float32)
        + recv_buf[1, minus, 1].astype(jnp.float32)
    ).astype(cross_buf.dtype)
    crossed = remote(cross_buf, cross_in, c_sem.at[0], c_sem.at[1], {"tensor": t_far})
    crossed.wait()
    o_ref[...] = (
        x_ref[t].astype(jnp.float32)
        + recv_buf[0, plus, 0].astype(jnp.float32)
        + recv_buf[1, minus, 0].astype(jnp.float32)
        + cross_in[...].astype(jnp.float32)
    )
    for copy in waits:
        copy.wait_send()
    for j in range(1, n_w):
        pltpu.make_async_copy(w_out.at[0], w_out.at[0], w_recv.at[j]).wait()
    own_w.wait()


def end_exchange(partial, paired, ring):
    n_t, rows, cols = partial.shape
    n_w = paired.shape[0]
    piece = (rows, cols)
    moved = 2 * (partial.size * partial.dtype.itemsize + paired.size * paired.dtype.itemsize)
    return pl.pallas_call(
        functools.partial(_end_body, ring),
        out_shape=[
            jax.ShapeDtypeStruct(piece, jnp.float32),
            jax.ShapeDtypeStruct(paired.shape, paired.dtype),
        ],
        in_specs=[pl.BlockSpec(memory_space=pltpu.VMEM), pl.BlockSpec(memory_space=pl.ANY)],
        out_specs=[pl.BlockSpec(memory_space=pltpu.VMEM), pl.BlockSpec(memory_space=pl.ANY)],
        scratch_shapes=[
            pltpu.VMEM((2, ring // 2, 2) + piece, partial.dtype),
            pltpu.VMEM((2, ring // 2, 2) + piece, partial.dtype),
            pltpu.VMEM(piece, partial.dtype),
            pltpu.VMEM(piece, partial.dtype),
            pltpu.SemaphoreType.DMA((2, ring // 2, 2)),
            pltpu.SemaphoreType.DMA((2, ring // 2, 2)),
            pltpu.SemaphoreType.DMA((2,)),
            pltpu.SemaphoreType.DMA((n_w,)),
            pltpu.SemaphoreType.DMA((n_w,)),
            pltpu.SemaphoreType.DMA((1,)),
        ],
        compiler_params=pltpu.CompilerParams(collective_id=1, has_side_effects=True),
        cost_estimate=pl.CostEstimate(flops=4 * partial.size, transcendentals=0, bytes_accessed=moved),
    )(partial, paired)


def local(tokens, norm_gain, query_weight, kv_weight, out_weight, grad_out, doc_lengths):
    tensor_size = lax.axis_size("tensor")
    data_size = lax.axis_size("dp")
    tensor_index = lax.axis_index("tensor")
    sharers = tensor_size // KVH
    levels = sharers.bit_length() - 1
    contract_last = (((1,), (1,)), ((), ()))
    query_width = query_weight.shape[1]
    kv_width = kv_weight.shape[1]
    values32 = tokens.astype(jnp.float32)
    root_mean = jnp.sqrt(jnp.mean(values32 * values32, axis=-1) + epsilon)
    unit = values32 / root_mean[:, None]
    gain32 = norm_gain.astype(jnp.float32)
    normed_local = (unit * gain32).astype(jnp.bfloat16)
    rows = tokens.shape[0]
    pieces = jnp.stack([normed_local, grad_out])
    weights_local = jnp.concatenate([query_weight, kv_weight, out_weight.T], axis=1)
    tens_parts, weight_parts = gather_start(pieces, weights_local, RING)
    normed = tens_parts[:, 0].reshape(tensor_size * rows, -1)
    grad_full = tens_parts[:, 1].reshape(tensor_size * rows, -1)
    seq_length = normed.shape[0]
    weights_full = weight_parts.reshape(-1, weights_local.shape[1])
    query_full = weights_full[:, :query_width]
    kv_local = weights_full[:, query_width : query_width + kv_width]
    out_full_t = weights_full[:, query_width + kv_width :]
    queries = jnp.dot(normed, query_full, preferred_element_type=jnp.float32).astype(jnp.bfloat16)
    keyvals = jnp.dot(normed, kv_local, preferred_element_type=jnp.float32).astype(jnp.bfloat16)
    for bit_index in range(levels):
        partner = partner_2(keyvals, "tensor", bit_index)
        joined_upper_half = tensor_index >> bit_index & 1 == 1
        keyvals = jnp.concatenate(
            [
                jnp.where(joined_upper_half, partner, keyvals),
                jnp.where(joined_upper_half, keyvals, partner),
            ],
            axis=1,
        )
    key_rows = keyvals[:, :HD]
    value_rows = keyvals[:, HD:]
    out_grad = jnp.dot(grad_full, out_full_t, preferred_element_type=jnp.float32).astype(
        jnp.bfloat16
    )
    local_heads = queries.shape[1] // HD
    query_heads = queries.reshape(seq_length, local_heads, HD)
    out_heads = out_grad.reshape(seq_length, local_heads, HD)
    allowed = document_mask(doc_lengths[0], seq_length)
    scores = jnp.einsum(
        "qhd,td->hqt", query_heads, key_rows, preferred_element_type=jnp.float32
    ) / math.sqrt(HD)
    scores = jnp.where(allowed[None, :, :], scores, -1e30)
    peak = jnp.max(scores, axis=-1, keepdims=True)
    expo = jnp.exp(scores - peak)
    probs = expo / jnp.sum(expo, axis=-1, keepdims=True)
    probs_low = probs.astype(jnp.bfloat16)
    prob_grad = jnp.einsum("qhd,td->hqt", out_heads, value_rows, preferred_element_type=jnp.float32)
    inner = jnp.sum(probs * prob_grad, axis=-1, keepdims=True)
    score_grad = (probs * (prob_grad - inner) / math.sqrt(HD)).astype(jnp.bfloat16)
    query_grad = jnp.einsum("hqt,td->qhd", score_grad, key_rows, preferred_element_type=jnp.float32)
    query_grad = query_grad.astype(jnp.bfloat16).reshape(seq_length, local_heads * HD)
    key_part = jnp.einsum(
        "hqt,qhd->td", score_grad, query_heads, preferred_element_type=jnp.float32
    )
    value_part = jnp.einsum("hqt,qhd->td", probs_low, out_heads, preferred_element_type=jnp.float32)
    kv_partial = jnp.concatenate([key_part, value_part], axis=1)
    for bit_index in reversed(range(levels)):
        half_cols = kv_partial.shape[1] // 2
        upper_half = tensor_index >> bit_index & 1 == 1
        lower_cols = kv_partial[:, :half_cols]
        higher_cols = kv_partial[:, half_cols:]
        kept = jnp.where(upper_half, higher_cols, lower_cols)
        handed = jnp.where(upper_half, lower_cols, higher_cols)
        kv_partial = kept + partner_2(handed.astype(jnp.bfloat16), "tensor", bit_index).astype(
            handed.dtype
        )
    kv_grad = kv_partial.astype(jnp.bfloat16)
    combined = jnp.concatenate([query_grad, kv_grad], axis=1)
    partial = lax.dot_general(
        combined, weights_full[:, : query_width + kv_width], contract_last,
        preferred_element_type=jnp.float32,
    ).astype(jnp.bfloat16).reshape(tensor_size, rows, -1)
    weight_partial = lax.dot_general(
        combined, normed, (((0,), (0,)), ((), ())), preferred_element_type=jnp.float32
    ).astype(jnp.bfloat16)
    block = weight_partial.shape[1] // data_size
    paired = pair_sum(weight_partial, block)
    normed_grad, weight_arrived = end_exchange(partial, paired, RING)
    scaled = normed_grad * gain32
    correction = unit * jnp.mean(scaled * unit, axis=-1, keepdims=True)
    input_grad = (grad_out.astype(jnp.float32) + (scaled - correction) / root_mean[:, None]).astype(
        jnp.bfloat16
    )
    weight_grads = (jnp.sum(weight_arrived.astype(jnp.float32), axis=0) / data_size).T
    return (input_grad, weight_grads[:, :query_width], weight_grads[:, query_width:])


def solution(mesh):
    placed = (
        P(("dp", "tensor"), None),
        P(),
        P("dp", "tensor"),
        P("dp", "tensor"),
        P("tensor", "dp"),
        P(("dp", "tensor"), None),
        P("dp", None),
    )
    return jax.shard_map(
        local,
        mesh=mesh,
        in_specs=placed,
        out_specs=(P(("dp", "tensor"), None), P("dp", "tensor"), P("dp", "tensor")),
        check_vma=False,
    )
```

```python
import functools
import math

import jax
import jax.numpy as jnp
from jax import lax
from jax.experimental import pallas as pl
from jax.experimental.pallas import tpu as pltpu
from jax.sharding import PartitionSpec as P

KVH = 4
HD = 128
MESH_ID = pl.DeviceIdType.MESH
RING = 8


epsilon = 1e-05


def partner_2(value, axis, bit):
    mask = 2**bit
    pairs = [(source, source ^ mask) for source in range(lax.axis_size(axis))]
    return lax.ppermute(value, axis, pairs)


def document_mask(lengths, length_total):
    ends = jnp.cumsum(lengths)
    positions = jnp.arange(length_total, dtype=jnp.int32)
    labels = jnp.sum((ends[None, :] <= positions[:, None]).astype(jnp.int32), axis=1)
    return (labels[:, None] == labels[None, :]) & (positions[None, :] <= positions[:, None])


def _push_body(plan, *refs):
    count = len(plan)
    ins = refs[:count]
    outs = refs[count : 2 * count]
    send_sems = refs[2 * count : 3 * count]
    recv_sems = refs[3 * count : 4 * count]
    local_sem = refs[4 * count]
    barrier = pltpu.get_barrier_semaphore()
    mine = []
    expected = 0
    places = []
    for axis, n, _, stride in plan:
        index = lax.axis_index(axis)
        me = lax.rem(index // stride, n)
        offset = index - me * stride
        mine.append(me)
        places.append(functools.partial(lambda o, st, p: o + p * st, offset, stride))
        for j in range(1, n):
            pl.semaphore_signal(
                barrier,
                inc=1,
                device_id={axis: places[-1](lax.rem(me + j, n))},
                device_id_type=MESH_ID,
            )
        expected += n - 1
    pl.semaphore_wait(barrier, expected)
    local = []
    for g, (axis, n, scatter, _) in enumerate(plan):
        me = mine[g]
        src = ins[g].at[me] if scatter else ins[g]
        copy = pltpu.make_async_copy(src, outs[g].at[me], local_sem.at[g])
        copy.start()
        local.append(copy)
    remote = []
    for j in range(1, max(n for _, n, _, _ in plan)):
        for g, (axis, n, scatter, _) in enumerate(plan):
            if j >= n:
                continue
            me = mine[g]
            peer = lax.rem(me + j, n)
            copy = pltpu.make_async_remote_copy(
                src_ref=ins[g].at[peer] if scatter else ins[g],
                dst_ref=outs[g].at[me],
                send_sem=send_sems[g].at[j],
                recv_sem=recv_sems[g].at[j],
                device_id={axis: places[g](peer)},
                device_id_type=MESH_ID,
            )
            copy.start()
            remote.append(copy)
    for copy in remote:
        copy.wait()
    for copy in local:
        copy.wait()


def push_exchange(groups, cid):
    groups = [g if len(g) == 5 else g + (1,) for g in groups]
    plan = tuple((axis, n, scatter, stride) for axis, n, _, scatter, stride in groups)
    arrays = [array for _, _, array, _, _ in groups]
    out_shape = []
    moved = 0
    for _, n, array, scatter, _ in groups:
        shape = array.shape if scatter else (n,) + array.shape
        out_shape.append(jax.ShapeDtypeStruct(shape, array.dtype))
        moved += 2 * math.prod(shape) * array.dtype.itemsize
    count = len(groups)
    return pl.pallas_call(
        functools.partial(_push_body, plan),
        out_shape=out_shape,
        in_specs=[pl.BlockSpec(memory_space=pl.ANY)] * count,
        out_specs=[pl.BlockSpec(memory_space=pl.ANY)] * count,
        scratch_shapes=[pltpu.SemaphoreType.DMA((n,)) for _, n, _, _, _ in groups]
        + [pltpu.SemaphoreType.DMA((n,)) for _, n, _, _, _ in groups]
        + [pltpu.SemaphoreType.DMA((count,))],
        compiler_params=pltpu.CompilerParams(collective_id=cid, has_side_effects=True),
        cost_estimate=pl.CostEstimate(flops=0, transcendentals=0, bytes_accessed=moved),
    )(*arrays)


def _gather_start_body(ring, pieces_ref, weights_ref, tens_out, dp_out, t_send, t_recv, t_cross,
                       d_send, d_recv, d_cross, pair_send, pair_recv, local_sem):
    n_t = lax.axis_size("tensor")
    n_d = lax.axis_size("dp")
    t = lax.axis_index("tensor")
    r = lax.axis_index("dp")
    z = lax.rem(t, ring)
    t_base = t - z
    t_other = lax.rem(t + ring, n_t) - z
    t_far = lax.rem(t + ring, n_t)
    d_ring = n_d // 4
    core = lax.rem(r, 2)
    y = lax.rem(r // 2, d_ring)
    x = r // (2 * d_ring)
    d_base = x * 2 * d_ring + core
    d_other = (1 - x) * 2 * d_ring + core
    d_far = d_other + 2 * y
    pair = r + 1 - 2 * core
    rings = (
        ("tensor", tens_out, pieces_ref, z, (t_base, t_other), 1, ring, t_send, t_recv),
        ("dp", dp_out, weights_ref, y, (d_base, d_other), 2, d_ring, d_send, d_recv),
    )

    def neighbours(pos, bases, stride, n):
        return (bases[0] + lax.rem(pos + 1, n) * stride, bases[0] + lax.rem(pos + n - 1, n) * stride)

    barrier = pltpu.get_barrier_semaphore()
    targets = [{"tensor": t_far}, {"dp": pair}, {"dp": d_far}]
    for axis, _, _, pos, bases, stride, n, _, _ in rings:
        targets.extend({axis: v} for v in neighbours(pos, bases, stride, n))
    for device in targets:
        pl.semaphore_signal(barrier, inc=1, device_id=device, device_id_type=MESH_ID)
    pl.semaphore_wait(barrier, len(targets))

    def remote(src, dst, send, recv, device):
        copy = pltpu.make_async_remote_copy(
            src_ref=src, dst_ref=dst, send_sem=send, recv_sem=recv,
            device_id=device, device_id_type=MESH_ID,
        )
        copy.start()
        return copy

    waits = []
    forwarded = [0]

    def forward(src, slot):
        f = forwarded[0]
        waits.append(remote(src, dp_out.at[slot], pair_send.at[f], pair_recv.at[f], {"dp": pair}))
        forwarded[0] = f + 1

    forward(weights_ref, r)
    t_crossed = remote(pieces_ref, tens_out.at[t], t_cross.at[0], t_cross.at[1], {"tensor": t_far})
    d_crossed = remote(weights_ref, dp_out.at[r], d_cross.at[0], d_cross.at[1], {"dp": d_far})
    own_t = pltpu.make_async_copy(pieces_ref, tens_out.at[t], local_sem.at[0])
    own_t.start()
    own_d = pltpu.make_async_copy(weights_ref, dp_out.at[r], local_sem.at[1])
    own_d.start()
    t_crossed.wait()
    d_crossed.wait()
    forward(dp_out.at[d_far], d_far)
    moving = {}
    for s in range(max(ring, d_ring) // 2):
        for k, (axis, out, own, pos, bases, stride, n, send, recv) in enumerate(rings):
            right, left = neighbours(pos, bases, stride, n)
            steps = (n // 2, n - 1 - n // 2)
            for d, (target, sign) in enumerate(((right, -1), (left, 1))):
                if s >= steps[d]:
                    continue
                origin = lax.rem(pos + sign * s + n, n)
                if s > 0:
                    for copy in moving[k, d]:
                        copy.wait_recv()
                    if k == 1:
                        for start in bases:
                            slot = start + origin * stride
                            forward(out.at[slot], slot)
                sent = []
                for h, start in enumerate(bases):
                    slot = start + origin * stride
                    src = own if (s == 0 and h == 0) else out.at[slot]
                    sent.append(remote(src, out.at[slot], send.at[d, s, h], recv.at[d, s, h],
                                       {axis: target}))
                waits.extend(sent)
                moving[k, d] = sent
    for k, (axis, out, own, pos, bases, stride, n, send, recv) in enumerate(rings):
        steps = (n // 2, n - 1 - n // 2)
        for d, sign in enumerate((-1, 1)):
            for copy in moving[k, d]:
                copy.wait_recv()
            if k == 1:
                origin = lax.rem(pos + sign * steps[d] + n, n)
                for start in bases:
                    slot = start + origin * stride
                    forward(out.at[slot], slot)
    for copy in waits:
        copy.wait_send()
    for f in range(forwarded[0]):
        pltpu.make_async_copy(dp_out.at[0], dp_out.at[0], pair_recv.at[f]).wait()
    own_t.wait()
    own_d.wait()


def gather_start(pieces, weights, ring):
    n_t = lax.axis_size("tensor")
    n_d = lax.axis_size("dp")
    d_ring = n_d // 4
    moved = 2 * (n_t * pieces.size * pieces.dtype.itemsize + n_d * weights.size * weights.dtype.itemsize)
    return pl.pallas_call(
        functools.partial(_gather_start_body, ring),
        out_shape=[
            jax.ShapeDtypeStruct((n_t,) + pieces.shape, pieces.dtype),
            jax.ShapeDtypeStruct((n_d,) + weights.shape, weights.dtype),
        ],
        in_specs=[pl.BlockSpec(memory_space=pl.ANY)] * 2,
        out_specs=[pl.BlockSpec(memory_space=pl.ANY)] * 2,
        scratch_shapes=[
            pltpu.SemaphoreType.DMA((2, ring // 2, 2)),
            pltpu.SemaphoreType.DMA((2, ring // 2, 2)),
            pltpu.SemaphoreType.DMA((2,)),
            pltpu.SemaphoreType.DMA((2, d_ring // 2, 2)),
            pltpu.SemaphoreType.DMA((2, d_ring // 2, 2)),
            pltpu.SemaphoreType.DMA((2,)),
            pltpu.SemaphoreType.DMA((2 * d_ring,)),
            pltpu.SemaphoreType.DMA((2 * d_ring,)),
            pltpu.SemaphoreType.DMA((2,)),
        ],
        compiler_params=pltpu.CompilerParams(collective_id=0, has_side_effects=True),
        cost_estimate=pl.CostEstimate(flops=0, transcendentals=0, bytes_accessed=moved),
    )(pieces, weights)


def _pair_body(x_ref, o_ref, mine, theirs, send_sem, recv_sem, local_sem):
    r = lax.axis_index("dp")
    parity = lax.rem(r, 2)
    pair = r + 1 - 2 * parity
    slots, _, width = mine.shape
    barrier = pltpu.get_barrier_semaphore()
    pl.semaphore_signal(barrier, inc=1, device_id={"dp": pair}, device_id_type=MESH_ID)
    pl.semaphore_wait(barrier, 1)
    sent = []
    kept = []
    for i in range(slots):
        give = pl.ds(pl.multiple_of((2 * i + 1 - parity) * width, width), width)
        keep = pl.ds(pl.multiple_of((2 * i + parity) * width, width), width)
        copy = pltpu.make_async_remote_copy(
            src_ref=x_ref.at[:, give], dst_ref=theirs.at[i], send_sem=send_sem.at[i],
            recv_sem=recv_sem.at[i], device_id={"dp": pair}, device_id_type=MESH_ID,
        )
        copy.start()
        sent.append(copy)
        own = pltpu.make_async_copy(x_ref.at[:, keep], mine.at[i], local_sem.at[i])
        own.start()
        kept.append(own)
    for copy in sent:
        copy.wait()
    for copy in kept:
        copy.wait()
    o_ref[...] = (mine[...].astype(jnp.float32) + theirs[...].astype(jnp.float32)).astype(o_ref.dtype)


def pair_sum(x, width):
    rows, cols = x.shape
    slots = cols // width // 2
    shape = (slots, rows, width)
    return pl.pallas_call(
        _pair_body,
        out_shape=jax.ShapeDtypeStruct(shape, x.dtype),
        in_specs=[pl.BlockSpec(memory_space=pl.ANY)],
        out_specs=pl.BlockSpec(memory_space=pltpu.VMEM),
        scratch_shapes=[
            pltpu.VMEM(shape, x.dtype),
            pltpu.VMEM(shape, x.dtype),
            pltpu.SemaphoreType.DMA((slots,)),
            pltpu.SemaphoreType.DMA((slots,)),
            pltpu.SemaphoreType.DMA((slots,)),
        ],
        compiler_params=pltpu.CompilerParams(collective_id=4, has_side_effects=True),
        cost_estimate=pl.CostEstimate(
            flops=x.size // 2, transcendentals=0, bytes_accessed=2 * x.size * x.dtype.itemsize
        ),
    )(x)


def _end_body(ring, x_ref, g_ref, o_ref, w_out, send_buf, recv_buf, cross_buf, cross_in,
              mine, theirs, w_ref, t_send, t_recv, c_sem, w_send, w_recv, p_send, p_recv, p_local,
              local_sem):
    n_t = lax.axis_size("tensor")
    n_d = lax.axis_size("dp")
    t = lax.axis_index("tensor")
    r = lax.axis_index("dp")
    z = lax.rem(t, ring)
    t_base = t - z
    t_other = lax.rem(t + ring, n_t) - z
    t_far = lax.rem(t + ring, n_t)
    right = t_base + lax.rem(z + 1, ring)
    left = t_base + lax.rem(z + ring - 1, ring)
    parity = lax.rem(r, 2)
    pair = r + 1 - 2 * parity
    n_w = n_d // 2
    me_w = r // 2
    width = mine.shape[2]
    barrier = pltpu.get_barrier_semaphore()
    for device in ({"tensor": t_far}, {"tensor": right}, {"tensor": left}, {"dp": pair}):
        pl.semaphore_signal(barrier, inc=1, device_id=device, device_id_type=MESH_ID)
    for j in range(1, n_w):
        peer = 2 * lax.rem(me_w + j, n_w) + parity
        pl.semaphore_signal(barrier, inc=1, device_id={"dp": peer}, device_id_type=MESH_ID)
    pl.semaphore_wait(barrier, 4 + n_w - 1)

    def remote(src, dst, send, recv, device):
        copy = pltpu.make_async_remote_copy(
            src_ref=src, dst_ref=dst, send_sem=send, recv_sem=recv,
            device_id=device, device_id_type=MESH_ID,
        )
        copy.start()
        return copy

    waits = []
    swapped = []
    kept = []
    for i in range(n_w):
        give = pl.ds(pl.multiple_of((2 * i + 1 - parity) * width, width), width)
        keep = pl.ds(pl.multiple_of((2 * i + parity) * width, width), width)
        swapped.append(remote(g_ref.at[:, give], theirs.at[i], p_send.at[i], p_recv.at[i],
                              {"dp": pair}))
        own = pltpu.make_async_copy(g_ref.at[:, keep], mine.at[i], p_local.at[i])
        own.start()
        kept.append(own)
    steps = (ring // 2, ring - 1 - ring // 2)
    moving = [None, None]
    own_w = None
    for s in range(max(steps)):
        if s == 1:
            for copy in swapped:
                copy.wait()
            for copy in kept:
                copy.wait()
            w_ref[...] = (
                mine[...].astype(jnp.float32) + theirs[...].astype(jnp.float32)
            ).astype(w_ref.dtype)
            for j in range(1, n_w):
                peer = lax.rem(me_w + j, n_w)
                waits.append(remote(w_ref.at[peer], w_out.at[me_w], w_send.at[j], w_recv.at[j],
                                    {"dp": 2 * peer + parity}))
            own_w = pltpu.make_async_copy(w_ref.at[me_w], w_out.at[me_w], local_sem.at[0])
            own_w.start()
        for d, (target, sign) in enumerate(((right, -1), (left, 1))):
            if s >= steps[d]:
                continue
            q = lax.rem(z - sign * (steps[d] - s) + 2 * ring, ring)
            sent = []
            for h, start in enumerate((t_base, t_other)):
                slot = start + q
                if s == 0:
                    src = x_ref.at[slot]
                else:
                    moving[d][h].wait_recv()
                    send_buf[d, s, h] = (
                        recv_buf[d, s - 1, h].astype(jnp.float32) + x_ref[slot].astype(jnp.float32)
                    ).astype(send_buf.dtype)
                    src = send_buf.at[d, s, h]
                sent.append(remote(src, recv_buf.at[d, s, h], t_send.at[d, s, h],
                                   t_recv.at[d, s, h], {"tensor": target}))
            waits.extend(sent)
            moving[d] = sent
    for d in range(2):
        for copy in moving[d]:
            copy.wait_recv()
    plus, minus = steps[0] - 1, steps[1] - 1
    cross_buf[...] = (
        x_ref[t_far].astype(jnp.float32)
        + recv_buf[0, plus, 1].astype(jnp.float32)
        + recv_buf[1, minus, 1].astype(jnp.float32)
    ).astype(cross_buf.dtype)
    crossed = remote(cross_buf, cross_in, c_sem.at[0], c_sem.at[1], {"tensor": t_far})
    crossed.wait()
    o_ref[...] = (
        x_ref[t].astype(jnp.float32)
        + recv_buf[0, plus, 0].astype(jnp.float32)
        + recv_buf[1, minus, 0].astype(jnp.float32)
        + cross_in[...].astype(jnp.float32)
    )
    for copy in waits:
        copy.wait_send()
    for j in range(1, n_w):
        pltpu.make_async_copy(w_out.at[0], w_out.at[0], w_recv.at[j]).wait()
    own_w.wait()


def end_exchange(partial, g, ring):
    n_t, rows, cols = partial.shape
    n_w = lax.axis_size("dp") // 2
    g_rows, g_cols = g.shape
    width = g_cols // (2 * n_w)
    slots = (n_w, g_rows, width)
    piece = (rows, cols)
    moved = 2 * (partial.size * partial.dtype.itemsize + g.size * g.dtype.itemsize)
    return pl.pallas_call(
        functools.partial(_end_body, ring),
        out_shape=[
            jax.ShapeDtypeStruct(piece, jnp.float32),
            jax.ShapeDtypeStruct(slots, g.dtype),
        ],
        in_specs=[pl.BlockSpec(memory_space=pltpu.VMEM), pl.BlockSpec(memory_space=pl.ANY)],
        out_specs=[pl.BlockSpec(memory_space=pltpu.VMEM), pl.BlockSpec(memory_space=pl.ANY)],
        scratch_shapes=[
            pltpu.VMEM((2, ring // 2, 2) + piece, partial.dtype),
            pltpu.VMEM((2, ring // 2, 2) + piece, partial.dtype),
            pltpu.VMEM(piece, partial.dtype),
            pltpu.VMEM(piece, partial.dtype),
            pltpu.VMEM(slots, g.dtype),
            pltpu.VMEM(slots, g.dtype),
            pltpu.VMEM(slots, g.dtype),
            pltpu.SemaphoreType.DMA((2, ring // 2, 2)),
            pltpu.SemaphoreType.DMA((2, ring // 2, 2)),
            pltpu.SemaphoreType.DMA((2,)),
            pltpu.SemaphoreType.DMA((n_w,)),
            pltpu.SemaphoreType.DMA((n_w,)),
            pltpu.SemaphoreType.DMA((n_w,)),
            pltpu.SemaphoreType.DMA((n_w,)),
            pltpu.SemaphoreType.DMA((n_w,)),
            pltpu.SemaphoreType.DMA((1,)),
        ],
        compiler_params=pltpu.CompilerParams(collective_id=1, has_side_effects=True),
        cost_estimate=pl.CostEstimate(flops=4 * partial.size, transcendentals=0, bytes_accessed=moved),
    )(partial, g)


def local(tokens, norm_gain, query_weight, kv_weight, out_weight, grad_out, doc_lengths):
    tensor_size = lax.axis_size("tensor")
    data_size = lax.axis_size("dp")
    tensor_index = lax.axis_index("tensor")
    sharers = tensor_size // KVH
    levels = sharers.bit_length() - 1
    contract_last = (((1,), (1,)), ((), ()))
    query_width = query_weight.shape[1]
    kv_width = kv_weight.shape[1]
    values32 = tokens.astype(jnp.float32)
    root_mean = jnp.sqrt(jnp.mean(values32 * values32, axis=-1) + epsilon)
    unit = values32 / root_mean[:, None]
    gain32 = norm_gain.astype(jnp.float32)
    normed_local = (unit * gain32).astype(jnp.bfloat16)
    rows = tokens.shape[0]
    pieces = jnp.stack([normed_local, grad_out])
    weights_local = jnp.concatenate([query_weight, kv_weight, out_weight.T], axis=1)
    tens_parts, weight_parts = gather_start(pieces, weights_local, RING)
    normed = tens_parts[:, 0].reshape(tensor_size * rows, -1)
    grad_full = tens_parts[:, 1].reshape(tensor_size * rows, -1)
    seq_length = normed.shape[0]
    weights_full = weight_parts.reshape(-1, weights_local.shape[1])
    query_full = weights_full[:, :query_width]
    kv_local = weights_full[:, query_width : query_width + kv_width]
    out_full_t = weights_full[:, query_width + kv_width :]
    queries = jnp.dot(normed, query_full, preferred_element_type=jnp.float32).astype(jnp.bfloat16)
    keyvals = jnp.dot(normed, kv_local, preferred_element_type=jnp.float32).astype(jnp.bfloat16)
    for bit_index in range(levels):
        partner = partner_2(keyvals, "tensor", bit_index)
        joined_upper_half = tensor_index >> bit_index & 1 == 1
        keyvals = jnp.concatenate(
            [
                jnp.where(joined_upper_half, partner, keyvals),
                jnp.where(joined_upper_half, keyvals, partner),
            ],
            axis=1,
        )
    key_rows = keyvals[:, :HD]
    value_rows = keyvals[:, HD:]
    out_grad = jnp.dot(grad_full, out_full_t, preferred_element_type=jnp.float32).astype(
        jnp.bfloat16
    )
    local_heads = queries.shape[1] // HD
    query_heads = queries.reshape(seq_length, local_heads, HD)
    out_heads = out_grad.reshape(seq_length, local_heads, HD)
    allowed = document_mask(doc_lengths[0], seq_length)
    scores = jnp.einsum(
        "qhd,td->hqt", query_heads, key_rows, preferred_element_type=jnp.float32
    ) / math.sqrt(HD)
    scores = jnp.where(allowed[None, :, :], scores, -1e30)
    peak = jnp.max(scores, axis=-1, keepdims=True)
    expo = jnp.exp(scores - peak)
    probs = expo / jnp.sum(expo, axis=-1, keepdims=True)
    probs_low = probs.astype(jnp.bfloat16)
    prob_grad = jnp.einsum("qhd,td->hqt", out_heads, value_rows, preferred_element_type=jnp.float32)
    inner = jnp.sum(probs * prob_grad, axis=-1, keepdims=True)
    score_grad = (probs * (prob_grad - inner) / math.sqrt(HD)).astype(jnp.bfloat16)
    query_grad = jnp.einsum("hqt,td->qhd", score_grad, key_rows, preferred_element_type=jnp.float32)
    query_grad = query_grad.astype(jnp.bfloat16).reshape(seq_length, local_heads * HD)
    key_part = jnp.einsum(
        "hqt,qhd->td", score_grad, query_heads, preferred_element_type=jnp.float32
    )
    value_part = jnp.einsum("hqt,qhd->td", probs_low, out_heads, preferred_element_type=jnp.float32)
    kv_partial = jnp.concatenate([key_part, value_part], axis=1)
    for bit_index in reversed(range(levels)):
        half_cols = kv_partial.shape[1] // 2
        upper_half = tensor_index >> bit_index & 1 == 1
        lower_cols = kv_partial[:, :half_cols]
        higher_cols = kv_partial[:, half_cols:]
        kept = jnp.where(upper_half, higher_cols, lower_cols)
        handed = jnp.where(upper_half, lower_cols, higher_cols)
        kv_partial = kept + partner_2(handed.astype(jnp.bfloat16), "tensor", bit_index).astype(
            handed.dtype
        )
    kv_grad = kv_partial.astype(jnp.bfloat16)
    from_query = lax.dot_general(
        query_grad, query_full, contract_last, preferred_element_type=jnp.float32
    )
    from_kv = lax.dot_general(kv_grad, kv_local, contract_last, preferred_element_type=jnp.float32)
    partial = (from_query + from_kv).astype(jnp.bfloat16).reshape(tensor_size, rows, -1)
    combined = jnp.concatenate([query_grad, kv_grad], axis=1)
    weight_partial = lax.dot_general(
        combined, normed, (((0,), (0,)), ((), ())), preferred_element_type=jnp.float32
    ).astype(jnp.bfloat16)
    block = weight_partial.shape[1] // data_size
    normed_grad, weight_arrived = end_exchange(partial, weight_partial, RING)
    scaled = normed_grad * gain32
    correction = unit * jnp.mean(scaled * unit, axis=-1, keepdims=True)
    input_grad = (grad_out.astype(jnp.float32) + (scaled - correction) / root_mean[:, None]).astype(
        jnp.bfloat16
    )
    weight_grads = (jnp.sum(weight_arrived.astype(jnp.float32), axis=0) / data_size).T
    return (input_grad, weight_grads[:, :query_width], weight_grads[:, query_width:])


def solution(mesh):
    placed = (
        P(("dp", "tensor"), None),
        P(),
        P("dp", "tensor"),
        P("dp", "tensor"),
        P("tensor", "dp"),
        P(("dp", "tensor"), None),
        P("dp", None),
    )
    return jax.shard_map(
        local,
        mesh=mesh,
        in_specs=placed,
        out_specs=(P(("dp", "tensor"), None), P("dp", "tensor"), P("dp", "tensor")),
        check_vma=False,
    )
```

```python
import functools
import math

import jax
import jax.numpy as jnp
from jax import lax
from jax.experimental import pallas as pl
from jax.experimental.pallas import tpu as pltpu
from jax.sharding import PartitionSpec as P

KVH = 4
HD = 128
MESH_ID = pl.DeviceIdType.MESH
RING = 8


epsilon = 1e-05


def partner_2(value, axis, bit):
    mask = 2**bit
    pairs = [(source, source ^ mask) for source in range(lax.axis_size(axis))]
    return lax.ppermute(value, axis, pairs)


def group_shift(size, group, k):
    return [(i, i - i % group + (i % group + k) % group) for i in range(size)]


def document_mask(lengths, length_total):
    ends = jnp.cumsum(lengths)
    positions = jnp.arange(length_total, dtype=jnp.int32)
    labels = jnp.sum((ends[None, :] <= positions[:, None]).astype(jnp.int32), axis=1)
    return (labels[:, None] == labels[None, :]) & (positions[None, :] <= positions[:, None])


def _push_body(plan, *refs):
    count = len(plan)
    ins = refs[:count]
    outs = refs[count : 2 * count]
    send_sems = refs[2 * count : 3 * count]
    recv_sems = refs[3 * count : 4 * count]
    local_sem = refs[4 * count]
    barrier = pltpu.get_barrier_semaphore()
    mine = []
    expected = 0
    places = []
    for axis, n, _, stride in plan:
        index = lax.axis_index(axis)
        me = lax.rem(index // stride, n)
        offset = index - me * stride
        mine.append(me)
        places.append(functools.partial(lambda o, st, p: o + p * st, offset, stride))
        for j in range(1, n):
            pl.semaphore_signal(
                barrier,
                inc=1,
                device_id={axis: places[-1](lax.rem(me + j, n))},
                device_id_type=MESH_ID,
            )
        expected += n - 1
    pl.semaphore_wait(barrier, expected)
    local = []
    for g, (axis, n, scatter, _) in enumerate(plan):
        me = mine[g]
        src = ins[g].at[me] if scatter else ins[g]
        copy = pltpu.make_async_copy(src, outs[g].at[me], local_sem.at[g])
        copy.start()
        local.append(copy)
    remote = []
    for j in range(1, max(n for _, n, _, _ in plan)):
        for g, (axis, n, scatter, _) in enumerate(plan):
            if j >= n:
                continue
            me = mine[g]
            peer = lax.rem(me + j, n)
            copy = pltpu.make_async_remote_copy(
                src_ref=ins[g].at[peer] if scatter else ins[g],
                dst_ref=outs[g].at[me],
                send_sem=send_sems[g].at[j],
                recv_sem=recv_sems[g].at[j],
                device_id={axis: places[g](peer)},
                device_id_type=MESH_ID,
            )
            copy.start()
            remote.append(copy)
    for copy in remote:
        copy.wait()
    for copy in local:
        copy.wait()


def push_exchange(groups, cid):
    groups = [g if len(g) == 5 else g + (1,) for g in groups]
    plan = tuple((axis, n, scatter, stride) for axis, n, _, scatter, stride in groups)
    arrays = [array for _, _, array, _, _ in groups]
    out_shape = []
    moved = 0
    for _, n, array, scatter, _ in groups:
        shape = array.shape if scatter else (n,) + array.shape
        out_shape.append(jax.ShapeDtypeStruct(shape, array.dtype))
        moved += 2 * math.prod(shape) * array.dtype.itemsize
    count = len(groups)
    return pl.pallas_call(
        functools.partial(_push_body, plan),
        out_shape=out_shape,
        in_specs=[pl.BlockSpec(memory_space=pl.ANY)] * count,
        out_specs=[pl.BlockSpec(memory_space=pl.ANY)] * count,
        scratch_shapes=[pltpu.SemaphoreType.DMA((n,)) for _, n, _, _, _ in groups]
        + [pltpu.SemaphoreType.DMA((n,)) for _, n, _, _, _ in groups]
        + [pltpu.SemaphoreType.DMA((count,))],
        compiler_params=pltpu.CompilerParams(collective_id=cid, has_side_effects=True),
        cost_estimate=pl.CostEstimate(flops=0, transcendentals=0, bytes_accessed=moved),
    )(*arrays)


def _gather_start_body(ring, pieces_ref, weights_ref, tens_out, dp_out, t_send, t_recv, t_cross,
                       d_send, d_recv, d_cross, pair_send, pair_recv, local_sem):
    n_t = lax.axis_size("tensor")
    n_d = lax.axis_size("dp")
    t = lax.axis_index("tensor")
    r = lax.axis_index("dp")
    z = lax.rem(t, ring)
    t_base = t - z
    t_other = lax.rem(t + ring, n_t) - z
    t_far = lax.rem(t + ring, n_t)
    d_ring = n_d // 4
    core = lax.rem(r, 2)
    y = lax.rem(r // 2, d_ring)
    x = r // (2 * d_ring)
    d_base = x * 2 * d_ring + core
    d_other = (1 - x) * 2 * d_ring + core
    d_far = d_other + 2 * y
    pair = r + 1 - 2 * core
    rings = (
        ("tensor", tens_out, pieces_ref, z, (t_base, t_other), 1, ring, t_send, t_recv),
        ("dp", dp_out, weights_ref, y, (d_base, d_other), 2, d_ring, d_send, d_recv),
    )

    def neighbours(pos, bases, stride, n):
        return (bases[0] + lax.rem(pos + 1, n) * stride, bases[0] + lax.rem(pos + n - 1, n) * stride)

    barrier = pltpu.get_barrier_semaphore()
    targets = [{"tensor": t_far}, {"dp": pair}, {"dp": d_far}]
    for axis, _, _, pos, bases, stride, n, _, _ in rings:
        targets.extend({axis: v} for v in neighbours(pos, bases, stride, n))
    for device in targets:
        pl.semaphore_signal(barrier, inc=1, device_id=device, device_id_type=MESH_ID)
    pl.semaphore_wait(barrier, len(targets))

    def remote(src, dst, send, recv, device):
        copy = pltpu.make_async_remote_copy(
            src_ref=src, dst_ref=dst, send_sem=send, recv_sem=recv,
            device_id=device, device_id_type=MESH_ID,
        )
        copy.start()
        return copy

    waits = []
    forwarded = [0]

    def forward(src, slot):
        f = forwarded[0]
        waits.append(remote(src, dp_out.at[slot], pair_send.at[f], pair_recv.at[f], {"dp": pair}))
        forwarded[0] = f + 1

    forward(weights_ref, r)
    t_crossed = remote(pieces_ref, tens_out.at[t], t_cross.at[0], t_cross.at[1], {"tensor": t_far})
    d_crossed = remote(weights_ref, dp_out.at[r], d_cross.at[0], d_cross.at[1], {"dp": d_far})
    own_t = pltpu.make_async_copy(pieces_ref, tens_out.at[t], local_sem.at[0])
    own_t.start()
    own_d = pltpu.make_async_copy(weights_ref, dp_out.at[r], local_sem.at[1])
    own_d.start()
    t_crossed.wait()
    d_crossed.wait()
    forward(dp_out.at[d_far], d_far)
    moving = {}
    for s in range(max(ring, d_ring) // 2):
        for k, (axis, out, own, pos, bases, stride, n, send, recv) in enumerate(rings):
            right, left = neighbours(pos, bases, stride, n)
            steps = (n // 2, n - 1 - n // 2)
            for d, (target, sign) in enumerate(((right, -1), (left, 1))):
                if s >= steps[d]:
                    continue
                origin = lax.rem(pos + sign * s + n, n)
                if s > 0:
                    for copy in moving[k, d]:
                        copy.wait_recv()
                    if k == 1:
                        for start in bases:
                            slot = start + origin * stride
                            forward(out.at[slot], slot)
                sent = []
                for h, start in enumerate(bases):
                    slot = start + origin * stride
                    src = own if (s == 0 and h == 0) else out.at[slot]
                    sent.append(remote(src, out.at[slot], send.at[d, s, h], recv.at[d, s, h],
                                       {axis: target}))
                waits.extend(sent)
                moving[k, d] = sent
    for k, (axis, out, own, pos, bases, stride, n, send, recv) in enumerate(rings):
        steps = (n // 2, n - 1 - n // 2)
        for d, sign in enumerate((-1, 1)):
            for copy in moving[k, d]:
                copy.wait_recv()
            if k == 1:
                origin = lax.rem(pos + sign * steps[d] + n, n)
                for start in bases:
                    slot = start + origin * stride
                    forward(out.at[slot], slot)
    for copy in waits:
        copy.wait_send()
    for f in range(forwarded[0]):
        pltpu.make_async_copy(dp_out.at[0], dp_out.at[0], pair_recv.at[f]).wait()
    own_t.wait()
    own_d.wait()


def gather_start(pieces, weights, ring):
    n_t = lax.axis_size("tensor")
    n_d = lax.axis_size("dp")
    d_ring = n_d // 4
    moved = 2 * (n_t * pieces.size * pieces.dtype.itemsize + n_d * weights.size * weights.dtype.itemsize)
    return pl.pallas_call(
        functools.partial(_gather_start_body, ring),
        out_shape=[
            jax.ShapeDtypeStruct((n_t,) + pieces.shape, pieces.dtype),
            jax.ShapeDtypeStruct((n_d,) + weights.shape, weights.dtype),
        ],
        in_specs=[pl.BlockSpec(memory_space=pl.ANY)] * 2,
        out_specs=[pl.BlockSpec(memory_space=pl.ANY)] * 2,
        scratch_shapes=[
            pltpu.SemaphoreType.DMA((2, ring // 2, 2)),
            pltpu.SemaphoreType.DMA((2, ring // 2, 2)),
            pltpu.SemaphoreType.DMA((2,)),
            pltpu.SemaphoreType.DMA((2, d_ring // 2, 2)),
            pltpu.SemaphoreType.DMA((2, d_ring // 2, 2)),
            pltpu.SemaphoreType.DMA((2,)),
            pltpu.SemaphoreType.DMA((2 * d_ring,)),
            pltpu.SemaphoreType.DMA((2 * d_ring,)),
            pltpu.SemaphoreType.DMA((2,)),
        ],
        compiler_params=pltpu.CompilerParams(collective_id=0, has_side_effects=True),
        cost_estimate=pl.CostEstimate(flops=0, transcendentals=0, bytes_accessed=moved),
    )(pieces, weights)


def _pair_body(x_ref, o_ref, mine, theirs, send_sem, recv_sem, local_sem):
    r = lax.axis_index("dp")
    parity = lax.rem(r, 2)
    pair = r + 1 - 2 * parity
    slots, _, width = mine.shape
    barrier = pltpu.get_barrier_semaphore()
    pl.semaphore_signal(barrier, inc=1, device_id={"dp": pair}, device_id_type=MESH_ID)
    pl.semaphore_wait(barrier, 1)
    sent = []
    kept = []
    for i in range(slots):
        give = pl.ds(pl.multiple_of((2 * i + 1 - parity) * width, width), width)
        keep = pl.ds(pl.multiple_of((2 * i + parity) * width, width), width)
        copy = pltpu.make_async_remote_copy(
            src_ref=x_ref.at[:, give], dst_ref=theirs.at[i], send_sem=send_sem.at[i],
            recv_sem=recv_sem.at[i], device_id={"dp": pair}, device_id_type=MESH_ID,
        )
        copy.start()
        sent.append(copy)
        own = pltpu.make_async_copy(x_ref.at[:, keep], mine.at[i], local_sem.at[i])
        own.start()
        kept.append(own)
    for copy in sent:
        copy.wait()
    for copy in kept:
        copy.wait()
    o_ref[...] = (mine[...].astype(jnp.float32) + theirs[...].astype(jnp.float32)).astype(o_ref.dtype)


def pair_sum(x, width):
    rows, cols = x.shape
    slots = cols // width // 2
    shape = (slots, rows, width)
    return pl.pallas_call(
        _pair_body,
        out_shape=jax.ShapeDtypeStruct(shape, x.dtype),
        in_specs=[pl.BlockSpec(memory_space=pl.ANY)],
        out_specs=pl.BlockSpec(memory_space=pltpu.VMEM),
        scratch_shapes=[
            pltpu.VMEM(shape, x.dtype),
            pltpu.VMEM(shape, x.dtype),
            pltpu.SemaphoreType.DMA((slots,)),
            pltpu.SemaphoreType.DMA((slots,)),
            pltpu.SemaphoreType.DMA((slots,)),
        ],
        compiler_params=pltpu.CompilerParams(collective_id=4, has_side_effects=True),
        cost_estimate=pl.CostEstimate(
            flops=x.size // 2, transcendentals=0, bytes_accessed=2 * x.size * x.dtype.itemsize
        ),
    )(x)


def _end_body(ring, x_ref, g_ref, o_ref, w_out, send_buf, recv_buf, cross_buf, cross_in,
              mine, theirs, w_ref, t_send, t_recv, c_sem, w_send, w_recv, p_send, p_recv, p_local,
              local_sem):
    n_t = lax.axis_size("tensor")
    n_d = lax.axis_size("dp")
    t = lax.axis_index("tensor")
    r = lax.axis_index("dp")
    z = lax.rem(t, ring)
    t_base = t - z
    t_other = lax.rem(t + ring, n_t) - z
    t_far = lax.rem(t + ring, n_t)
    right = t_base + lax.rem(z + 1, ring)
    left = t_base + lax.rem(z + ring - 1, ring)
    parity = lax.rem(r, 2)
    pair = r + 1 - 2 * parity
    n_w = n_d // 2
    me_w = r // 2
    width = mine.shape[2]
    barrier = pltpu.get_barrier_semaphore()
    for device in ({"tensor": t_far}, {"tensor": right}, {"tensor": left}, {"dp": pair}):
        pl.semaphore_signal(barrier, inc=1, device_id=device, device_id_type=MESH_ID)
    for j in range(1, n_w):
        peer = 2 * lax.rem(me_w + j, n_w) + parity
        pl.semaphore_signal(barrier, inc=1, device_id={"dp": peer}, device_id_type=MESH_ID)
    pl.semaphore_wait(barrier, 4 + n_w - 1)

    def remote(src, dst, send, recv, device):
        copy = pltpu.make_async_remote_copy(
            src_ref=src, dst_ref=dst, send_sem=send, recv_sem=recv,
            device_id=device, device_id_type=MESH_ID,
        )
        copy.start()
        return copy

    waits = []
    swapped = []
    kept = []
    for i in range(n_w):
        give = pl.ds(pl.multiple_of((2 * i + 1 - parity) * width, width), width)
        keep = pl.ds(pl.multiple_of((2 * i + parity) * width, width), width)
        swapped.append(remote(g_ref.at[:, give], theirs.at[i], p_send.at[i], p_recv.at[i],
                              {"dp": pair}))
        own = pltpu.make_async_copy(g_ref.at[:, keep], mine.at[i], p_local.at[i])
        own.start()
        kept.append(own)
    steps = (ring // 2, ring - 1 - ring // 2)
    moving = [None, None]
    own_w = None
    for s in range(max(steps)):
        if s == 1:
            for copy in swapped:
                copy.wait()
            for copy in kept:
                copy.wait()
            w_ref[...] = (
                mine[...].astype(jnp.float32) + theirs[...].astype(jnp.float32)
            ).astype(w_ref.dtype)
            for j in range(1, n_w):
                peer = lax.rem(me_w + j, n_w)
                waits.append(remote(w_ref.at[peer], w_out.at[me_w], w_send.at[j], w_recv.at[j],
                                    {"dp": 2 * peer + parity}))
            own_w = pltpu.make_async_copy(w_ref.at[me_w], w_out.at[me_w], local_sem.at[0])
            own_w.start()
        for d, (target, sign) in enumerate(((right, -1), (left, 1))):
            if s >= steps[d]:
                continue
            q = lax.rem(z - sign * (steps[d] - s) + 2 * ring, ring)
            sent = []
            for h, start in enumerate((t_base, t_other)):
                slot = start + q
                if s == 0:
                    src = x_ref.at[slot]
                else:
                    moving[d][h].wait_recv()
                    send_buf[d, s, h] = (
                        recv_buf[d, s - 1, h].astype(jnp.float32) + x_ref[slot].astype(jnp.float32)
                    ).astype(send_buf.dtype)
                    src = send_buf.at[d, s, h]
                sent.append(remote(src, recv_buf.at[d, s, h], t_send.at[d, s, h],
                                   t_recv.at[d, s, h], {"tensor": target}))
            waits.extend(sent)
            moving[d] = sent
    for d in range(2):
        for copy in moving[d]:
            copy.wait_recv()
    plus, minus = steps[0] - 1, steps[1] - 1
    cross_buf[...] = (
        x_ref[t_far].astype(jnp.float32)
        + recv_buf[0, plus, 1].astype(jnp.float32)
        + recv_buf[1, minus, 1].astype(jnp.float32)
    ).astype(cross_buf.dtype)
    crossed = remote(cross_buf, cross_in, c_sem.at[0], c_sem.at[1], {"tensor": t_far})
    crossed.wait()
    o_ref[...] = (
        x_ref[t].astype(jnp.float32)
        + recv_buf[0, plus, 0].astype(jnp.float32)
        + recv_buf[1, minus, 0].astype(jnp.float32)
        + cross_in[...].astype(jnp.float32)
    )
    for copy in waits:
        copy.wait_send()
    for j in range(1, n_w):
        pltpu.make_async_copy(w_out.at[0], w_out.at[0], w_recv.at[j]).wait()
    own_w.wait()


def end_exchange(partial, g, ring):
    n_t, rows, cols = partial.shape
    n_w = lax.axis_size("dp") // 2
    g_rows, g_cols = g.shape
    width = g_cols // (2 * n_w)
    slots = (n_w, g_rows, width)
    piece = (rows, cols)
    moved = 2 * (partial.size * partial.dtype.itemsize + g.size * g.dtype.itemsize)
    return pl.pallas_call(
        functools.partial(_end_body, ring),
        out_shape=[
            jax.ShapeDtypeStruct(piece, jnp.float32),
            jax.ShapeDtypeStruct(slots, g.dtype),
        ],
        in_specs=[pl.BlockSpec(memory_space=pltpu.VMEM), pl.BlockSpec(memory_space=pl.ANY)],
        out_specs=[pl.BlockSpec(memory_space=pltpu.VMEM), pl.BlockSpec(memory_space=pl.ANY)],
        scratch_shapes=[
            pltpu.VMEM((2, ring // 2, 2) + piece, partial.dtype),
            pltpu.VMEM((2, ring // 2, 2) + piece, partial.dtype),
            pltpu.VMEM(piece, partial.dtype),
            pltpu.VMEM(piece, partial.dtype),
            pltpu.VMEM(slots, g.dtype),
            pltpu.VMEM(slots, g.dtype),
            pltpu.VMEM(slots, g.dtype),
            pltpu.SemaphoreType.DMA((2, ring // 2, 2)),
            pltpu.SemaphoreType.DMA((2, ring // 2, 2)),
            pltpu.SemaphoreType.DMA((2,)),
            pltpu.SemaphoreType.DMA((n_w,)),
            pltpu.SemaphoreType.DMA((n_w,)),
            pltpu.SemaphoreType.DMA((n_w,)),
            pltpu.SemaphoreType.DMA((n_w,)),
            pltpu.SemaphoreType.DMA((n_w,)),
            pltpu.SemaphoreType.DMA((1,)),
        ],
        compiler_params=pltpu.CompilerParams(collective_id=1, has_side_effects=True),
        cost_estimate=pl.CostEstimate(flops=4 * partial.size, transcendentals=0, bytes_accessed=moved),
    )(partial, g)


def local(tokens, norm_gain, query_weight, kv_weight, out_weight, grad_out, doc_lengths):
    tensor_size = lax.axis_size("tensor")
    data_size = lax.axis_size("dp")
    tensor_index = lax.axis_index("tensor")
    sharers = tensor_size // KVH
    levels = sharers.bit_length() - 1
    contract_last = (((1,), (1,)), ((), ()))
    query_width = query_weight.shape[1]
    kv_width = kv_weight.shape[1]
    values32 = tokens.astype(jnp.float32)
    root_mean = jnp.sqrt(jnp.mean(values32 * values32, axis=-1) + epsilon)
    unit = values32 / root_mean[:, None]
    gain32 = norm_gain.astype(jnp.float32)
    normed_local = (unit * gain32).astype(jnp.bfloat16)
    rows = tokens.shape[0]
    pieces = jnp.stack([normed_local, grad_out])
    weights_local = jnp.concatenate([query_weight, kv_weight, out_weight.T], axis=1)
    tens_parts, weight_parts = gather_start(pieces, weights_local, RING)
    normed = tens_parts[:, 0].reshape(tensor_size * rows, -1)
    grad_full = tens_parts[:, 1].reshape(tensor_size * rows, -1)
    seq_length = normed.shape[0]
    weights_full = weight_parts.reshape(-1, weights_local.shape[1])
    query_full = weights_full[:, :query_width]
    kv_local = weights_full[:, query_width : query_width + kv_width]
    out_full_t = weights_full[:, query_width + kv_width :]
    queries = jnp.dot(normed, query_full, preferred_element_type=jnp.float32).astype(jnp.bfloat16)
    keyvals = jnp.dot(normed, kv_local, preferred_element_type=jnp.float32).astype(jnp.bfloat16)
    slot = lax.rem(lax.axis_index("tensor"), sharers)
    shifted = [keyvals]
    for k in range(1, sharers):
        shifted.append(lax.ppermute(keyvals, "tensor", group_shift(tensor_size, sharers, k)))
    shifted = jnp.stack(shifted)
    order = lax.rem(slot - jnp.arange(sharers) + sharers, sharers)
    keyvals = jnp.moveaxis(jnp.take(shifted, order, axis=0), 0, 1).reshape(seq_length, -1)
    key_rows = keyvals[:, :HD]
    value_rows = keyvals[:, HD:]
    out_grad = jnp.dot(grad_full, out_full_t, preferred_element_type=jnp.float32).astype(
        jnp.bfloat16
    )
    local_heads = queries.shape[1] // HD
    query_heads = queries.reshape(seq_length, local_heads, HD)
    out_heads = out_grad.reshape(seq_length, local_heads, HD)
    allowed = document_mask(doc_lengths[0], seq_length)
    scores = jnp.einsum(
        "qhd,td->hqt", query_heads, key_rows, preferred_element_type=jnp.float32
    ) / math.sqrt(HD)
    scores = jnp.where(allowed[None, :, :], scores, -1e30)
    peak = jnp.max(scores, axis=-1, keepdims=True)
    expo = jnp.exp(scores - peak)
    probs = expo / jnp.sum(expo, axis=-1, keepdims=True)
    probs_low = probs.astype(jnp.bfloat16)
    prob_grad = jnp.einsum("qhd,td->hqt", out_heads, value_rows, preferred_element_type=jnp.float32)
    inner = jnp.sum(probs * prob_grad, axis=-1, keepdims=True)
    score_grad = (probs * (prob_grad - inner) / math.sqrt(HD)).astype(jnp.bfloat16)
    query_grad = jnp.einsum("hqt,td->qhd", score_grad, key_rows, preferred_element_type=jnp.float32)
    query_grad = query_grad.astype(jnp.bfloat16).reshape(seq_length, local_heads * HD)
    key_part = jnp.einsum(
        "hqt,qhd->td", score_grad, query_heads, preferred_element_type=jnp.float32
    )
    value_part = jnp.einsum("hqt,qhd->td", probs_low, out_heads, preferred_element_type=jnp.float32)
    kv_partial = jnp.concatenate([key_part, value_part], axis=1)
    blocks = jnp.moveaxis(kv_partial.reshape(seq_length, sharers, -1), 1, 0)
    kv_sum = jnp.take(blocks, slot, axis=0)
    for k in range(1, sharers):
        handed = jnp.take(blocks, lax.rem(slot + k, sharers), axis=0).astype(jnp.bfloat16)
        kv_sum = kv_sum + lax.ppermute(handed, "tensor", group_shift(tensor_size, sharers, k)).astype(
            jnp.float32
        )
    kv_partial = kv_sum
    kv_grad = kv_partial.astype(jnp.bfloat16)
    from_query = lax.dot_general(
        query_grad, query_full, contract_last, preferred_element_type=jnp.float32
    )
    from_kv = lax.dot_general(kv_grad, kv_local, contract_last, preferred_element_type=jnp.float32)
    partial = (from_query + from_kv).astype(jnp.bfloat16).reshape(tensor_size, rows, -1)
    combined = jnp.concatenate([query_grad, kv_grad], axis=1)
    weight_partial = lax.dot_general(
        combined, normed, (((0,), (0,)), ((), ())), preferred_element_type=jnp.float32
    ).astype(jnp.bfloat16)
    block = weight_partial.shape[1] // data_size
    normed_grad, weight_arrived = end_exchange(partial, weight_partial, RING)
    scaled = normed_grad * gain32
    correction = unit * jnp.mean(scaled * unit, axis=-1, keepdims=True)
    input_grad = (grad_out.astype(jnp.float32) + (scaled - correction) / root_mean[:, None]).astype(
        jnp.bfloat16
    )
    weight_grads = (jnp.sum(weight_arrived.astype(jnp.float32), axis=0) / data_size).T
    return (input_grad, weight_grads[:, :query_width], weight_grads[:, query_width:])


def solution(mesh):
    placed = (
        P(("dp", "tensor"), None),
        P(),
        P("dp", "tensor"),
        P("dp", "tensor"),
        P("tensor", "dp"),
        P(("dp", "tensor"), None),
        P("dp", None),
    )
    return jax.shard_map(
        local,
        mesh=mesh,
        in_specs=placed,
        out_specs=(P(("dp", "tensor"), None), P("dp", "tensor"), P("dp", "tensor")),
        check_vma=False,
    )
```

```python
import functools
import math

import jax
import jax.numpy as jnp
from jax import lax
from jax.experimental import pallas as pl
from jax.experimental.pallas import tpu as pltpu
from jax.sharding import PartitionSpec as P

KVH = 4
HD = 128
MESH_ID = pl.DeviceIdType.MESH
RING = 8


epsilon = 1e-05


def partner_2(value, axis, bit):
    mask = 2**bit
    pairs = [(source, source ^ mask) for source in range(lax.axis_size(axis))]
    return lax.ppermute(value, axis, pairs)


def document_mask(lengths, length_total):
    ends = jnp.cumsum(lengths)
    positions = jnp.arange(length_total, dtype=jnp.int32)
    labels = jnp.sum((ends[None, :] <= positions[:, None]).astype(jnp.int32), axis=1)
    return (labels[:, None] == labels[None, :]) & (positions[None, :] <= positions[:, None])


def _push_body(plan, *refs):
    count = len(plan)
    ins = refs[:count]
    outs = refs[count : 2 * count]
    send_sems = refs[2 * count : 3 * count]
    recv_sems = refs[3 * count : 4 * count]
    local_sem = refs[4 * count]
    barrier = pltpu.get_barrier_semaphore()
    mine = []
    expected = 0
    places = []
    for axis, n, _, stride in plan:
        index = lax.axis_index(axis)
        me = lax.rem(index // stride, n)
        offset = index - me * stride
        mine.append(me)
        places.append(functools.partial(lambda o, st, p: o + p * st, offset, stride))
        for j in range(1, n):
            pl.semaphore_signal(
                barrier,
                inc=1,
                device_id={axis: places[-1](lax.rem(me + j, n))},
                device_id_type=MESH_ID,
            )
        expected += n - 1
    pl.semaphore_wait(barrier, expected)
    local = []
    for g, (axis, n, scatter, _) in enumerate(plan):
        me = mine[g]
        src = ins[g].at[me] if scatter else ins[g]
        copy = pltpu.make_async_copy(src, outs[g].at[me], local_sem.at[g])
        copy.start()
        local.append(copy)
    remote = []
    for j in range(1, max(n for _, n, _, _ in plan)):
        for g, (axis, n, scatter, _) in enumerate(plan):
            if j >= n:
                continue
            me = mine[g]
            peer = lax.rem(me + j, n)
            copy = pltpu.make_async_remote_copy(
                src_ref=ins[g].at[peer] if scatter else ins[g],
                dst_ref=outs[g].at[me],
                send_sem=send_sems[g].at[j],
                recv_sem=recv_sems[g].at[j],
                device_id={axis: places[g](peer)},
                device_id_type=MESH_ID,
            )
            copy.start()
            remote.append(copy)
    for copy in remote:
        copy.wait()
    for copy in local:
        copy.wait()


def push_exchange(groups, cid):
    groups = [g if len(g) == 5 else g + (1,) for g in groups]
    plan = tuple((axis, n, scatter, stride) for axis, n, _, scatter, stride in groups)
    arrays = [array for _, _, array, _, _ in groups]
    out_shape = []
    moved = 0
    for _, n, array, scatter, _ in groups:
        shape = array.shape if scatter else (n,) + array.shape
        out_shape.append(jax.ShapeDtypeStruct(shape, array.dtype))
        moved += 2 * math.prod(shape) * array.dtype.itemsize
    count = len(groups)
    return pl.pallas_call(
        functools.partial(_push_body, plan),
        out_shape=out_shape,
        in_specs=[pl.BlockSpec(memory_space=pl.ANY)] * count,
        out_specs=[pl.BlockSpec(memory_space=pl.ANY)] * count,
        scratch_shapes=[pltpu.SemaphoreType.DMA((n,)) for _, n, _, _, _ in groups]
        + [pltpu.SemaphoreType.DMA((n,)) for _, n, _, _, _ in groups]
        + [pltpu.SemaphoreType.DMA((count,))],
        compiler_params=pltpu.CompilerParams(collective_id=cid, has_side_effects=True),
        cost_estimate=pl.CostEstimate(flops=0, transcendentals=0, bytes_accessed=moved),
    )(*arrays)


def _gather_start_body(ring, pieces_ref, weights_ref, tens_out, dp_out, t_send, t_recv, t_cross,
                       d_send, d_recv, d_cross, pair_send, pair_recv, local_sem):
    n_t = lax.axis_size("tensor")
    n_d = lax.axis_size("dp")
    t = lax.axis_index("tensor")
    r = lax.axis_index("dp")
    z = lax.rem(t, ring)
    t_base = t - z
    t_other = lax.rem(t + ring, n_t) - z
    t_far = lax.rem(t + ring, n_t)
    d_ring = n_d // 4
    core = lax.rem(r, 2)
    y = lax.rem(r // 2, d_ring)
    x = r // (2 * d_ring)
    d_base = x * 2 * d_ring + core
    d_other = (1 - x) * 2 * d_ring + core
    d_far = d_other + 2 * y
    pair = r + 1 - 2 * core
    rings = (
        ("tensor", tens_out, pieces_ref, z, (t_base, t_other), 1, ring, t_send, t_recv),
        ("dp", dp_out, weights_ref, y, (d_base, d_other), 2, d_ring, d_send, d_recv),
    )

    def neighbours(pos, bases, stride, n):
        return (bases[0] + lax.rem(pos + 1, n) * stride, bases[0] + lax.rem(pos + n - 1, n) * stride)

    barrier = pltpu.get_barrier_semaphore()
    targets = [{"tensor": t_far}, {"dp": pair}, {"dp": d_far}]
    for axis, _, _, pos, bases, stride, n, _, _ in rings:
        targets.extend({axis: v} for v in neighbours(pos, bases, stride, n))
    for device in targets:
        pl.semaphore_signal(barrier, inc=1, device_id=device, device_id_type=MESH_ID)
    pl.semaphore_wait(barrier, len(targets))

    def remote(src, dst, send, recv, device):
        copy = pltpu.make_async_remote_copy(
            src_ref=src, dst_ref=dst, send_sem=send, recv_sem=recv,
            device_id=device, device_id_type=MESH_ID,
        )
        copy.start()
        return copy

    waits = []
    forwarded = [0]

    def forward(src, slot):
        f = forwarded[0]
        waits.append(remote(src, dp_out.at[slot], pair_send.at[f], pair_recv.at[f], {"dp": pair}))
        forwarded[0] = f + 1

    forward(weights_ref, r)
    t_crossed = remote(pieces_ref, tens_out.at[t], t_cross.at[0], t_cross.at[1], {"tensor": t_far})
    d_crossed = remote(weights_ref, dp_out.at[r], d_cross.at[0], d_cross.at[1], {"dp": d_far})
    own_t = pltpu.make_async_copy(pieces_ref, tens_out.at[t], local_sem.at[0])
    own_t.start()
    own_d = pltpu.make_async_copy(weights_ref, dp_out.at[r], local_sem.at[1])
    own_d.start()
    moving = {}
    for k, (axis, out, own, pos, bases, stride, n, send, recv) in enumerate(rings):
        for d, target in enumerate(neighbours(pos, bases, stride, n)):
            first = remote(own, out.at[bases[0] + pos * stride], send.at[d, 0, 0], recv.at[d, 0, 0],
                           {axis: target})
            waits.append(first)
            moving[k, d] = [first]
    t_crossed.wait()
    d_crossed.wait()
    forward(dp_out.at[d_far], d_far)
    for s in range(max(ring, d_ring) // 2):
        for k, (axis, out, own, pos, bases, stride, n, send, recv) in enumerate(rings):
            right, left = neighbours(pos, bases, stride, n)
            steps = (n // 2, n - 1 - n // 2)
            for d, (target, sign) in enumerate(((right, -1), (left, 1))):
                if s >= steps[d]:
                    continue
                origin = lax.rem(pos + sign * s + n, n)
                if s > 0:
                    for copy in moving[k, d]:
                        copy.wait_recv()
                    if k == 1:
                        for start in bases:
                            slot = start + origin * stride
                            forward(out.at[slot], slot)
                sent = list(moving[k, d]) if s == 0 else []
                for h, start in enumerate(bases):
                    if s == 0 and h == 0:
                        continue
                    slot = start + origin * stride
                    sent.append(remote(out.at[slot], out.at[slot], send.at[d, s, h],
                                       recv.at[d, s, h], {axis: target}))
                    waits.append(sent[-1])
                moving[k, d] = sent
    for k, (axis, out, own, pos, bases, stride, n, send, recv) in enumerate(rings):
        steps = (n // 2, n - 1 - n // 2)
        for d, sign in enumerate((-1, 1)):
            for copy in moving[k, d]:
                copy.wait_recv()
            if k == 1:
                origin = lax.rem(pos + sign * steps[d] + n, n)
                for start in bases:
                    slot = start + origin * stride
                    forward(out.at[slot], slot)
    for copy in waits:
        copy.wait_send()
    for f in range(forwarded[0]):
        pltpu.make_async_copy(dp_out.at[0], dp_out.at[0], pair_recv.at[f]).wait()
    own_t.wait()
    own_d.wait()


def gather_start(pieces, weights, ring):
    n_t = lax.axis_size("tensor")
    n_d = lax.axis_size("dp")
    d_ring = n_d // 4
    moved = 2 * (n_t * pieces.size * pieces.dtype.itemsize + n_d * weights.size * weights.dtype.itemsize)
    return pl.pallas_call(
        functools.partial(_gather_start_body, ring),
        out_shape=[
            jax.ShapeDtypeStruct((n_t,) + pieces.shape, pieces.dtype),
            jax.ShapeDtypeStruct((n_d,) + weights.shape, weights.dtype),
        ],
        in_specs=[pl.BlockSpec(memory_space=pl.ANY)] * 2,
        out_specs=[pl.BlockSpec(memory_space=pl.ANY)] * 2,
        scratch_shapes=[
            pltpu.SemaphoreType.DMA((2, ring // 2, 2)),
            pltpu.SemaphoreType.DMA((2, ring // 2, 2)),
            pltpu.SemaphoreType.DMA((2,)),
            pltpu.SemaphoreType.DMA((2, d_ring // 2, 2)),
            pltpu.SemaphoreType.DMA((2, d_ring // 2, 2)),
            pltpu.SemaphoreType.DMA((2,)),
            pltpu.SemaphoreType.DMA((2 * d_ring,)),
            pltpu.SemaphoreType.DMA((2 * d_ring,)),
            pltpu.SemaphoreType.DMA((2,)),
        ],
        compiler_params=pltpu.CompilerParams(collective_id=0, has_side_effects=True),
        cost_estimate=pl.CostEstimate(flops=0, transcendentals=0, bytes_accessed=moved),
    )(pieces, weights)


def _pair_body(x_ref, o_ref, mine, theirs, send_sem, recv_sem, local_sem):
    r = lax.axis_index("dp")
    parity = lax.rem(r, 2)
    pair = r + 1 - 2 * parity
    slots, _, width = mine.shape
    barrier = pltpu.get_barrier_semaphore()
    pl.semaphore_signal(barrier, inc=1, device_id={"dp": pair}, device_id_type=MESH_ID)
    pl.semaphore_wait(barrier, 1)
    sent = []
    kept = []
    for i in range(slots):
        give = pl.ds(pl.multiple_of((2 * i + 1 - parity) * width, width), width)
        keep = pl.ds(pl.multiple_of((2 * i + parity) * width, width), width)
        copy = pltpu.make_async_remote_copy(
            src_ref=x_ref.at[:, give], dst_ref=theirs.at[i], send_sem=send_sem.at[i],
            recv_sem=recv_sem.at[i], device_id={"dp": pair}, device_id_type=MESH_ID,
        )
        copy.start()
        sent.append(copy)
        own = pltpu.make_async_copy(x_ref.at[:, keep], mine.at[i], local_sem.at[i])
        own.start()
        kept.append(own)
    for copy in sent:
        copy.wait()
    for copy in kept:
        copy.wait()
    o_ref[...] = (mine[...].astype(jnp.float32) + theirs[...].astype(jnp.float32)).astype(o_ref.dtype)


def pair_sum(x, width):
    rows, cols = x.shape
    slots = cols // width // 2
    shape = (slots, rows, width)
    return pl.pallas_call(
        _pair_body,
        out_shape=jax.ShapeDtypeStruct(shape, x.dtype),
        in_specs=[pl.BlockSpec(memory_space=pl.ANY)],
        out_specs=pl.BlockSpec(memory_space=pltpu.VMEM),
        scratch_shapes=[
            pltpu.VMEM(shape, x.dtype),
            pltpu.VMEM(shape, x.dtype),
            pltpu.SemaphoreType.DMA((slots,)),
            pltpu.SemaphoreType.DMA((slots,)),
            pltpu.SemaphoreType.DMA((slots,)),
        ],
        compiler_params=pltpu.CompilerParams(collective_id=4, has_side_effects=True),
        cost_estimate=pl.CostEstimate(
            flops=x.size // 2, transcendentals=0, bytes_accessed=2 * x.size * x.dtype.itemsize
        ),
    )(x)


def _end_body(ring, x_ref, g_ref, o_ref, w_out, send_buf, recv_buf, cross_buf, cross_in,
              mine, theirs, w_ref, t_send, t_recv, c_sem, w_send, w_recv, p_send, p_recv, p_local,
              local_sem):
    n_t = lax.axis_size("tensor")
    n_d = lax.axis_size("dp")
    t = lax.axis_index("tensor")
    r = lax.axis_index("dp")
    z = lax.rem(t, ring)
    t_base = t - z
    t_other = lax.rem(t + ring, n_t) - z
    t_far = lax.rem(t + ring, n_t)
    right = t_base + lax.rem(z + 1, ring)
    left = t_base + lax.rem(z + ring - 1, ring)
    parity = lax.rem(r, 2)
    pair = r + 1 - 2 * parity
    n_w = n_d // 2
    me_w = r // 2
    width = mine.shape[2]
    barrier = pltpu.get_barrier_semaphore()
    for device in ({"tensor": t_far}, {"tensor": right}, {"tensor": left}, {"dp": pair}):
        pl.semaphore_signal(barrier, inc=1, device_id=device, device_id_type=MESH_ID)
    for j in range(1, n_w):
        peer = 2 * lax.rem(me_w + j, n_w) + parity
        pl.semaphore_signal(barrier, inc=1, device_id={"dp": peer}, device_id_type=MESH_ID)
    pl.semaphore_wait(barrier, 4 + n_w - 1)

    def remote(src, dst, send, recv, device):
        copy = pltpu.make_async_remote_copy(
            src_ref=src, dst_ref=dst, send_sem=send, recv_sem=recv,
            device_id=device, device_id_type=MESH_ID,
        )
        copy.start()
        return copy

    waits = []
    swapped = []
    kept = []
    for i in range(n_w):
        give = pl.ds(pl.multiple_of((2 * i + 1 - parity) * width, width), width)
        keep = pl.ds(pl.multiple_of((2 * i + parity) * width, width), width)
        swapped.append(remote(g_ref.at[:, give], theirs.at[i], p_send.at[i], p_recv.at[i],
                              {"dp": pair}))
        own = pltpu.make_async_copy(g_ref.at[:, keep], mine.at[i], p_local.at[i])
        own.start()
        kept.append(own)
    steps = (ring // 2, ring - 1 - ring // 2)
    moving = [None, None]
    own_w = None
    for s in range(max(steps)):
        if s == 1:
            for copy in swapped:
                copy.wait()
            for copy in kept:
                copy.wait()
            w_ref[...] = (
                mine[...].astype(jnp.float32) + theirs[...].astype(jnp.float32)
            ).astype(w_ref.dtype)
            for j in range(1, n_w):
                peer = lax.rem(me_w + j, n_w)
                waits.append(remote(w_ref.at[peer], w_out.at[me_w], w_send.at[j], w_recv.at[j],
                                    {"dp": 2 * peer + parity}))
            own_w = pltpu.make_async_copy(w_ref.at[me_w], w_out.at[me_w], local_sem.at[0])
            own_w.start()
        for d, (target, sign) in enumerate(((right, -1), (left, 1))):
            if s >= steps[d]:
                continue
            q = lax.rem(z - sign * (steps[d] - s) + 2 * ring, ring)
            sent = []
            for h, start in enumerate((t_base, t_other)):
                slot = start + q
                if s == 0:
                    src = x_ref.at[slot]
                else:
                    moving[d][h].wait_recv()
                    send_buf[d, s, h] = (
                        recv_buf[d, s - 1, h].astype(jnp.float32) + x_ref[slot].astype(jnp.float32)
                    ).astype(send_buf.dtype)
                    src = send_buf.at[d, s, h]
                sent.append(remote(src, recv_buf.at[d, s, h], t_send.at[d, s, h],
                                   t_recv.at[d, s, h], {"tensor": target}))
            waits.extend(sent)
            moving[d] = sent
    for d in range(2):
        for copy in moving[d]:
            copy.wait_recv()
    plus, minus = steps[0] - 1, steps[1] - 1
    cross_buf[...] = (
        x_ref[t_far].astype(jnp.float32)
        + recv_buf[0, plus, 1].astype(jnp.float32)
        + recv_buf[1, minus, 1].astype(jnp.float32)
    ).astype(cross_buf.dtype)
    crossed = remote(cross_buf, cross_in, c_sem.at[0], c_sem.at[1], {"tensor": t_far})
    crossed.wait()
    o_ref[...] = (
        x_ref[t].astype(jnp.float32)
        + recv_buf[0, plus, 0].astype(jnp.float32)
        + recv_buf[1, minus, 0].astype(jnp.float32)
        + cross_in[...].astype(jnp.float32)
    )
    for copy in waits:
        copy.wait_send()
    for j in range(1, n_w):
        pltpu.make_async_copy(w_out.at[0], w_out.at[0], w_recv.at[j]).wait()
    own_w.wait()


def end_exchange(partial, g, ring):
    n_t, rows, cols = partial.shape
    n_w = lax.axis_size("dp") // 2
    g_rows, g_cols = g.shape
    width = g_cols // (2 * n_w)
    slots = (n_w, g_rows, width)
    piece = (rows, cols)
    moved = 2 * (partial.size * partial.dtype.itemsize + g.size * g.dtype.itemsize)
    return pl.pallas_call(
        functools.partial(_end_body, ring),
        out_shape=[
            jax.ShapeDtypeStruct(piece, jnp.float32),
            jax.ShapeDtypeStruct(slots, g.dtype),
        ],
        in_specs=[pl.BlockSpec(memory_space=pltpu.VMEM), pl.BlockSpec(memory_space=pl.ANY)],
        out_specs=[pl.BlockSpec(memory_space=pltpu.VMEM), pl.BlockSpec(memory_space=pl.ANY)],
        scratch_shapes=[
            pltpu.VMEM((2, ring // 2, 2) + piece, partial.dtype),
            pltpu.VMEM((2, ring // 2, 2) + piece, partial.dtype),
            pltpu.VMEM(piece, partial.dtype),
            pltpu.VMEM(piece, partial.dtype),
            pltpu.VMEM(slots, g.dtype),
            pltpu.VMEM(slots, g.dtype),
            pltpu.VMEM(slots, g.dtype),
            pltpu.SemaphoreType.DMA((2, ring // 2, 2)),
            pltpu.SemaphoreType.DMA((2, ring // 2, 2)),
            pltpu.SemaphoreType.DMA((2,)),
            pltpu.SemaphoreType.DMA((n_w,)),
            pltpu.SemaphoreType.DMA((n_w,)),
            pltpu.SemaphoreType.DMA((n_w,)),
            pltpu.SemaphoreType.DMA((n_w,)),
            pltpu.SemaphoreType.DMA((n_w,)),
            pltpu.SemaphoreType.DMA((1,)),
        ],
        compiler_params=pltpu.CompilerParams(collective_id=1, has_side_effects=True),
        cost_estimate=pl.CostEstimate(flops=4 * partial.size, transcendentals=0, bytes_accessed=moved),
    )(partial, g)


def local(tokens, norm_gain, query_weight, kv_weight, out_weight, grad_out, doc_lengths):
    tensor_size = lax.axis_size("tensor")
    data_size = lax.axis_size("dp")
    tensor_index = lax.axis_index("tensor")
    sharers = tensor_size // KVH
    levels = sharers.bit_length() - 1
    contract_last = (((1,), (1,)), ((), ()))
    query_width = query_weight.shape[1]
    kv_width = kv_weight.shape[1]
    values32 = tokens.astype(jnp.float32)
    root_mean = jnp.sqrt(jnp.mean(values32 * values32, axis=-1) + epsilon)
    unit = values32 / root_mean[:, None]
    gain32 = norm_gain.astype(jnp.float32)
    normed_local = (unit * gain32).astype(jnp.bfloat16)
    rows = tokens.shape[0]
    pieces = jnp.stack([normed_local, grad_out])
    weights_local = jnp.concatenate([query_weight, kv_weight, out_weight.T], axis=1)
    tens_parts, weight_parts = gather_start(pieces, weights_local, RING)
    normed = tens_parts[:, 0].reshape(tensor_size * rows, -1)
    grad_full = tens_parts[:, 1].reshape(tensor_size * rows, -1)
    seq_length = normed.shape[0]
    weights_full = weight_parts.reshape(-1, weights_local.shape[1])
    query_full = weights_full[:, :query_width]
    kv_local = weights_full[:, query_width : query_width + kv_width]
    out_full_t = weights_full[:, query_width + kv_width :]
    queries = jnp.dot(normed, query_full, preferred_element_type=jnp.float32).astype(jnp.bfloat16)
    keyvals = jnp.dot(normed, kv_local, preferred_element_type=jnp.float32).astype(jnp.bfloat16)
    for bit_index in range(levels):
        partner = partner_2(keyvals, "tensor", bit_index)
        joined_upper_half = tensor_index >> bit_index & 1 == 1
        keyvals = jnp.concatenate(
            [
                jnp.where(joined_upper_half, partner, keyvals),
                jnp.where(joined_upper_half, keyvals, partner),
            ],
            axis=1,
        )
    key_rows = keyvals[:, :HD]
    value_rows = keyvals[:, HD:]
    out_grad = jnp.dot(grad_full, out_full_t, preferred_element_type=jnp.float32).astype(
        jnp.bfloat16
    )
    local_heads = queries.shape[1] // HD
    query_heads = queries.reshape(seq_length, local_heads, HD)
    out_heads = out_grad.reshape(seq_length, local_heads, HD)
    allowed = document_mask(doc_lengths[0], seq_length)
    scores = jnp.einsum(
        "qhd,td->hqt", query_heads, key_rows, preferred_element_type=jnp.float32
    ) / math.sqrt(HD)
    scores = jnp.where(allowed[None, :, :], scores, -1e30)
    peak = jnp.max(scores, axis=-1, keepdims=True)
    expo = jnp.exp(scores - peak)
    probs = expo / jnp.sum(expo, axis=-1, keepdims=True)
    probs_low = probs.astype(jnp.bfloat16)
    prob_grad = jnp.einsum("qhd,td->hqt", out_heads, value_rows, preferred_element_type=jnp.float32)
    inner = jnp.sum(probs * prob_grad, axis=-1, keepdims=True)
    score_grad = (probs * (prob_grad - inner) / math.sqrt(HD)).astype(jnp.bfloat16)
    query_grad = jnp.einsum("hqt,td->qhd", score_grad, key_rows, preferred_element_type=jnp.float32)
    query_grad = query_grad.astype(jnp.bfloat16).reshape(seq_length, local_heads * HD)
    key_part = jnp.einsum(
        "hqt,qhd->td", score_grad, query_heads, preferred_element_type=jnp.float32
    )
    value_part = jnp.einsum("hqt,qhd->td", probs_low, out_heads, preferred_element_type=jnp.float32)
    kv_partial = jnp.concatenate([key_part, value_part], axis=1)
    for bit_index in reversed(range(levels)):
        half_cols = kv_partial.shape[1] // 2
        upper_half = tensor_index >> bit_index & 1 == 1
        lower_cols = kv_partial[:, :half_cols]
        higher_cols = kv_partial[:, half_cols:]
        kept = jnp.where(upper_half, higher_cols, lower_cols)
        handed = jnp.where(upper_half, lower_cols, higher_cols)
        kv_partial = kept + partner_2(handed.astype(jnp.bfloat16), "tensor", bit_index).astype(
            handed.dtype
        )
    kv_grad = kv_partial.astype(jnp.bfloat16)
    from_query = lax.dot_general(
        query_grad, query_full, contract_last, preferred_element_type=jnp.float32
    )
    from_kv = lax.dot_general(kv_grad, kv_local, contract_last, preferred_element_type=jnp.float32)
    partial = (from_query + from_kv).astype(jnp.bfloat16).reshape(tensor_size, rows, -1)
    combined = jnp.concatenate([query_grad, kv_grad], axis=1)
    weight_partial = lax.dot_general(
        combined, normed, (((0,), (0,)), ((), ())), preferred_element_type=jnp.float32
    ).astype(jnp.bfloat16)
    block = weight_partial.shape[1] // data_size
    normed_grad, weight_arrived = end_exchange(partial, weight_partial, RING)
    scaled = normed_grad * gain32
    correction = unit * jnp.mean(scaled * unit, axis=-1, keepdims=True)
    input_grad = (grad_out.astype(jnp.float32) + (scaled - correction) / root_mean[:, None]).astype(
        jnp.bfloat16
    )
    weight_grads = (jnp.sum(weight_arrived.astype(jnp.float32), axis=0) / data_size).T
    return (input_grad, weight_grads[:, :query_width], weight_grads[:, query_width:])


def solution(mesh):
    placed = (
        P(("dp", "tensor"), None),
        P(),
        P("dp", "tensor"),
        P("dp", "tensor"),
        P("tensor", "dp"),
        P(("dp", "tensor"), None),
        P("dp", None),
    )
    return jax.shard_map(
        local,
        mesh=mesh,
        in_specs=placed,
        out_specs=(P(("dp", "tensor"), None), P("dp", "tensor"), P("dp", "tensor")),
        check_vma=False,
    )
```

```python
import functools
import math

import jax
import jax.numpy as jnp
from jax import lax
from jax.experimental import pallas as pl
from jax.experimental.pallas import tpu as pltpu
from jax.sharding import PartitionSpec as P

KVH = 4
HD = 128
MESH_ID = pl.DeviceIdType.MESH
RING = 8


epsilon = 1e-05


def partner_2(value, axis, bit):
    mask = 2**bit
    pairs = [(source, source ^ mask) for source in range(lax.axis_size(axis))]
    return lax.ppermute(value, axis, pairs)


def document_mask(lengths, length_total):
    ends = jnp.cumsum(lengths)
    positions = jnp.arange(length_total, dtype=jnp.int32)
    labels = jnp.sum((ends[None, :] <= positions[:, None]).astype(jnp.int32), axis=1)
    return (labels[:, None] == labels[None, :]) & (positions[None, :] <= positions[:, None])


def _push_body(plan, *refs):
    count = len(plan)
    ins = refs[:count]
    outs = refs[count : 2 * count]
    send_sems = refs[2 * count : 3 * count]
    recv_sems = refs[3 * count : 4 * count]
    local_sem = refs[4 * count]
    barrier = pltpu.get_barrier_semaphore()
    mine = []
    expected = 0
    places = []
    for axis, n, _, stride in plan:
        index = lax.axis_index(axis)
        me = lax.rem(index // stride, n)
        offset = index - me * stride
        mine.append(me)
        places.append(functools.partial(lambda o, st, p: o + p * st, offset, stride))
        for j in range(1, n):
            pl.semaphore_signal(
                barrier,
                inc=1,
                device_id={axis: places[-1](lax.rem(me + j, n))},
                device_id_type=MESH_ID,
            )
        expected += n - 1
    pl.semaphore_wait(barrier, expected)
    local = []
    for g, (axis, n, scatter, _) in enumerate(plan):
        me = mine[g]
        src = ins[g].at[me] if scatter else ins[g]
        copy = pltpu.make_async_copy(src, outs[g].at[me], local_sem.at[g])
        copy.start()
        local.append(copy)
    remote = []
    for j in range(1, max(n for _, n, _, _ in plan)):
        for g, (axis, n, scatter, _) in enumerate(plan):
            if j >= n:
                continue
            me = mine[g]
            peer = lax.rem(me + j, n)
            copy = pltpu.make_async_remote_copy(
                src_ref=ins[g].at[peer] if scatter else ins[g],
                dst_ref=outs[g].at[me],
                send_sem=send_sems[g].at[j],
                recv_sem=recv_sems[g].at[j],
                device_id={axis: places[g](peer)},
                device_id_type=MESH_ID,
            )
            copy.start()
            remote.append(copy)
    for copy in remote:
        copy.wait()
    for copy in local:
        copy.wait()


def push_exchange(groups, cid):
    groups = [g if len(g) == 5 else g + (1,) for g in groups]
    plan = tuple((axis, n, scatter, stride) for axis, n, _, scatter, stride in groups)
    arrays = [array for _, _, array, _, _ in groups]
    out_shape = []
    moved = 0
    for _, n, array, scatter, _ in groups:
        shape = array.shape if scatter else (n,) + array.shape
        out_shape.append(jax.ShapeDtypeStruct(shape, array.dtype))
        moved += 2 * math.prod(shape) * array.dtype.itemsize
    count = len(groups)
    return pl.pallas_call(
        functools.partial(_push_body, plan),
        out_shape=out_shape,
        in_specs=[pl.BlockSpec(memory_space=pl.ANY)] * count,
        out_specs=[pl.BlockSpec(memory_space=pl.ANY)] * count,
        scratch_shapes=[pltpu.SemaphoreType.DMA((n,)) for _, n, _, _, _ in groups]
        + [pltpu.SemaphoreType.DMA((n,)) for _, n, _, _, _ in groups]
        + [pltpu.SemaphoreType.DMA((count,))],
        compiler_params=pltpu.CompilerParams(collective_id=cid, has_side_effects=True),
        cost_estimate=pl.CostEstimate(flops=0, transcendentals=0, bytes_accessed=moved),
    )(*arrays)


def _gather_start_body(ring, pieces_ref, weights_ref, tens_out, dp_out, t_send, t_recv, t_cross,
                       d_send, d_recv, d_cross, pair_send, pair_recv, local_sem):
    n_t = lax.axis_size("tensor")
    n_d = lax.axis_size("dp")
    t = lax.axis_index("tensor")
    r = lax.axis_index("dp")
    z = lax.rem(t, ring)
    t_base = t - z
    t_other = lax.rem(t + ring, n_t) - z
    t_far = lax.rem(t + ring, n_t)
    d_ring = n_d // 4
    core = lax.rem(r, 2)
    y = lax.rem(r // 2, d_ring)
    x = r // (2 * d_ring)
    d_base = x * 2 * d_ring + core
    d_other = (1 - x) * 2 * d_ring + core
    d_far = d_other + 2 * y
    pair = r + 1 - 2 * core
    rings = (
        ("tensor", tens_out, pieces_ref, z, (t_base, t_other), 1, ring, t_send, t_recv),
        ("dp", dp_out, weights_ref, y, (d_base, d_other), 2, d_ring, d_send, d_recv),
    )

    def neighbours(pos, bases, stride, n):
        return (bases[0] + lax.rem(pos + 1, n) * stride, bases[0] + lax.rem(pos + n - 1, n) * stride)

    barrier = pltpu.get_barrier_semaphore()
    targets = [{"tensor": t_far}, {"dp": pair}, {"dp": d_far}]
    for axis, _, _, pos, bases, stride, n, _, _ in rings:
        targets.extend({axis: v} for v in neighbours(pos, bases, stride, n))
    for device in targets:
        pl.semaphore_signal(barrier, inc=1, device_id=device, device_id_type=MESH_ID)
    pl.semaphore_wait(barrier, len(targets))

    def remote(src, dst, send, recv, device):
        copy = pltpu.make_async_remote_copy(
            src_ref=src, dst_ref=dst, send_sem=send, recv_sem=recv,
            device_id=device, device_id_type=MESH_ID,
        )
        copy.start()
        return copy

    waits = []
    forwarded = [0]

    halves = []

    def forward(src, slot, dst=None):
        f = forwarded[0]
        waits.append(remote(src, dst if dst is not None else dp_out.at[slot], pair_send.at[f],
                            pair_recv.at[f], {"dp": pair}))
        halves.append(dst is not None)
        forwarded[0] = f + 1

    forward(weights_ref, r)
    t_crossed = remote(pieces_ref, tens_out.at[t], t_cross.at[0], t_cross.at[1], {"tensor": t_far})
    d_crossed = remote(weights_ref, dp_out.at[r], d_cross.at[0], d_cross.at[1], {"dp": d_far})
    own_t = pltpu.make_async_copy(pieces_ref, tens_out.at[t], local_sem.at[0])
    own_t.start()
    own_d = pltpu.make_async_copy(weights_ref, dp_out.at[r], local_sem.at[1])
    own_d.start()
    moving = {}
    for k, (axis, out, own, pos, bases, stride, n, send, recv) in enumerate(rings):
        for d, target in enumerate(neighbours(pos, bases, stride, n)):
            first = remote(own, out.at[bases[0] + pos * stride], send.at[d, 0, 0], recv.at[d, 0, 0],
                           {axis: target})
            waits.append(first)
            moving[k, d] = [first]
    t_crossed.wait()
    d_crossed.wait()
    forward(dp_out.at[d_far], d_far)
    sizes = [None] * 2

    def part(ref, d, last):
        if not last:
            return ref
        rows = ref.shape[0] // 2
        return ref.at[pl.ds(d * rows, rows)]

    for s in range(max(ring, d_ring) // 2):
        for k, (axis, out, own, pos, bases, stride, n, send, recv) in enumerate(rings):
            right, left = neighbours(pos, bases, stride, n)
            steps = n // 2
            for d, (target, sign) in enumerate(((right, -1), (left, 1))):
                if s >= steps:
                    continue
                origin = lax.rem(pos + sign * s + n, n)
                if s > 0:
                    for copy in moving[k, d]:
                        copy.wait_recv()
                    if k == 1:
                        for start in bases:
                            slot = start + origin * stride
                            forward(out.at[slot], slot)
                last = s == steps - 1
                sent = list(moving[k, d]) if s == 0 else []
                for h, start in enumerate(bases):
                    if s == 0 and h == 0:
                        continue
                    slot = start + origin * stride
                    piece = part(out.at[slot], d, last)
                    sent.append(remote(piece, piece, send.at[d, s, h], recv.at[d, s, h],
                                       {axis: target}))
                    waits.append(sent[-1])
                moving[k, d] = sent
    for k, (axis, out, own, pos, bases, stride, n, send, recv) in enumerate(rings):
        steps = n // 2
        for d, sign in enumerate((-1, 1)):
            for copy in moving[k, d]:
                copy.wait_recv()
            if k == 1:
                origin = lax.rem(pos + sign * steps + n, n)
                for start in bases:
                    slot = start + origin * stride
                    piece = part(out.at[slot], d, True)
                    forward(piece, slot, piece)
    for copy in waits:
        copy.wait_send()
    for f in range(forwarded[0]):
        probe = dp_out.at[0]
        if halves[f]:
            probe = probe.at[pl.ds(0, probe.shape[0] // 2)]
        pltpu.make_async_copy(probe, probe, pair_recv.at[f]).wait()
    own_t.wait()
    own_d.wait()


def gather_start(pieces, weights, ring):
    n_t = lax.axis_size("tensor")
    n_d = lax.axis_size("dp")
    d_ring = n_d // 4
    moved = 2 * (n_t * pieces.size * pieces.dtype.itemsize + n_d * weights.size * weights.dtype.itemsize)
    return pl.pallas_call(
        functools.partial(_gather_start_body, ring),
        out_shape=[
            jax.ShapeDtypeStruct((n_t,) + pieces.shape, pieces.dtype),
            jax.ShapeDtypeStruct((n_d,) + weights.shape, weights.dtype),
        ],
        in_specs=[pl.BlockSpec(memory_space=pl.ANY)] * 2,
        out_specs=[pl.BlockSpec(memory_space=pl.ANY)] * 2,
        scratch_shapes=[
            pltpu.SemaphoreType.DMA((2, ring // 2, 2)),
            pltpu.SemaphoreType.DMA((2, ring // 2, 2)),
            pltpu.SemaphoreType.DMA((2,)),
            pltpu.SemaphoreType.DMA((2, d_ring // 2, 2)),
            pltpu.SemaphoreType.DMA((2, d_ring // 2, 2)),
            pltpu.SemaphoreType.DMA((2,)),
            pltpu.SemaphoreType.DMA((2 * d_ring + 2,)),
            pltpu.SemaphoreType.DMA((2 * d_ring + 2,)),
            pltpu.SemaphoreType.DMA((2,)),
        ],
        compiler_params=pltpu.CompilerParams(collective_id=0, has_side_effects=True),
        cost_estimate=pl.CostEstimate(flops=0, transcendentals=0, bytes_accessed=moved),
    )(pieces, weights)


def _pair_body(x_ref, o_ref, mine, theirs, send_sem, recv_sem, local_sem):
    r = lax.axis_index("dp")
    parity = lax.rem(r, 2)
    pair = r + 1 - 2 * parity
    slots, _, width = mine.shape
    barrier = pltpu.get_barrier_semaphore()
    pl.semaphore_signal(barrier, inc=1, device_id={"dp": pair}, device_id_type=MESH_ID)
    pl.semaphore_wait(barrier, 1)
    sent = []
    kept = []
    for i in range(slots):
        give = pl.ds(pl.multiple_of((2 * i + 1 - parity) * width, width), width)
        keep = pl.ds(pl.multiple_of((2 * i + parity) * width, width), width)
        copy = pltpu.make_async_remote_copy(
            src_ref=x_ref.at[:, give], dst_ref=theirs.at[i], send_sem=send_sem.at[i],
            recv_sem=recv_sem.at[i], device_id={"dp": pair}, device_id_type=MESH_ID,
        )
        copy.start()
        sent.append(copy)
        own = pltpu.make_async_copy(x_ref.at[:, keep], mine.at[i], local_sem.at[i])
        own.start()
        kept.append(own)
    for copy in sent:
        copy.wait()
    for copy in kept:
        copy.wait()
    o_ref[...] = (mine[...].astype(jnp.float32) + theirs[...].astype(jnp.float32)).astype(o_ref.dtype)


def pair_sum(x, width):
    rows, cols = x.shape
    slots = cols // width // 2
    shape = (slots, rows, width)
    return pl.pallas_call(
        _pair_body,
        out_shape=jax.ShapeDtypeStruct(shape, x.dtype),
        in_specs=[pl.BlockSpec(memory_space=pl.ANY)],
        out_specs=pl.BlockSpec(memory_space=pltpu.VMEM),
        scratch_shapes=[
            pltpu.VMEM(shape, x.dtype),
            pltpu.VMEM(shape, x.dtype),
            pltpu.SemaphoreType.DMA((slots,)),
            pltpu.SemaphoreType.DMA((slots,)),
            pltpu.SemaphoreType.DMA((slots,)),
        ],
        compiler_params=pltpu.CompilerParams(collective_id=4, has_side_effects=True),
        cost_estimate=pl.CostEstimate(
            flops=x.size // 2, transcendentals=0, bytes_accessed=2 * x.size * x.dtype.itemsize
        ),
    )(x)


def _end_body(ring, x_ref, g_ref, o_ref, w_out, send_buf, recv_buf, cross_buf, cross_in,
              mine, theirs, w_ref, t_send, t_recv, c_sem, w_send, w_recv, p_send, p_recv, p_local,
              local_sem):
    n_t = lax.axis_size("tensor")
    n_d = lax.axis_size("dp")
    t = lax.axis_index("tensor")
    r = lax.axis_index("dp")
    z = lax.rem(t, ring)
    t_base = t - z
    t_other = lax.rem(t + ring, n_t) - z
    t_far = lax.rem(t + ring, n_t)
    right = t_base + lax.rem(z + 1, ring)
    left = t_base + lax.rem(z + ring - 1, ring)
    parity = lax.rem(r, 2)
    pair = r + 1 - 2 * parity
    n_w = n_d // 2
    me_w = r // 2
    width = mine.shape[2]
    barrier = pltpu.get_barrier_semaphore()
    for device in ({"tensor": t_far}, {"tensor": right}, {"tensor": left}, {"dp": pair}):
        pl.semaphore_signal(barrier, inc=1, device_id=device, device_id_type=MESH_ID)
    for j in range(1, n_w):
        peer = 2 * lax.rem(me_w + j, n_w) + parity
        pl.semaphore_signal(barrier, inc=1, device_id={"dp": peer}, device_id_type=MESH_ID)
    pl.semaphore_wait(barrier, 4 + n_w - 1)

    def remote(src, dst, send, recv, device):
        copy = pltpu.make_async_remote_copy(
            src_ref=src, dst_ref=dst, send_sem=send, recv_sem=recv,
            device_id=device, device_id_type=MESH_ID,
        )
        copy.start()
        return copy

    waits = []
    swapped = []
    kept = []
    for i in range(n_w):
        give = pl.ds(pl.multiple_of((2 * i + 1 - parity) * width, width), width)
        keep = pl.ds(pl.multiple_of((2 * i + parity) * width, width), width)
        swapped.append(remote(g_ref.at[:, give], theirs.at[i], p_send.at[i], p_recv.at[i],
                              {"dp": pair}))
        own = pltpu.make_async_copy(g_ref.at[:, keep], mine.at[i], p_local.at[i])
        own.start()
        kept.append(own)
    steps = (ring // 2, ring - 1 - ring // 2)
    moving = [None, None]
    own_w = None
    for s in range(max(steps)):
        if s == 1:
            for copy in swapped:
                copy.wait()
            for copy in kept:
                copy.wait()
            w_ref[...] = (
                mine[...].astype(jnp.float32) + theirs[...].astype(jnp.float32)
            ).astype(w_ref.dtype)
            for j in range(1, n_w):
                peer = lax.rem(me_w + j, n_w)
                waits.append(remote(w_ref.at[peer], w_out.at[me_w], w_send.at[j], w_recv.at[j],
                                    {"dp": 2 * peer + parity}))
            own_w = pltpu.make_async_copy(w_ref.at[me_w], w_out.at[me_w], local_sem.at[0])
            own_w.start()
        for d, (target, sign) in enumerate(((right, -1), (left, 1))):
            if s >= steps[d]:
                continue
            q = lax.rem(z - sign * (steps[d] - s) + 2 * ring, ring)
            sent = []
            for h, start in enumerate((t_base, t_other)):
                slot = start + q
                if s == 0:
                    src = x_ref.at[slot]
                else:
                    moving[d][h].wait_recv()
                    send_buf[d, s, h] = (
                        recv_buf[d, s - 1, h].astype(jnp.float32) + x_ref[slot].astype(jnp.float32)
                    ).astype(send_buf.dtype)
                    src = send_buf.at[d, s, h]
                sent.append(remote(src, recv_buf.at[d, s, h], t_send.at[d, s, h],
                                   t_recv.at[d, s, h], {"tensor": target}))
            waits.extend(sent)
            moving[d] = sent
    for d in range(2):
        for copy in moving[d]:
            copy.wait_recv()
    plus, minus = steps[0] - 1, steps[1] - 1
    cross_buf[...] = (
        x_ref[t_far].astype(jnp.float32)
        + recv_buf[0, plus, 1].astype(jnp.float32)
        + recv_buf[1, minus, 1].astype(jnp.float32)
    ).astype(cross_buf.dtype)
    crossed = remote(cross_buf, cross_in, c_sem.at[0], c_sem.at[1], {"tensor": t_far})
    crossed.wait()
    o_ref[...] = (
        x_ref[t].astype(jnp.float32)
        + recv_buf[0, plus, 0].astype(jnp.float32)
        + recv_buf[1, minus, 0].astype(jnp.float32)
        + cross_in[...].astype(jnp.float32)
    )
    for copy in waits:
        copy.wait_send()
    for j in range(1, n_w):
        pltpu.make_async_copy(w_out.at[0], w_out.at[0], w_recv.at[j]).wait()
    own_w.wait()


def end_exchange(partial, g, ring):
    n_t, rows, cols = partial.shape
    n_w = lax.axis_size("dp") // 2
    g_rows, g_cols = g.shape
    width = g_cols // (2 * n_w)
    slots = (n_w, g_rows, width)
    piece = (rows, cols)
    moved = 2 * (partial.size * partial.dtype.itemsize + g.size * g.dtype.itemsize)
    return pl.pallas_call(
        functools.partial(_end_body, ring),
        out_shape=[
            jax.ShapeDtypeStruct(piece, jnp.float32),
            jax.ShapeDtypeStruct(slots, g.dtype),
        ],
        in_specs=[pl.BlockSpec(memory_space=pltpu.VMEM), pl.BlockSpec(memory_space=pl.ANY)],
        out_specs=[pl.BlockSpec(memory_space=pltpu.VMEM), pl.BlockSpec(memory_space=pl.ANY)],
        scratch_shapes=[
            pltpu.VMEM((2, ring // 2, 2) + piece, partial.dtype),
            pltpu.VMEM((2, ring // 2, 2) + piece, partial.dtype),
            pltpu.VMEM(piece, partial.dtype),
            pltpu.VMEM(piece, partial.dtype),
            pltpu.VMEM(slots, g.dtype),
            pltpu.VMEM(slots, g.dtype),
            pltpu.VMEM(slots, g.dtype),
            pltpu.SemaphoreType.DMA((2, ring // 2, 2)),
            pltpu.SemaphoreType.DMA((2, ring // 2, 2)),
            pltpu.SemaphoreType.DMA((2,)),
            pltpu.SemaphoreType.DMA((n_w,)),
            pltpu.SemaphoreType.DMA((n_w,)),
            pltpu.SemaphoreType.DMA((n_w,)),
            pltpu.SemaphoreType.DMA((n_w,)),
            pltpu.SemaphoreType.DMA((n_w,)),
            pltpu.SemaphoreType.DMA((1,)),
        ],
        compiler_params=pltpu.CompilerParams(collective_id=1, has_side_effects=True),
        cost_estimate=pl.CostEstimate(flops=4 * partial.size, transcendentals=0, bytes_accessed=moved),
    )(partial, g)


def local(tokens, norm_gain, query_weight, kv_weight, out_weight, grad_out, doc_lengths):
    tensor_size = lax.axis_size("tensor")
    data_size = lax.axis_size("dp")
    tensor_index = lax.axis_index("tensor")
    sharers = tensor_size // KVH
    levels = sharers.bit_length() - 1
    contract_last = (((1,), (1,)), ((), ()))
    query_width = query_weight.shape[1]
    kv_width = kv_weight.shape[1]
    values32 = tokens.astype(jnp.float32)
    root_mean = jnp.sqrt(jnp.mean(values32 * values32, axis=-1) + epsilon)
    unit = values32 / root_mean[:, None]
    gain32 = norm_gain.astype(jnp.float32)
    normed_local = (unit * gain32).astype(jnp.bfloat16)
    rows = tokens.shape[0]
    pieces = jnp.stack([normed_local, grad_out])
    weights_local = jnp.concatenate([query_weight, kv_weight, out_weight.T], axis=1)
    tens_parts, weight_parts = gather_start(pieces, weights_local, RING)
    normed = tens_parts[:, 0].reshape(tensor_size * rows, -1)
    grad_full = tens_parts[:, 1].reshape(tensor_size * rows, -1)
    seq_length = normed.shape[0]
    weights_full = weight_parts.reshape(-1, weights_local.shape[1])
    query_full = weights_full[:, :query_width]
    kv_local = weights_full[:, query_width : query_width + kv_width]
    out_full_t = weights_full[:, query_width + kv_width :]
    queries = jnp.dot(normed, query_full, preferred_element_type=jnp.float32).astype(jnp.bfloat16)
    keyvals = jnp.dot(normed, kv_local, preferred_element_type=jnp.float32).astype(jnp.bfloat16)
    for bit_index in range(levels):
        partner = partner_2(keyvals, "tensor", bit_index)
        joined_upper_half = tensor_index >> bit_index & 1 == 1
        keyvals = jnp.concatenate(
            [
                jnp.where(joined_upper_half, partner, keyvals),
                jnp.where(joined_upper_half, keyvals, partner),
            ],
            axis=1,
        )
    key_rows = keyvals[:, :HD]
    value_rows = keyvals[:, HD:]
    out_grad = jnp.dot(grad_full, out_full_t, preferred_element_type=jnp.float32).astype(
        jnp.bfloat16
    )
    local_heads = queries.shape[1] // HD
    query_heads = queries.reshape(seq_length, local_heads, HD)
    out_heads = out_grad.reshape(seq_length, local_heads, HD)
    allowed = document_mask(doc_lengths[0], seq_length)
    scores = jnp.einsum(
        "qhd,td->hqt", query_heads, key_rows, preferred_element_type=jnp.float32
    ) / math.sqrt(HD)
    scores = jnp.where(allowed[None, :, :], scores, -1e30)
    peak = jnp.max(scores, axis=-1, keepdims=True)
    expo = jnp.exp(scores - peak)
    probs = expo / jnp.sum(expo, axis=-1, keepdims=True)
    probs_low = probs.astype(jnp.bfloat16)
    prob_grad = jnp.einsum("qhd,td->hqt", out_heads, value_rows, preferred_element_type=jnp.float32)
    inner = jnp.sum(probs * prob_grad, axis=-1, keepdims=True)
    score_grad = (probs * (prob_grad - inner) / math.sqrt(HD)).astype(jnp.bfloat16)
    query_grad = jnp.einsum("hqt,td->qhd", score_grad, key_rows, preferred_element_type=jnp.float32)
    query_grad = query_grad.astype(jnp.bfloat16).reshape(seq_length, local_heads * HD)
    key_part = jnp.einsum(
        "hqt,qhd->td", score_grad, query_heads, preferred_element_type=jnp.float32
    )
    value_part = jnp.einsum("hqt,qhd->td", probs_low, out_heads, preferred_element_type=jnp.float32)
    kv_partial = jnp.concatenate([key_part, value_part], axis=1)
    for bit_index in reversed(range(levels)):
        half_cols = kv_partial.shape[1] // 2
        upper_half = tensor_index >> bit_index & 1 == 1
        lower_cols = kv_partial[:, :half_cols]
        higher_cols = kv_partial[:, half_cols:]
        kept = jnp.where(upper_half, higher_cols, lower_cols)
        handed = jnp.where(upper_half, lower_cols, higher_cols)
        kv_partial = kept + partner_2(handed.astype(jnp.bfloat16), "tensor", bit_index).astype(
            handed.dtype
        )
    kv_grad = kv_partial.astype(jnp.bfloat16)
    from_query = lax.dot_general(
        query_grad, query_full, contract_last, preferred_element_type=jnp.float32
    )
    from_kv = lax.dot_general(kv_grad, kv_local, contract_last, preferred_element_type=jnp.float32)
    partial = (from_query + from_kv).astype(jnp.bfloat16).reshape(tensor_size, rows, -1)
    combined = jnp.concatenate([query_grad, kv_grad], axis=1)
    weight_partial = lax.dot_general(
        combined, normed, (((0,), (0,)), ((), ())), preferred_element_type=jnp.float32
    ).astype(jnp.bfloat16)
    block = weight_partial.shape[1] // data_size
    normed_grad, weight_arrived = end_exchange(partial, weight_partial, RING)
    scaled = normed_grad * gain32
    correction = unit * jnp.mean(scaled * unit, axis=-1, keepdims=True)
    input_grad = (grad_out.astype(jnp.float32) + (scaled - correction) / root_mean[:, None]).astype(
        jnp.bfloat16
    )
    weight_grads = (jnp.sum(weight_arrived.astype(jnp.float32), axis=0) / data_size).T
    return (input_grad, weight_grads[:, :query_width], weight_grads[:, query_width:])


def solution(mesh):
    placed = (
        P(("dp", "tensor"), None),
        P(),
        P("dp", "tensor"),
        P("dp", "tensor"),
        P("tensor", "dp"),
        P(("dp", "tensor"), None),
        P("dp", None),
    )
    return jax.shard_map(
        local,
        mesh=mesh,
        in_specs=placed,
        out_specs=(P(("dp", "tensor"), None), P("dp", "tensor"), P("dp", "tensor")),
        check_vma=False,
    )
```

```python
import functools
import math

import jax
import jax.numpy as jnp
from jax import lax
from jax.experimental import pallas as pl
from jax.experimental.pallas import tpu as pltpu
from jax.sharding import PartitionSpec as P

KVH = 4
HD = 128
MESH_ID = pl.DeviceIdType.MESH
RING = 8


epsilon = 1e-05


def partner_2(value, axis, bit):
    mask = 2**bit
    pairs = [(source, source ^ mask) for source in range(lax.axis_size(axis))]
    return lax.ppermute(value, axis, pairs)


def document_mask(lengths, length_total):
    ends = jnp.cumsum(lengths)
    positions = jnp.arange(length_total, dtype=jnp.int32)
    labels = jnp.sum((ends[None, :] <= positions[:, None]).astype(jnp.int32), axis=1)
    return (labels[:, None] == labels[None, :]) & (positions[None, :] <= positions[:, None])


def _push_body(plan, *refs):
    count = len(plan)
    ins = refs[:count]
    outs = refs[count : 2 * count]
    send_sems = refs[2 * count : 3 * count]
    recv_sems = refs[3 * count : 4 * count]
    local_sem = refs[4 * count]
    barrier = pltpu.get_barrier_semaphore()
    mine = []
    expected = 0
    places = []
    for axis, n, _, stride in plan:
        index = lax.axis_index(axis)
        me = lax.rem(index // stride, n)
        offset = index - me * stride
        mine.append(me)
        places.append(functools.partial(lambda o, st, p: o + p * st, offset, stride))
        for j in range(1, n):
            pl.semaphore_signal(
                barrier,
                inc=1,
                device_id={axis: places[-1](lax.rem(me + j, n))},
                device_id_type=MESH_ID,
            )
        expected += n - 1
    pl.semaphore_wait(barrier, expected)
    local = []
    for g, (axis, n, scatter, _) in enumerate(plan):
        me = mine[g]
        src = ins[g].at[me] if scatter else ins[g]
        copy = pltpu.make_async_copy(src, outs[g].at[me], local_sem.at[g])
        copy.start()
        local.append(copy)
    remote = []
    for j in range(1, max(n for _, n, _, _ in plan)):
        for g, (axis, n, scatter, _) in enumerate(plan):
            if j >= n:
                continue
            me = mine[g]
            peer = lax.rem(me + j, n)
            copy = pltpu.make_async_remote_copy(
                src_ref=ins[g].at[peer] if scatter else ins[g],
                dst_ref=outs[g].at[me],
                send_sem=send_sems[g].at[j],
                recv_sem=recv_sems[g].at[j],
                device_id={axis: places[g](peer)},
                device_id_type=MESH_ID,
            )
            copy.start()
            remote.append(copy)
    for copy in remote:
        copy.wait()
    for copy in local:
        copy.wait()


def push_exchange(groups, cid):
    groups = [g if len(g) == 5 else g + (1,) for g in groups]
    plan = tuple((axis, n, scatter, stride) for axis, n, _, scatter, stride in groups)
    arrays = [array for _, _, array, _, _ in groups]
    out_shape = []
    moved = 0
    for _, n, array, scatter, _ in groups:
        shape = array.shape if scatter else (n,) + array.shape
        out_shape.append(jax.ShapeDtypeStruct(shape, array.dtype))
        moved += 2 * math.prod(shape) * array.dtype.itemsize
    count = len(groups)
    return pl.pallas_call(
        functools.partial(_push_body, plan),
        out_shape=out_shape,
        in_specs=[pl.BlockSpec(memory_space=pl.ANY)] * count,
        out_specs=[pl.BlockSpec(memory_space=pl.ANY)] * count,
        scratch_shapes=[pltpu.SemaphoreType.DMA((n,)) for _, n, _, _, _ in groups]
        + [pltpu.SemaphoreType.DMA((n,)) for _, n, _, _, _ in groups]
        + [pltpu.SemaphoreType.DMA((count,))],
        compiler_params=pltpu.CompilerParams(collective_id=cid, has_side_effects=True),
        cost_estimate=pl.CostEstimate(flops=0, transcendentals=0, bytes_accessed=moved),
    )(*arrays)


def _gather_start_body(ring, pieces_ref, weights_ref, tens_out, dp_out, t_send, t_recv, t_cross,
                       d_send, d_recv, d_cross, pair_send, pair_recv, local_sem):
    n_t = lax.axis_size("tensor")
    n_d = lax.axis_size("dp")
    t = lax.axis_index("tensor")
    r = lax.axis_index("dp")
    z = lax.rem(t, ring)
    t_base = t - z
    t_other = lax.rem(t + ring, n_t) - z
    t_far = lax.rem(t + ring, n_t)
    d_ring = n_d // 4
    core = lax.rem(r, 2)
    y = lax.rem(r // 2, d_ring)
    x = r // (2 * d_ring)
    d_base = x * 2 * d_ring + core
    d_other = (1 - x) * 2 * d_ring + core
    d_far = d_other + 2 * y
    pair = r + 1 - 2 * core
    rings = (
        ("tensor", tens_out, pieces_ref, z, (t_base, t_other), 1, ring, t_send, t_recv),
        ("dp", dp_out, weights_ref, y, (d_base, d_other), 2, d_ring, d_send, d_recv),
    )

    def neighbours(pos, bases, stride, n):
        return (bases[0] + lax.rem(pos + 1, n) * stride, bases[0] + lax.rem(pos + n - 1, n) * stride)

    barrier = pltpu.get_barrier_semaphore()
    targets = [{"tensor": t_far}, {"dp": pair}, {"dp": d_far}]
    for axis, _, _, pos, bases, stride, n, _, _ in rings:
        targets.extend({axis: v} for v in neighbours(pos, bases, stride, n))
    for device in targets:
        pl.semaphore_signal(barrier, inc=1, device_id=device, device_id_type=MESH_ID)
    pl.semaphore_wait(barrier, len(targets))

    def remote(src, dst, send, recv, device):
        copy = pltpu.make_async_remote_copy(
            src_ref=src, dst_ref=dst, send_sem=send, recv_sem=recv,
            device_id=device, device_id_type=MESH_ID,
        )
        copy.start()
        return copy

    waits = []
    forwarded = [0]

    halves = []

    def forward(src, slot, dst=None):
        f = forwarded[0]
        waits.append(remote(src, dst if dst is not None else dp_out.at[slot], pair_send.at[f],
                            pair_recv.at[f], {"dp": pair}))
        halves.append(dst is not None)
        forwarded[0] = f + 1

    moving = {}
    for k, (axis, out, own, pos, bases, stride, n, send, recv) in enumerate(rings):
        for d, target in enumerate(neighbours(pos, bases, stride, n)):
            first = remote(own, out.at[bases[0] + pos * stride], send.at[d, 0, 0], recv.at[d, 0, 0],
                           {axis: target})
            waits.append(first)
            moving[k, d] = [first]
    forward(weights_ref, r)
    t_crossed = remote(pieces_ref, tens_out.at[t], t_cross.at[0], t_cross.at[1], {"tensor": t_far})
    d_crossed = remote(weights_ref, dp_out.at[r], d_cross.at[0], d_cross.at[1], {"dp": d_far})
    own_t = pltpu.make_async_copy(pieces_ref, tens_out.at[t], local_sem.at[0])
    own_t.start()
    own_d = pltpu.make_async_copy(weights_ref, dp_out.at[r], local_sem.at[1])
    own_d.start()
    t_crossed.wait()
    d_crossed.wait()
    forward(dp_out.at[d_far], d_far)
    sizes = [None] * 2

    def part(ref, d, last):
        if not last:
            return ref
        rows = ref.shape[0] // 2
        return ref.at[pl.ds(d * rows, rows)]

    for s in range(max(ring, d_ring) // 2):
        for k, (axis, out, own, pos, bases, stride, n, send, recv) in enumerate(rings):
            right, left = neighbours(pos, bases, stride, n)
            steps = n // 2
            for d, (target, sign) in enumerate(((right, -1), (left, 1))):
                if s >= steps:
                    continue
                origin = lax.rem(pos + sign * s + n, n)
                if s > 0:
                    for copy in moving[k, d]:
                        copy.wait_recv()
                    if k == 1:
                        for start in bases:
                            slot = start + origin * stride
                            forward(out.at[slot], slot)
                last = s == steps - 1
                sent = list(moving[k, d]) if s == 0 else []
                for h, start in enumerate(bases):
                    if s == 0 and h == 0:
                        continue
                    slot = start + origin * stride
                    piece = part(out.at[slot], d, last)
                    sent.append(remote(piece, piece, send.at[d, s, h], recv.at[d, s, h],
                                       {axis: target}))
                    waits.append(sent[-1])
                moving[k, d] = sent
    for k, (axis, out, own, pos, bases, stride, n, send, recv) in enumerate(rings):
        steps = n // 2
        for d, sign in enumerate((-1, 1)):
            for copy in moving[k, d]:
                copy.wait_recv()
            if k == 1:
                origin = lax.rem(pos + sign * steps + n, n)
                for start in bases:
                    slot = start + origin * stride
                    piece = part(out.at[slot], d, True)
                    forward(piece, slot, piece)
    for copy in waits:
        copy.wait_send()
    for f in range(forwarded[0]):
        probe = dp_out.at[0]
        if halves[f]:
            probe = probe.at[pl.ds(0, probe.shape[0] // 2)]
        pltpu.make_async_copy(probe, probe, pair_recv.at[f]).wait()
    own_t.wait()
    own_d.wait()


def gather_start(pieces, weights, ring):
    n_t = lax.axis_size("tensor")
    n_d = lax.axis_size("dp")
    d_ring = n_d // 4
    moved = 2 * (n_t * pieces.size * pieces.dtype.itemsize + n_d * weights.size * weights.dtype.itemsize)
    return pl.pallas_call(
        functools.partial(_gather_start_body, ring),
        out_shape=[
            jax.ShapeDtypeStruct((n_t,) + pieces.shape, pieces.dtype),
            jax.ShapeDtypeStruct((n_d,) + weights.shape, weights.dtype),
        ],
        in_specs=[pl.BlockSpec(memory_space=pl.ANY)] * 2,
        out_specs=[pl.BlockSpec(memory_space=pl.ANY)] * 2,
        scratch_shapes=[
            pltpu.SemaphoreType.DMA((2, ring // 2, 2)),
            pltpu.SemaphoreType.DMA((2, ring // 2, 2)),
            pltpu.SemaphoreType.DMA((2,)),
            pltpu.SemaphoreType.DMA((2, d_ring // 2, 2)),
            pltpu.SemaphoreType.DMA((2, d_ring // 2, 2)),
            pltpu.SemaphoreType.DMA((2,)),
            pltpu.SemaphoreType.DMA((2 * d_ring + 2,)),
            pltpu.SemaphoreType.DMA((2 * d_ring + 2,)),
            pltpu.SemaphoreType.DMA((2,)),
        ],
        compiler_params=pltpu.CompilerParams(collective_id=0, has_side_effects=True),
        cost_estimate=pl.CostEstimate(flops=0, transcendentals=0, bytes_accessed=moved),
    )(pieces, weights)


def _pair_body(x_ref, o_ref, mine, theirs, send_sem, recv_sem, local_sem):
    r = lax.axis_index("dp")
    parity = lax.rem(r, 2)
    pair = r + 1 - 2 * parity
    slots, _, width = mine.shape
    barrier = pltpu.get_barrier_semaphore()
    pl.semaphore_signal(barrier, inc=1, device_id={"dp": pair}, device_id_type=MESH_ID)
    pl.semaphore_wait(barrier, 1)
    sent = []
    kept = []
    for i in range(slots):
        give = pl.ds(pl.multiple_of((2 * i + 1 - parity) * width, width), width)
        keep = pl.ds(pl.multiple_of((2 * i + parity) * width, width), width)
        copy = pltpu.make_async_remote_copy(
            src_ref=x_ref.at[:, give], dst_ref=theirs.at[i], send_sem=send_sem.at[i],
            recv_sem=recv_sem.at[i], device_id={"dp": pair}, device_id_type=MESH_ID,
        )
        copy.start()
        sent.append(copy)
        own = pltpu.make_async_copy(x_ref.at[:, keep], mine.at[i], local_sem.at[i])
        own.start()
        kept.append(own)
    for copy in sent:
        copy.wait()
    for copy in kept:
        copy.wait()
    o_ref[...] = (mine[...].astype(jnp.float32) + theirs[...].astype(jnp.float32)).astype(o_ref.dtype)


def pair_sum(x, width):
    rows, cols = x.shape
    slots = cols // width // 2
    shape = (slots, rows, width)
    return pl.pallas_call(
        _pair_body,
        out_shape=jax.ShapeDtypeStruct(shape, x.dtype),
        in_specs=[pl.BlockSpec(memory_space=pl.ANY)],
        out_specs=pl.BlockSpec(memory_space=pltpu.VMEM),
        scratch_shapes=[
            pltpu.VMEM(shape, x.dtype),
            pltpu.VMEM(shape, x.dtype),
            pltpu.SemaphoreType.DMA((slots,)),
            pltpu.SemaphoreType.DMA((slots,)),
            pltpu.SemaphoreType.DMA((slots,)),
        ],
        compiler_params=pltpu.CompilerParams(collective_id=4, has_side_effects=True),
        cost_estimate=pl.CostEstimate(
            flops=x.size // 2, transcendentals=0, bytes_accessed=2 * x.size * x.dtype.itemsize
        ),
    )(x)


def _end_body(ring, x_ref, g_ref, o_ref, w_out, send_buf, recv_buf, cross_buf, cross_in,
              mine, theirs, w_ref, t_send, t_recv, c_sem, w_send, w_recv, p_send, p_recv, p_local,
              local_sem):
    n_t = lax.axis_size("tensor")
    n_d = lax.axis_size("dp")
    t = lax.axis_index("tensor")
    r = lax.axis_index("dp")
    z = lax.rem(t, ring)
    t_base = t - z
    t_other = lax.rem(t + ring, n_t) - z
    t_far = lax.rem(t + ring, n_t)
    right = t_base + lax.rem(z + 1, ring)
    left = t_base + lax.rem(z + ring - 1, ring)
    parity = lax.rem(r, 2)
    pair = r + 1 - 2 * parity
    n_w = n_d // 2
    me_w = r // 2
    width = mine.shape[2]
    barrier = pltpu.get_barrier_semaphore()
    for device in ({"tensor": t_far}, {"tensor": right}, {"tensor": left}, {"dp": pair}):
        pl.semaphore_signal(barrier, inc=1, device_id=device, device_id_type=MESH_ID)
    for j in range(1, n_w):
        peer = 2 * lax.rem(me_w + j, n_w) + parity
        pl.semaphore_signal(barrier, inc=1, device_id={"dp": peer}, device_id_type=MESH_ID)
    pl.semaphore_wait(barrier, 4 + n_w - 1)

    def remote(src, dst, send, recv, device):
        copy = pltpu.make_async_remote_copy(
            src_ref=src, dst_ref=dst, send_sem=send, recv_sem=recv,
            device_id=device, device_id_type=MESH_ID,
        )
        copy.start()
        return copy

    waits = []
    swapped = []
    kept = []
    steps = (ring // 2, ring - 1 - ring // 2)
    moving = [None, None]
    own_w = None
    for s in range(max(steps)):
        if s == 1:
            for copy in swapped:
                copy.wait()
            for copy in kept:
                copy.wait()
            w_ref[...] = (
                mine[...].astype(jnp.float32) + theirs[...].astype(jnp.float32)
            ).astype(w_ref.dtype)
            for j in range(1, n_w):
                peer = lax.rem(me_w + j, n_w)
                waits.append(remote(w_ref.at[peer], w_out.at[me_w], w_send.at[j], w_recv.at[j],
                                    {"dp": 2 * peer + parity}))
            own_w = pltpu.make_async_copy(w_ref.at[me_w], w_out.at[me_w], local_sem.at[0])
            own_w.start()
        for d, (target, sign) in enumerate(((right, -1), (left, 1))):
            if s >= steps[d]:
                continue
            q = lax.rem(z - sign * (steps[d] - s) + 2 * ring, ring)
            sent = []
            for h, start in enumerate((t_base, t_other)):
                slot = start + q
                if s == 0:
                    src = x_ref.at[slot]
                else:
                    moving[d][h].wait_recv()
                    send_buf[d, s, h] = (
                        recv_buf[d, s - 1, h].astype(jnp.float32) + x_ref[slot].astype(jnp.float32)
                    ).astype(send_buf.dtype)
                    src = send_buf.at[d, s, h]
                sent.append(remote(src, recv_buf.at[d, s, h], t_send.at[d, s, h],
                                   t_recv.at[d, s, h], {"tensor": target}))
            waits.extend(sent)
            moving[d] = sent
        if s == 0:
            for i in range(n_w):
                give = pl.ds(pl.multiple_of((2 * i + 1 - parity) * width, width), width)
                keep = pl.ds(pl.multiple_of((2 * i + parity) * width, width), width)
                swapped.append(remote(g_ref.at[:, give], theirs.at[i], p_send.at[i], p_recv.at[i],
                                      {"dp": pair}))
                own = pltpu.make_async_copy(g_ref.at[:, keep], mine.at[i], p_local.at[i])
                own.start()
                kept.append(own)
    for d in range(2):
        for copy in moving[d]:
            copy.wait_recv()
    plus, minus = steps[0] - 1, steps[1] - 1
    cross_buf[...] = (
        x_ref[t_far].astype(jnp.float32)
        + recv_buf[0, plus, 1].astype(jnp.float32)
        + recv_buf[1, minus, 1].astype(jnp.float32)
    ).astype(cross_buf.dtype)
    crossed = remote(cross_buf, cross_in, c_sem.at[0], c_sem.at[1], {"tensor": t_far})
    crossed.wait()
    o_ref[...] = (
        x_ref[t].astype(jnp.float32)
        + recv_buf[0, plus, 0].astype(jnp.float32)
        + recv_buf[1, minus, 0].astype(jnp.float32)
        + cross_in[...].astype(jnp.float32)
    )
    for copy in waits:
        copy.wait_send()
    for j in range(1, n_w):
        pltpu.make_async_copy(w_out.at[0], w_out.at[0], w_recv.at[j]).wait()
    own_w.wait()


def end_exchange(partial, g, ring):
    n_t, rows, cols = partial.shape
    n_w = lax.axis_size("dp") // 2
    g_rows, g_cols = g.shape
    width = g_cols // (2 * n_w)
    slots = (n_w, g_rows, width)
    piece = (rows, cols)
    moved = 2 * (partial.size * partial.dtype.itemsize + g.size * g.dtype.itemsize)
    return pl.pallas_call(
        functools.partial(_end_body, ring),
        out_shape=[
            jax.ShapeDtypeStruct(piece, jnp.float32),
            jax.ShapeDtypeStruct(slots, g.dtype),
        ],
        in_specs=[pl.BlockSpec(memory_space=pltpu.VMEM), pl.BlockSpec(memory_space=pl.ANY)],
        out_specs=[pl.BlockSpec(memory_space=pltpu.VMEM), pl.BlockSpec(memory_space=pl.ANY)],
        scratch_shapes=[
            pltpu.VMEM((2, ring // 2, 2) + piece, partial.dtype),
            pltpu.VMEM((2, ring // 2, 2) + piece, partial.dtype),
            pltpu.VMEM(piece, partial.dtype),
            pltpu.VMEM(piece, partial.dtype),
            pltpu.VMEM(slots, g.dtype),
            pltpu.VMEM(slots, g.dtype),
            pltpu.VMEM(slots, g.dtype),
            pltpu.SemaphoreType.DMA((2, ring // 2, 2)),
            pltpu.SemaphoreType.DMA((2, ring // 2, 2)),
            pltpu.SemaphoreType.DMA((2,)),
            pltpu.SemaphoreType.DMA((n_w,)),
            pltpu.SemaphoreType.DMA((n_w,)),
            pltpu.SemaphoreType.DMA((n_w,)),
            pltpu.SemaphoreType.DMA((n_w,)),
            pltpu.SemaphoreType.DMA((n_w,)),
            pltpu.SemaphoreType.DMA((1,)),
        ],
        compiler_params=pltpu.CompilerParams(collective_id=1, has_side_effects=True),
        cost_estimate=pl.CostEstimate(flops=4 * partial.size, transcendentals=0, bytes_accessed=moved),
    )(partial, g)


def local(tokens, norm_gain, query_weight, kv_weight, out_weight, grad_out, doc_lengths):
    tensor_size = lax.axis_size("tensor")
    data_size = lax.axis_size("dp")
    tensor_index = lax.axis_index("tensor")
    sharers = tensor_size // KVH
    levels = sharers.bit_length() - 1
    contract_last = (((1,), (1,)), ((), ()))
    query_width = query_weight.shape[1]
    kv_width = kv_weight.shape[1]
    values32 = tokens.astype(jnp.float32)
    root_mean = jnp.sqrt(jnp.mean(values32 * values32, axis=-1) + epsilon)
    unit = values32 / root_mean[:, None]
    gain32 = norm_gain.astype(jnp.float32)
    normed_local = (unit * gain32).astype(jnp.bfloat16)
    rows = tokens.shape[0]
    pieces = jnp.stack([normed_local, grad_out])
    weights_local = jnp.concatenate([query_weight, kv_weight, out_weight.T], axis=1)
    tens_parts, weight_parts = gather_start(pieces, weights_local, RING)
    normed = tens_parts[:, 0].reshape(tensor_size * rows, -1)
    grad_full = tens_parts[:, 1].reshape(tensor_size * rows, -1)
    seq_length = normed.shape[0]
    weights_full = weight_parts.reshape(-1, weights_local.shape[1])
    query_full = weights_full[:, :query_width]
    kv_local = weights_full[:, query_width : query_width + kv_width]
    out_full_t = weights_full[:, query_width + kv_width :]
    queries = jnp.dot(normed, query_full, preferred_element_type=jnp.float32).astype(jnp.bfloat16)
    keyvals = jnp.dot(normed, kv_local, preferred_element_type=jnp.float32).astype(jnp.bfloat16)
    for bit_index in range(levels):
        partner = partner_2(keyvals, "tensor", bit_index)
        joined_upper_half = tensor_index >> bit_index & 1 == 1
        keyvals = jnp.concatenate(
            [
                jnp.where(joined_upper_half, partner, keyvals),
                jnp.where(joined_upper_half, keyvals, partner),
            ],
            axis=1,
        )
    key_rows = keyvals[:, :HD]
    value_rows = keyvals[:, HD:]
    out_grad = jnp.dot(grad_full, out_full_t, preferred_element_type=jnp.float32).astype(
        jnp.bfloat16
    )
    local_heads = queries.shape[1] // HD
    query_heads = queries.reshape(seq_length, local_heads, HD)
    out_heads = out_grad.reshape(seq_length, local_heads, HD)
    allowed = document_mask(doc_lengths[0], seq_length)
    scores = jnp.einsum(
        "qhd,td->hqt", query_heads, key_rows, preferred_element_type=jnp.float32
    ) / math.sqrt(HD)
    scores = jnp.where(allowed[None, :, :], scores, -1e30)
    peak = jnp.max(scores, axis=-1, keepdims=True)
    expo = jnp.exp(scores - peak)
    probs = expo / jnp.sum(expo, axis=-1, keepdims=True)
    probs_low = probs.astype(jnp.bfloat16)
    prob_grad = jnp.einsum("qhd,td->hqt", out_heads, value_rows, preferred_element_type=jnp.float32)
    inner = jnp.sum(probs * prob_grad, axis=-1, keepdims=True)
    score_grad = (probs * (prob_grad - inner) / math.sqrt(HD)).astype(jnp.bfloat16)
    query_grad = jnp.einsum("hqt,td->qhd", score_grad, key_rows, preferred_element_type=jnp.float32)
    query_grad = query_grad.astype(jnp.bfloat16).reshape(seq_length, local_heads * HD)
    key_part = jnp.einsum(
        "hqt,qhd->td", score_grad, query_heads, preferred_element_type=jnp.float32
    )
    value_part = jnp.einsum("hqt,qhd->td", probs_low, out_heads, preferred_element_type=jnp.float32)
    kv_partial = jnp.concatenate([key_part, value_part], axis=1)
    for bit_index in reversed(range(levels)):
        half_cols = kv_partial.shape[1] // 2
        upper_half = tensor_index >> bit_index & 1 == 1
        lower_cols = kv_partial[:, :half_cols]
        higher_cols = kv_partial[:, half_cols:]
        kept = jnp.where(upper_half, higher_cols, lower_cols)
        handed = jnp.where(upper_half, lower_cols, higher_cols)
        kv_partial = kept + partner_2(handed.astype(jnp.bfloat16), "tensor", bit_index).astype(
            handed.dtype
        )
    kv_grad = kv_partial.astype(jnp.bfloat16)
    from_query = lax.dot_general(
        query_grad, query_full, contract_last, preferred_element_type=jnp.float32
    )
    from_kv = lax.dot_general(kv_grad, kv_local, contract_last, preferred_element_type=jnp.float32)
    partial = (from_query + from_kv).astype(jnp.bfloat16).reshape(tensor_size, rows, -1)
    combined = jnp.concatenate([query_grad, kv_grad], axis=1)
    weight_partial = lax.dot_general(
        combined, normed, (((0,), (0,)), ((), ())), preferred_element_type=jnp.float32
    ).astype(jnp.bfloat16)
    block = weight_partial.shape[1] // data_size
    normed_grad, weight_arrived = end_exchange(partial, weight_partial, RING)
    scaled = normed_grad * gain32
    correction = unit * jnp.mean(scaled * unit, axis=-1, keepdims=True)
    input_grad = (grad_out.astype(jnp.float32) + (scaled - correction) / root_mean[:, None]).astype(
        jnp.bfloat16
    )
    weight_grads = (jnp.sum(weight_arrived.astype(jnp.float32), axis=0) / data_size).T
    return (input_grad, weight_grads[:, :query_width], weight_grads[:, query_width:])


def solution(mesh):
    placed = (
        P(("dp", "tensor"), None),
        P(),
        P("dp", "tensor"),
        P("dp", "tensor"),
        P("tensor", "dp"),
        P(("dp", "tensor"), None),
        P("dp", None),
    )
    return jax.shard_map(
        local,
        mesh=mesh,
        in_specs=placed,
        out_specs=(P(("dp", "tensor"), None), P("dp", "tensor"), P("dp", "tensor")),
        check_vma=False,
    )
```
